32 devices in a mesh: dp: 4 (over z), graph: 8 (over y, x, core).
Axes of the slice: x: 2, y: 2, z: 4, core: 2. Of those that a mesh axis runs over, the one named last changes fastest.
Arguments:
- features: float32 [4, 128, 3200], P('dp', 'graph'), may hold values from -6 to 6
- cotangent: float32 [4, 128, 1600], P('dp', 'graph'), may hold values from -6 to 6
- rotation: bfloat16 [4, 114, 1536], P('dp', None, 'graph'), may hold values from -2.6875 to 2.6875
- send_left: int32 [4, 64], P('dp', 'graph'), may hold values from 0 to 16, as said below
- send_right: int32 [4, 64], P('dp', 'graph'), may hold values from 0 to 16, as said below
- edge_src: int32 [4, 1536], P('dp', 'graph'), may hold values from 0 to 31, as said below
- edge_tgt: int32 [4, 1536], P('dp', 'graph'), may hold values from 0 to 15, as said below
- w_zero: bfloat16 [640, 832], P('graph'), may hold values from -0.25 to 0.25
- w_one_re: bfloat16 [512, 256], P('graph'), may hold values from -0.1875 to 0.1875
- w_one_im: bfloat16 [512, 256], P('graph'), may hold values from -0.1875 to 0.1875
- w_two_re: bfloat16 [384, 192], P('graph'), may hold values from -0.21875 to 0.21875
- w_two_im: bfloat16 [384, 192], P('graph'), may hold values from -0.21875 to 0.21875
- w_target: bfloat16 [128, 512], P('graph'), may hold values from -0.5 to 0.5
- alpha_vec: bfloat16 [64, 8], P('graph'), may hold values from -0.75 to 0.75
Outputs:
- attended: bfloat16 [4, 128, 1600], P('dp', 'graph')
- grad_features: float32 [4, 128, 3200], P('dp', 'graph')
- grad_zero: float32 [640, 832], P('graph')
- grad_one_re: float32 [512, 256], P('graph')
- grad_one_im: float32 [512, 256], P('graph')
- grad_two_re: float32 [384, 192], P('graph')
- grad_two_im: float32 [384, 192], P('graph')
- grad_target: float32 [128, 512], P('graph')
- grad_alpha: float32 [64, 8], P('graph')
The draws below stay inside these ranges and needn't reach their ends.
Inputs may be any that keep to these rules, and one draw needn't show every extreme that they name: `send_left`: filled slots come first and name distinct atoms; the value 16 marks an empty slot; each list holds 4 or more atoms, and in every cell some slab fills all 8 slots. `send_right`: like send_left. `edge_src`: values below 16 are the slab's own atoms; 16 + k is slot k of slab g-1's send_right, 24 + k slot k of slab g+1's send_left; never an empty slot. `edge_tgt`: every atom of a slab is the target of one edge or more.
All inputs are finite; a program needn't handle non-finite values.
Results may differ from the reference program's by a relative error of at most 0.0085.
Values may be sent and summed in bfloat16 or wider, within the bound.
A program may use at most 128 MiB of HBM per device.

```python
from functools import partial
import jax
import jax.numpy as jnp
from jax import lax

CH = 128
HIDDEN_SIZE = 64
HEADS = 8
ALPHA = 64
ROTS = 114
ATOM_DEV = 16
GHOST = 8
EDGE_DEV = 192
SLABS = 8
ATOMS = 128
EDGES = 1536
CELLS = 4


def ghost_tables(key):
    base = jax.random.fold_in(key, 11)
    keys = jax.random.split(base, 10)
    slab_ids = jnp.arange(SLABS, dtype=jnp.int32)

    def counts_of(first_key, second_key):
        drawn = jax.random.randint(first_key, (CELLS, SLABS), GHOST - GHOST // 2, GHOST + 1, dtype=jnp.int32)
        fullest = jax.random.randint(second_key, (CELLS, 1), 0, SLABS, dtype=jnp.int32)
        return jnp.where(slab_ids[None, :] == fullest, GHOST, drawn)
    count_left = counts_of(keys[0], keys[1])
    count_right = counts_of(keys[2], keys[3])
    base_ids = jnp.broadcast_to(jnp.arange(ATOM_DEV, dtype=jnp.int32), (CELLS * SLABS, ATOM_DEV))
    order_left = jax.random.permutation(keys[4], base_ids, axis=1, independent=True)[:, :GHOST].reshape(CELLS, SLABS, GHOST)
    order_right = jax.random.permutation(keys[5], base_ids, axis=1, independent=True)[:, :GHOST].reshape(CELLS, SLABS, GHOST)
    slots = jnp.arange(GHOST, dtype=jnp.int32)[None, None, :]
    send_left = jnp.where(slots < count_left[:, :, None], order_left, ATOM_DEV)
    send_right = jnp.where(slots < count_right[:, :, None], order_right, ATOM_DEV)
    first_targets = jnp.broadcast_to(jnp.arange(ATOM_DEV, dtype=jnp.int32), (CELLS, SLABS, ATOM_DEV))
    more_targets = jax.random.randint(keys[6], (CELLS, SLABS, EDGE_DEV - ATOM_DEV), 0, ATOM_DEV, dtype=jnp.int32)
    edge_tgt = jnp.concatenate([first_targets, more_targets], axis=2)
    kinds = jax.random.randint(keys[7], (CELLS, SLABS, EDGE_DEV), 0, 4, dtype=jnp.int32)
    local_src = jax.random.randint(keys[8], (CELLS, SLABS, EDGE_DEV), 0, ATOM_DEV, dtype=jnp.int32)
    raw_slot = jax.random.randint(keys[9], (CELLS, SLABS, EDGE_DEV), 0, 1048576, dtype=jnp.int32)
    left_have = jnp.roll(count_right, 1, axis=1)[:, :, None]
    right_have = jnp.roll(count_left, -1, axis=1)[:, :, None]
    ghost_src = jnp.where(kinds == 2, ATOM_DEV + raw_slot % left_have, ATOM_DEV + GHOST + raw_slot % right_have)
    edge_src = jnp.where(kinds < 2, local_src, ghost_src)
    last_src = ATOM_DEV + GHOST + right_have[:, :, 0] - 1
    edge_src = edge_src.at[:, :, EDGE_DEV - 1].set(last_src)
    return (send_left.reshape(CELLS, SLABS * GHOST), send_right.reshape(CELLS, SLABS * GHOST), edge_src.reshape(CELLS, SLABS * EDGE_DEV), edge_tgt.reshape(CELLS, SLABS * EDGE_DEV))


def draw_send_left(key, part):
    return ghost_tables(key)[0]


def draw_send_right(key, part):
    return ghost_tables(key)[1]


def draw_edge_src(key, part):
    return ghost_tables(key)[2]


def draw_edge_tgt(key, part):
    return ghost_tables(key)[3]


def levels(rng, dims, cuts, smallest, top_value):
    loudness, own = 1.0, jax.random.fold_in(rng, 6)
    for dim, blocks in cuts:
        heights = jnp.exp(jax.random.uniform(jax.random.fold_in(own, dim), (blocks,), jnp.float32, smallest / len(cuts), top_value / len(cuts)))
        loudness = loudness * jnp.repeat(heights, dims[dim] // blocks).reshape([-1 if axis == dim else 1 for axis in range(len(dims))])
    return loudness


def gaussian(rng, shape, scale, reach, shards=(), kind=jnp.bfloat16):
    values = scale * jax.random.normal(rng, shape, jnp.float32)
    if shards:
        values = values * levels(rng, shape, shards, -0.22, 0.18)
    return jnp.clip(values, -reach, reach).astype(kind)


def setup_inputs(seed: int = 0) -> dict:
    seeds = jax.random.split(jax.random.key(seed), 15)
    return {
        "features": gaussian(seeds[0], (CELLS, ATOMS, 25 * CH), 1.0, 6.0, ((0, 4), (1, 8)), jnp.float32),
        "cotangent": gaussian(seeds[1], (CELLS, ATOMS, 25 * HIDDEN_SIZE), 1.0, 6.0, ((0, 4), (1, 8)), jnp.float32),
        "rotation": gaussian(seeds[2], (CELLS, ROTS, EDGES), 0.45, 2.6875, ((0, 4), (2, 8))),
        "send_left": draw_send_left(jax.random.fold_in(seeds[14], 71), 0),
        "send_right": draw_send_right(jax.random.fold_in(seeds[14], 71), 0),
        "edge_src": draw_edge_src(jax.random.fold_in(seeds[14], 71), 0),
        "edge_tgt": draw_edge_tgt(jax.random.fold_in(seeds[14], 71), 0),
        "w_zero": gaussian(seeds[7], (5 * CH, 5 * HIDDEN_SIZE + HEADS * ALPHA), (5 * CH) ** -0.5, 0.25, ((0, 8),)),
        "w_one_re": gaussian(seeds[8], (4 * CH, 4 * HIDDEN_SIZE), (8 * CH) ** -0.5, 0.1875, ((0, 8),)),
        "w_one_im": gaussian(seeds[9], (4 * CH, 4 * HIDDEN_SIZE), (8 * CH) ** -0.5, 0.1875, ((0, 8),)),
        "w_two_re": gaussian(seeds[10], (3 * CH, 3 * HIDDEN_SIZE), (6 * CH) ** -0.5, 0.21875, ((0, 8),)),
        "w_two_im": gaussian(seeds[11], (3 * CH, 3 * HIDDEN_SIZE), (6 * CH) ** -0.5, 0.21875, ((0, 8),)),
        "w_target": gaussian(seeds[12], (CH, HEADS * ALPHA), CH ** -0.5, 0.5, ((0, 8),)),
        "alpha_vec": gaussian(seeds[13], (ALPHA, HEADS), ALPHA ** -0.5, 0.75, ((0, 8),)),
    }


def turn_blocks(rotation, edge_count):
    blocks = []
    offset = 0
    for degree in range(1, 5):
        kept_order = min(degree, 2)
        row_count = 2 * kept_order + 1
        column_count = 2 * degree + 1
        piece_block = rotation[offset:offset + row_count * column_count].astype(jnp.float32)
        blocks.append(piece_block.reshape(row_count, column_count, edge_count))
        offset = offset + row_count * column_count
    return blocks

def pick_order(turned, azimuth, degrees, edge_count):
    chosen = jnp.stack([turned[degree][:, min(degree, 2) + azimuth, :] for degree in degrees], axis=1)
    return chosen.reshape(edge_count, -1).astype(jnp.bfloat16)

def attend(extended, w_zero, w_one_re, w_one_im, w_two_re, w_two_im, w_target, alpha_vec, rotation, edge_src, edge_tgt, atom_count):
    edge_count = edge_src.shape[0]
    channels = w_target.shape[0]
    hidden = w_one_re.shape[1] // 4
    head_count = alpha_vec.shape[1]
    alpha_width = alpha_vec.shape[0]
    blocks = turn_blocks(rotation, edge_count)
    coeffs = extended.reshape(extended.shape[0], 25, channels)
    turned = [jnp.take(coeffs[:, 0:1, :], edge_src, axis=0)]
    for degree in range(1, 5):
        source_part = jnp.take(coeffs[:, degree * degree:(degree + 1) * (degree + 1), :], edge_src, axis=0)
        turned.append(jnp.einsum('rne,enc->erc', blocks[degree - 1], source_part, precision=lax.Precision.HIGHEST))
    zero_in = pick_order(turned, 0, range(5), edge_count)
    one_pos = pick_order(turned, 1, range(1, 5), edge_count)
    one_neg = pick_order(turned, -1, range(1, 5), edge_count)
    two_pos = pick_order(turned, 2, range(2, 5), edge_count)
    two_neg = pick_order(turned, -2, range(2, 5), edge_count)
    mixed = jnp.dot(zero_in, w_zero, preferred_element_type=jnp.float32)
    hidden_zero = mixed[:, :5 * hidden].reshape(edge_count, 5, hidden)
    target_in = extended[:atom_count, :channels].astype(jnp.bfloat16)
    per_atom = jnp.dot(target_in, w_target, preferred_element_type=jnp.float32)
    alpha_pre = mixed[:, 5 * hidden:] + jnp.take(per_atom, edge_tgt, axis=0)
    one_up = jnp.dot(one_pos, w_one_re, preferred_element_type=jnp.float32) - jnp.dot(one_neg, w_one_im, preferred_element_type=jnp.float32)
    one_down = jnp.dot(one_neg, w_one_re, preferred_element_type=jnp.float32) + jnp.dot(one_pos, w_one_im, preferred_element_type=jnp.float32)
    two_up = jnp.dot(two_pos, w_two_re, preferred_element_type=jnp.float32) - jnp.dot(two_neg, w_two_im, preferred_element_type=jnp.float32)
    two_down = jnp.dot(two_neg, w_two_re, preferred_element_type=jnp.float32) + jnp.dot(two_pos, w_two_im, preferred_element_type=jnp.float32)
    scalar = hidden_zero[:, 0, :]
    gating = jax.nn.sigmoid(scalar)[:, None, :]
    value_zero = jnp.concatenate([jax.nn.silu(scalar)[:, None, :], hidden_zero[:, 1:, :] * gating], axis=1)
    one_up = one_up.reshape(edge_count, 4, hidden) * gating
    one_down = one_down.reshape(edge_count, 4, hidden) * gating
    two_up = two_up.reshape(edge_count, 3, hidden) * gating
    two_down = two_down.reshape(edge_count, 3, hidden) * gating
    scores = alpha_pre.reshape(edge_count, head_count, alpha_width)
    centre = scores - lax.optimization_barrier(jnp.mean(scores, axis=-1, keepdims=True))
    normed = centre * lax.rsqrt(lax.optimization_barrier(jnp.mean(centre * centre, axis=-1, keepdims=True)) + 1e-05)
    activated = normed * (0.2 + 0.8 * jax.nn.sigmoid(normed))
    logits = jnp.einsum('ehc,ch->eh', activated, alpha_vec.astype(jnp.float32), precision=lax.Precision.HIGHEST)
    raised = jnp.exp(logits)
    member = (edge_tgt[:, None] == jnp.arange(atom_count, dtype=jnp.int32)[None, :]).astype(jnp.float32)
    totals = jnp.dot(member.T, raised, precision=lax.Precision.HIGHEST)
    weights = raised / jnp.take(totals, edge_tgt, axis=0)
    spread = jnp.repeat(weights, hidden // head_count, axis=1)[:, None, :]
    value_zero = value_zero * spread
    one_up = one_up * spread
    one_down = one_down * spread
    two_up = two_up * spread
    two_down = two_down * spread
    pieces = [value_zero[:, 0:1, :]]
    for degree in range(1, 5):
        kept_order = min(degree, 2)
        row_list = []
        for azimuth in range(-kept_order, kept_order + 1):
            if azimuth == 0:
                row_list.append(value_zero[:, degree])
            elif azimuth == 1:
                row_list.append(one_up[:, degree - 1])
            elif azimuth == -1:
                row_list.append(one_down[:, degree - 1])
            elif azimuth == 2:
                row_list.append(two_up[:, degree - 2])
            else:
                row_list.append(two_down[:, degree - 2])
        stacked = jnp.stack(row_list, axis=1)
        pieces.append(jnp.einsum('rne,erc->enc', blocks[degree - 1], stacked, precision=lax.Precision.HIGHEST))
    message = jnp.concatenate(pieces, axis=1).reshape(edge_count, -1).astype(jnp.bfloat16)
    return jnp.dot(member.T.astype(jnp.bfloat16), message, preferred_element_type=jnp.float32)

def take_rows(source_rows, index_list):
    return jnp.take(source_rows, index_list, axis=0)

def add_back(own_rows, right_list, right_grad, left_list, left_grad):
    padded = jnp.concatenate([own_rows, jnp.zeros((1, own_rows.shape[1]), jnp.float32)], axis=0)
    padded = padded.at[right_list].add(right_grad)
    padded = padded.at[left_list].add(left_grad)
    return padded[:own_rows.shape[0]]

def reference(features, cotangent, rotation, send_left, send_right, edge_src, edge_tgt, w_zero, w_one_re, w_one_im, w_two_re, w_two_im, w_target, alpha_vec):
    weight_list = (w_zero, w_one_re, w_one_im, w_two_re, w_two_im, w_target, alpha_vec)
    row_width = features.shape[2]

    def one_cell(carry, cell):
        cell_rows, cell_cot, cell_rot, left_flat, right_flat, src_flat, tgt_flat = cell
        slab_rows = cell_rows.reshape(SLABS, ATOM_DEV, row_width)
        padded = jnp.concatenate([slab_rows, jnp.zeros((SLABS, 1, row_width), jnp.float32)], axis=1)
        left_lists = left_flat.reshape(SLABS, GHOST)
        right_lists = right_flat.reshape(SLABS, GHOST)
        sent_left = jax.vmap(take_rows)(padded, left_lists)
        sent_right = jax.vmap(take_rows)(padded, right_lists)
        from_left = jnp.roll(sent_right, 1, axis=0)
        from_right = jnp.roll(sent_left, -1, axis=0)
        extended = jnp.concatenate([slab_rows, from_left, from_right], axis=1)
        slab_rot = cell_rot.reshape(ROTS, SLABS, EDGE_DEV).transpose(1, 0, 2)
        slab_src = src_flat.reshape(SLABS, EDGE_DEV)
        slab_tgt = tgt_flat.reshape(SLABS, EDGE_DEV)
        slab_cot = cell_cot.reshape(SLABS, ATOM_DEV, -1)

        def one_slab(sums, slab):
            ext_rows, rot_rows, src_rows, tgt_rows, cot_rows = slab
            local_fn = partial(attend, rotation=rot_rows, edge_src=src_rows, edge_tgt=tgt_rows, atom_count=ATOM_DEV)
            summed, pullback = jax.vjp(local_fn, ext_rows, w_zero, w_one_re, w_one_im, w_two_re, w_two_im, w_target, alpha_vec)
            pulled = pullback(cot_rows)
            sums = tuple((running + term.astype(jnp.float32) for running, term in zip(sums, pulled[1:])))
            return (sums, (summed.astype(jnp.bfloat16), pulled[0]))
        carry, outputs = lax.scan(one_slab, carry, (extended, slab_rot, slab_src, slab_tgt, slab_cot))
        attended_slabs, ext_grads = outputs
        own_grads = ext_grads[:, :ATOM_DEV]
        back_left = jnp.roll(ext_grads[:, ATOM_DEV:ATOM_DEV + GHOST], -1, axis=0)
        back_right = jnp.roll(ext_grads[:, ATOM_DEV + GHOST:], 1, axis=0)
        feature_grads = jax.vmap(add_back)(own_grads, right_lists, back_left, left_lists, back_right)
        return (carry, (attended_slabs.reshape(ATOMS, -1), feature_grads.reshape(ATOMS, -1)))
    start = tuple((jnp.zeros(weight.shape, jnp.float32) for weight in weight_list))
    sums, outputs = lax.scan(one_cell, start, (features, cotangent, rotation, send_left, send_right, edge_src, edge_tgt))
    attended, grad_features = outputs
    return (attended, grad_features, sums[0], sums[1], sums[2], sums[3], sums[4], sums[5], sums[6])
```

```python
from functools import partial

import jax
import jax.numpy as jnp
from jax import lax
from jax.experimental import pallas as pl
from jax.experimental.pallas import tpu as pltpu
from jax.sharding import PartitionSpec as P

F32 = jnp.float32
BF16 = jnp.bfloat16
OFFSETS = {1: 0, 2: 9, 3: 34, 4: 69}
DEGREES = (1, 2, 3, 4)
BLOCK_C = 32
BLOCK_H = 16
MESH = pl.DeviceIdType.MESH
EXACT = lax.Precision.HIGHEST


def slot(degree, azimuth):
    return {0: degree, 1: 4 + degree, -1: 8 + degree, 2: 11 + degree, -2: 14 + degree}[azimuth]


def orders(degree):
    kept = min(degree, 2)
    return range(-kept, kept + 1)


def rot_row(degree, azimuth, column):
    return OFFSETS[degree] + (azimuth + min(degree, 2)) * (2 * degree + 1) + column


def dot(a, b, ca, cb, precision=None):
    return lax.dot_general(
        a, b, (((ca,), (cb,)), ((), ())), preferred_element_type=F32, precision=precision
    )


def flip(index, power):
    bit = lax.rem(lax.div(index, power), 2)
    return index + (1 - 2 * bit) * power


def flips(index, powers, chosen):
    for j in chosen:
        index = flip(index, powers[j])
    return index


def subsets(steps):
    found = [()]
    for j in steps:
        found = found + [s + (j,) for s in found]
    return found


class Halving:
    def __init__(self, count):
        self.steps = count.bit_length() - 1
        self.rest = [subsets(range(j + 1, self.steps)) for j in range(self.steps)]
        self.base = [0]
        for found in self.rest:
            self.base.append(self.base[-1] + len(found))

    def spot(self, step, chosen):
        return self.base[step] + self.rest[step].index(chosen)


def slab_kernel(n, depth, sizes, *refs):
    take = iter(refs)
    feat_ref, cot_ref, rot_ref, src_ref, tgt_ref, left_ref, right_ref = [next(take) for _ in range(7)]
    count = len(sizes["weights"])
    items = len(sizes["terms"])
    shards = [next(take) for _ in range(count)]
    att_ref, grad_ref = next(take), next(take)
    final = [next(take) for _ in range(items)]
    (ext_ref, alphas, d_alphas, rotf, xs, turned, hid, msg, dmsg, scores, dhid, dmixed, dturned,
     dxs, small, spreads) = [next(take) for _ in range(16)]
    outgoing, near, ghost, back = [next(take) for _ in range(4)]
    full = [next(take) for _ in range(count)]
    mats = [next(take) for _ in range(count)]
    terms = [next(take) for _ in range(items)]
    landed = [next(take) for _ in range(items)]
    out_xy = [next(take) for _ in range(items)]
    in_xy = [next(take) for _ in range(items)]
    layers = [next(take) for _ in range(items)]
    out_z = [next(take) for _ in range(items)]
    in_z = [next(take) for _ in range(items)]
    (side_send, side_recv, hop_send, hop_recv, core_send, core_recv, sib_send, sib_recv,
     xy_send, xy_recv, z_send, z_recv, last_send, last_recv) = list(take)

    edges = src_ref.shape[1]
    rows = ext_ref.shape[0]
    atoms = att_ref.shape[0]
    channels = n * sizes["weights"][5][0]
    hidden = sizes["weights"][1][1] // 4
    heads = small.shape[1]
    width = alphas.shape[0]
    slots = left_ref.shape[1]

    me = lax.axis_index("graph")
    row = lax.axis_index("dp")
    half = n // 2
    chip = lax.div(me, 2)
    parity = lax.rem(me, 2)
    sibling = me + 1 - 2 * parity
    right, left = lax.rem(me + 1, n), lax.rem(me + n - 1, n)
    plan = Halving(half)
    steps = plan.steps
    powers = [2 ** j + parity * (2 ** ((j + 1) % steps) - 2 ** j) for j in range(steps)]
    deep = Halving(depth)
    deep_powers = [2 ** j for j in range(deep.steps)]

    barrier = pltpu.get_barrier_semaphore()
    partners = [(row, sibling), (row, right), (row, left)]
    partners += [(row, 2 * flip(chip, p) + parity) for p in powers]
    partners += [(lax.rem(row + z, depth), me) for z in range(1, depth)]
    for partner in partners:
        pl.semaphore_signal(barrier, inc=1, device_id=partner, device_id_type=MESH)

    def remote(src, dst, send, recv, target):
        copy = pltpu.make_async_remote_copy(
            src_ref=src, dst_ref=dst, send_sem=send, recv_sem=recv,
            device_id=target, device_id_type=MESH)
        copy.start()
        return copy

    started = []

    own = feat_ref[...].astype(BF16)
    ext_ref[:atoms, :] = own
    for side, list_ref in ((0, left_ref), (1, right_ref)):
        ids = lax.broadcasted_iota(jnp.int32, (atoms, slots), 0)
        pick = (ids == list_ref[...]).astype(F32).astype(BF16)
        outgoing[side] = dot(pick, own, 0, 0).astype(BF16)
    for w in range(count):
        full[w][chip, parity] = shards[w][...]
    src_hot = (
        lax.broadcasted_iota(jnp.int32, (rows, edges), 0) == src_ref[...]
    ).astype(F32).astype(BF16)
    member = (lax.broadcasted_iota(jnp.int32, (atoms, edges), 0) == tgt_ref[...]).astype(F32)
    member_b = member.astype(BF16)

    pl.semaphore_wait(barrier, len(partners))

    sides = []
    for side, target in ((1, left), (0, right)):
        sides.append(remote(outgoing.at[1 - side], near.at[side], side_send.at[side],
                            side_recv.at[side], (row, target)))
    arrivals = {}

    def hop(j, w):
        target = (row, 2 * flip(chip, powers[j]) + parity)
        for t, chosen in enumerate(subsets(range(j))):
            unit = flips(chip, powers, chosen)
            source = shards[w] if j == 0 else full[w].at[unit, parity]
            copy = remote(source, full[w].at[unit, parity], hop_send.at[2 ** j + t - 1, w],
                          hop_recv.at[2 ** j + t - 1, w], target)
            arrivals[j, t, w] = copy
            started.append(copy)

    crossing = {}

    def cross(spot, unit, w, source=None):
        copy = remote(full[w].at[unit, parity] if source is None else source,
                      full[w].at[unit, parity], core_send.at[spot, w], core_recv.at[spot, w],
                      (row, sibling))
        crossing[spot, w] = copy
        started.append(copy)

    def land(j, w):
        partner = flip(chip, powers[j])
        for t, chosen in enumerate(subsets(range(j))):
            arrivals[j, t, w].wait_recv()
            cross(2 ** j + t, flips(partner, powers, chosen), w)

    weight_order = (0, 5, 6, 1, 2, 3, 4)
    for w in weight_order:
        hop(0, w)
    for w in weight_order:
        cross(0, chip, w, shards[w])

    edge_eye = (
        lax.broadcasted_iota(jnp.int32, (rot_ref.shape[1], rot_ref.shape[1]), 0)
        == lax.broadcasted_iota(jnp.int32, (rot_ref.shape[1], rot_ref.shape[1]), 1)
    ).astype(F32).astype(BF16)
    rotf[...] = dot(edge_eye, rot_ref[...], 1, 1)
    for k in range(25):
        dmsg[k] = dot(
            cot_ref[:, k * hidden:(k + 1) * hidden].astype(BF16), member_b, 0, 0
        )
    for copy in sides:
        copy.wait_recv()
    ext_ref[atoms:, :] = near[...].astype(F32).reshape(rows - atoms, -1).astype(BF16)
    for k in range(25):
        xs[k] = dot(ext_ref[:, k * channels:(k + 1) * channels], src_hot, 0, 0)

    for j in range(1, steps):
        for w in weight_order:
            land(j - 1, w)
            hop(j, w)

    def turn(i, carry):
        part = pl.ds(pl.multiple_of(i * BLOCK_C, BLOCK_C), BLOCK_C)
        turned[0, part, :] = xs[0, part, :].astype(BF16)
        for degree in DEGREES:
            for azimuth in orders(degree):
                total = None
                for m in range(2 * degree + 1):
                    k = rot_row(degree, azimuth, m)
                    term = rotf[k:k + 1, :] * xs[degree * degree + m, part, :]
                    total = term if total is None else total + term
                turned[slot(degree, azimuth), part, :] = total.astype(BF16)
        return carry

    lax.fori_loop(0, channels // BLOCK_C, turn, 0)

    zero_in = turned[0:5].reshape(5 * channels, edges)
    one_pos = turned[5:9].reshape(4 * channels, edges)
    one_neg = turned[9:13].reshape(4 * channels, edges)
    two_pos = turned[13:16].reshape(3 * channels, edges)
    two_neg = turned[16:19].reshape(3 * channels, edges)

    def settle(w):
        for spot in range(half):
            crossing[spot, w].wait_recv()
        block = sizes["weights"][w][0]
        if block % 16:
            for u in range(half):
                for c in range(2):
                    at = (2 * u + c) * block
                    mats[w][at:at + block, :] = full[w][u, c].astype(mats[w].dtype)

    def weight(w, begin=0, end=None):
        block, wide = sizes["weights"][w]
        end = wide if end is None else end
        if block % 16:
            return mats[w][:, begin:end].astype(BF16)
        return full[w][:, :, :, begin:end].reshape(n * block, end - begin)

    for w in (0, 5, 6):
        land(steps - 1, w)
    for w in (1, 2):
        land(steps - 1, w)
    for w in (0, 5, 6):
        settle(w)
    alpha_rows = sizes["weights"][6][0]
    for u in range(half):
        for c in range(2):
            at = (2 * u + c) * alpha_rows
            alphas[at:at + alpha_rows, :] = full[6][u, c].astype(F32)

    per_atom = dot(ext_ref[:atoms, :channels], weight(5), 1, 0)
    high = per_atom.astype(BF16)
    low = (per_atom - high.astype(F32)).astype(BF16)
    scores[...] = (
        dot(weight(0, 5 * hidden), zero_in, 0, 0)
        + dot(high, member_b, 0, 0)
        + dot(low, member_b, 0, 0)
    )
    hid[0:5] = dot(weight(0, 0, 5 * hidden), zero_in, 0, 0).reshape(5, hidden, edges)

    for w in (3, 4):
        land(steps - 1, w)

    for h in range(heads):
        part = slice(h * width, (h + 1) * width)
        value = scores[part, :]
        centre = value - jnp.mean(value, axis=0, keepdims=True)
        scale = lax.rsqrt(jnp.mean(centre * centre, axis=0, keepdims=True) + 1e-05)
        normed = centre * scale
        scores[part, :] = normed
        gate = 0.2 + 0.8 * jax.nn.sigmoid(normed)
        small[0, h:h + 1, :] = jnp.sum(
            normed * gate * alphas[:, h:h + 1], axis=0, keepdims=True
        )
        small[1, h:h + 1, :] = scale

    raised = jnp.exp(small[0])
    totals = dot(dot(raised, member, 1, 1, EXACT), member, 1, 0, EXACT)
    weights = raised / totals
    spreads[0] = jnp.broadcast_to(
        weights[:, None, :], (heads, hidden // heads, edges)
    ).reshape(hidden, edges)

    settle(1)
    settle(2)
    hid[5:9] = (dot(weight(1), one_pos, 0, 0) - dot(weight(2), one_neg, 0, 0)).reshape(
        4, hidden, edges)
    hid[9:13] = (dot(weight(1), one_neg, 0, 0) + dot(weight(2), one_pos, 0, 0)).reshape(
        4, hidden, edges)
    settle(3)
    settle(4)
    hid[13:16] = (dot(weight(3), two_pos, 0, 0) - dot(weight(4), two_neg, 0, 0)).reshape(
        3, hidden, edges)
    hid[16:19] = (dot(weight(3), two_neg, 0, 0) + dot(weight(4), two_pos, 0, 0)).reshape(
        3, hidden, edges)

    def mix(i, carry):
        part = pl.ds(pl.multiple_of(i * BLOCK_H, BLOCK_H), BLOCK_H)
        spread = spreads[0, part, :]
        scalar = hid[0, part, :]
        gating = jax.nn.sigmoid(scalar)
        silu = scalar * gating
        both = gating * spread
        msg[0, part, :] = (silu * spread).astype(BF16)
        d_first = dmsg[0, part, :]
        inner = jnp.zeros_like(scalar)
        for degree in DEGREES:
            size = 2 * degree + 1
            sums = [None] * size
            for azimuth in orders(degree):
                raw = hid[slot(degree, azimuth), part, :]
                value = raw * both
                back_sum = None
                for m in range(size):
                    k = rot_row(degree, azimuth, m)
                    line = rotf[k:k + 1, :]
                    term = line * value
                    sums[m] = term if sums[m] is None else sums[m] + term
                    other = line * dmsg[degree * degree + m, part, :]
                    back_sum = other if back_sum is None else back_sum + other
                inner = inner + back_sum * raw
                dhid[slot(degree, azimuth), part, :] = (back_sum * both).astype(BF16)
            for m in range(size):
                msg[degree * degree + m, part, :] = sums[m].astype(BF16)
        spreads[1, part, :] = inner * gating + d_first * silu
        d_scalar = d_first * spread * gating * (1.0 + scalar * (1.0 - gating)) + (
            inner * spread * gating * (1.0 - gating)
        )
        dhid[0, part, :] = d_scalar.astype(BF16)
        return carry

    lax.fori_loop(0, hidden // BLOCK_H, mix, 0)

    def put(i, value):
        block, wide = sizes["terms"][i]
        if block % 16:
            for u in range(half):
                for c in range(2):
                    at = (2 * u + c) * block
                    terms[i][u, c] = value[at:at + block, :].astype(BF16)
        else:
            terms[i][...] = value.astype(BF16).reshape(half, 2, block, wide)

    flights = {}
    even = [terms[i].shape[2] % depth == 0 for i in range(items)]

    def launch(key, src, dst, send, recv, target):
        copy = remote(src, dst, send, recv, target)
        flights[key] = copy
        started.append(copy)

    def to_sibling(i):
        launch(("core", i), terms[i].at[:, 1 - parity], landed[i], sib_send.at[i], sib_recv.at[i],
               (row, sibling))

    def chip_sum(i, step, chosen):
        unit = flips(chip, powers, chosen)
        total = terms[i][unit, parity].astype(F32) + landed[i][unit].astype(F32)
        for s in range(step):
            total = total + in_xy[i][plan.spot(s, chosen)].astype(F32)
        return total

    def to_chip(i, step):
        if step == 0:
            flights["core", i].wait_recv()
        else:
            flights["xy", step - 1, i].wait_recv()
        begin, end = plan.base[step], plan.base[step + 1]
        for t, rest in enumerate(plan.rest[step]):
            out_xy[i][begin + t] = chip_sum(i, step, (step,) + rest).astype(BF16)
        target = (row, 2 * flip(chip, powers[step]) + parity)
        launch(("xy", step, i), out_xy[i].at[begin:end], in_xy[i].at[begin:end],
               xy_send.at[step, i], xy_recv.at[step, i], target)

    def layer_sum(i, step, chosen):
        total = layers[i][flips(row, deep_powers, chosen)]
        for s in range(step):
            total = total + in_z[i][deep.spot(s, chosen)].astype(F32)
        return total

    def share(i):
        for z in range(1, depth):
            launch(("last", z, i), final[i].at[row], final[i].at[row], last_send.at[z, i],
                   last_recv.at[z, i], (lax.rem(row + z, depth), me))

    def to_layer(i, step):
        if step == 0:
            flights["xy", steps - 1, i].wait_recv()
            total = chip_sum(i, steps, ())
            if not even[i]:
                final[i][row] = total.astype(BF16)
                share(i)
                return
            size = total.shape[0] // depth
            for z in range(depth):
                layers[i][z] = total[z * size:(z + 1) * size]
        elif even[i]:
            flights["z", step - 1, i].wait_recv()
        if not even[i]:
            return
        if step == deep.steps:
            final[i][row] = layer_sum(i, step, ()).astype(BF16)
            share(i)
            return
        begin, end = deep.base[step], deep.base[step + 1]
        for t, rest in enumerate(deep.rest[step]):
            out_z[i][begin + t] = layer_sum(i, step, (step,) + rest).astype(BF16)
        launch(("z", step, i), out_z[i].at[begin:end], in_z[i].at[begin:end],
               z_send.at[step, i], z_recv.at[step, i], (flip(row, deep_powers[step]), me))

    def advance(i, stage):
        if stage == 0:
            to_sibling(i)
        elif stage <= steps:
            to_chip(i, stage - 1)
        else:
            to_layer(i, stage - 1 - steps)

    last_stage = steps + deep.steps + 1

    def gradient_pair(first, number, re_item, im_item, pos, neg):
        middle = first + number
        last = middle + number
        up = dhid[first:middle].reshape(number * hidden, edges)
        down = dhid[middle:last].reshape(number * hidden, edges)
        put(re_item, dot(pos, up, 1, 1) + dot(neg, down, 1, 1))
        advance(re_item, 0)
        put(im_item, dot(pos, down, 1, 1) - dot(neg, up, 1, 1))
        advance(im_item, 0)

    gradient_pair(5, 4, 0, 1, one_pos, one_neg)
    gradient_pair(13, 3, 2, 3, two_pos, two_neg)
    advance(0, 1)
    advance(1, 1)
    d_values = dhid[0:5].reshape(5 * hidden, edges)
    dmixed[:5 * hidden, :] = d_values
    put(4, dot(zero_in, d_values, 1, 1))
    advance(4, 0)
    advance(2, 1)
    advance(3, 1)

    d_weights = jnp.sum(
        spreads[1].reshape(heads, hidden // heads, edges), axis=1
    )
    product = weights * d_weights
    d_logits = product - weights * dot(
        dot(product, member, 1, 1, EXACT), member, 1, 0, EXACT
    )
    small[0] = d_logits
    for h in range(heads):
        part = slice(h * width, (h + 1) * width)
        normed = scores[part, :]
        sig = jax.nn.sigmoid(normed)
        gate = 0.2 + 0.8 * sig
        d_logit = small[0, h:h + 1, :]
        d_alphas[:, h:h + 1] = jnp.sum(normed * gate * d_logit, axis=1, keepdims=True)
        d_norm = d_logit * alphas[:, h:h + 1] * (gate + 0.8 * normed * sig * (1.0 - sig))
        first = jnp.mean(d_norm, axis=0, keepdims=True)
        second = jnp.mean(d_norm * normed, axis=0, keepdims=True)
        d_score = small[1, h:h + 1, :] * (d_norm - first - normed * second)
        dmixed[5 * hidden + h * width:5 * hidden + (h + 1) * width, :] = d_score.astype(BF16)
        scores[part, :] = d_score
    put(5, dot(zero_in, dmixed[5 * hidden:, :], 1, 1))
    advance(5, 0)
    advance(4, 1)
    d_per_atom = dot(member, scores[...], 1, 1, EXACT).astype(BF16)
    put(6, dot(ext_ref[:atoms, :channels], d_per_atom, 0, 0))
    advance(6, 0)
    for u in range(half):
        for c in range(2):
            at = (2 * u + c) * alpha_rows
            terms[7][u, c] = d_alphas[at:at + alpha_rows, :].astype(BF16)
    advance(7, 0)
    advance(0, 2)
    advance(1, 2)
    advance(5, 1)
    advance(6, 1)
    advance(7, 1)
    advance(2, 2)
    advance(3, 2)

    dturned[0:5] = dot(weight(0), dmixed[...], 1, 0).reshape(5, channels, edges)

    def turn_pair(first, number, re_item, im_item):
        middle = first + number
        last = middle + number
        up = dhid[first:middle].reshape(number * hidden, edges)
        down = dhid[middle:last].reshape(number * hidden, edges)
        dturned[first:middle] = (
            dot(weight(re_item), up, 1, 0) + dot(weight(im_item), down, 1, 0)
        ).reshape(number, channels, edges)
        dturned[middle:last] = (
            dot(weight(re_item), down, 1, 0) - dot(weight(im_item), up, 1, 0)
        ).reshape(number, channels, edges)

    turn_pair(5, 4, 1, 2)
    advance(0, 3)
    advance(1, 3)
    advance(4, 2)
    advance(5, 2)
    advance(6, 2)
    advance(7, 2)
    turn_pair(13, 3, 3, 4)

    def turn_back(i, carry):
        part = pl.ds(pl.multiple_of(i * BLOCK_C, BLOCK_C), BLOCK_C)
        dxs[0, part, :] = dturned[0, part, :].astype(BF16)
        for degree in DEGREES:
            for m in range(2 * degree + 1):
                total = None
                for azimuth in orders(degree):
                    k = rot_row(degree, azimuth, m)
                    term = rotf[k:k + 1, :] * dturned[slot(degree, azimuth), part, :]
                    total = term if total is None else total + term
                dxs[degree * degree + m, part, :] = total.astype(BF16)
        return carry

    lax.fori_loop(0, channels // BLOCK_C, turn_back, 0)
    advance(2, 3)
    advance(3, 3)
    advance(0, 4)
    advance(1, 4)

    d_target = dot(d_per_atom, weight(5), 1, 1)
    ext_grad = dot(src_hot, dxs[...].reshape(25 * channels, edges), 1, 1)
    grad_ref[...] = ext_grad[:atoms]
    grad_ref[:, :channels] = ext_grad[:atoms, :channels] + d_target
    for side in range(2):
        begin = atoms + side * slots
        ghost[side] = ext_grad[begin:begin + slots].astype(BF16)
    returns = [
        remote(ghost.at[0], back.at[0], side_send.at[2], side_recv.at[2], (row, left)),
        remote(ghost.at[1], back.at[1], side_send.at[3], side_recv.at[3], (row, right)),
    ]
    done = {0: 4, 1: 4, 2: 3, 3: 3, 4: 2, 5: 2, 6: 2, 7: 2}
    for i in (4, 5, 6, 7):
        done[i] += 1
        advance(i, done[i])
    att_ref[...] = dot(member_b, msg[...].reshape(25 * hidden, edges), 1, 1).astype(BF16)
    while any(done[i] < last_stage for i in done):
        for i in range(items):
            if done[i] < last_stage:
                done[i] += 1
                advance(i, done[i])

    for copy in returns:
        copy.wait_recv()
    total = grad_ref[...]
    for side, list_ref in ((0, right_ref), (1, left_ref)):
        ids = lax.broadcasted_iota(jnp.int32, (atoms, slots), 0)
        place = (ids == list_ref[...]).astype(F32).astype(BF16)
        total = total + dot(place, back[side], 1, 0)
    grad_ref[...] = total
    for i in range(items):
        for z in range(1, depth):
            flights["last", z, i].wait_recv()
    for copy in sides + returns + started:
        copy.wait_send()


def slab(n, depth, features, cotangent, rotation, src, tgt, send_left, send_right, weights):
    atoms = features.shape[0]
    edges = src.shape[1]
    slots = send_left.shape[1]
    heads = weights[6].shape[1]
    head_width = n * weights[6].shape[0]
    channels = n * weights[5].shape[0]
    hidden = weights[1].shape[1] // 4
    half = n // 2
    w_shapes = [tuple(w.shape) for w in weights]
    block = w_shapes[0][0]
    t_shapes = w_shapes[1:5] + [(block, 5 * hidden), (block, w_shapes[0][1] - 5 * hidden)]
    t_shapes += w_shapes[5:]
    sizes = {"weights": w_shapes, "terms": t_shapes}
    count, items = len(w_shapes), len(t_shapes)

    def layered(t):
        return (depth, t[0] if t[0] % depth else t[0] // depth, t[1])

    def lower(t):
        return (max(depth - 1, 1), *layered(t)[1:])

    shape = jax.ShapeDtypeStruct
    vmem = pl.BlockSpec(memory_space=pltpu.VMEM)
    out_shape = [shape((atoms, 25 * hidden), BF16), shape((atoms, 25 * channels), F32)]
    out_shape += [shape(layered(t), BF16) for t in t_shapes]
    rows = atoms + 2 * slots
    mixed = w_shapes[0][1]
    rots = rotation.shape[1]
    dma = pltpu.SemaphoreType.DMA
    scratch = [
        pltpu.VMEM((rows, 25 * channels), BF16),
        pltpu.VMEM((head_width, heads), F32),
        pltpu.VMEM((head_width, heads), F32),
        pltpu.VMEM((rots, edges), F32),
        pltpu.VMEM((25, channels, edges), F32),
        pltpu.VMEM((19, channels, edges), BF16),
        pltpu.VMEM((19, hidden, edges), F32),
        pltpu.VMEM((25, hidden, edges), BF16),
        pltpu.VMEM((25, hidden, edges), F32),
        pltpu.VMEM((head_width * heads, edges), F32),
        pltpu.VMEM((19, hidden, edges), BF16),
        pltpu.VMEM((mixed, edges), BF16),
        pltpu.VMEM((19, channels, edges), F32),
        pltpu.VMEM((25, channels, edges), BF16),
        pltpu.VMEM((2, heads, edges), F32),
        pltpu.VMEM((2, hidden, edges), F32),
    ]
    scratch += [pltpu.VMEM((2, slots, 25 * channels), BF16) for _ in range(4)]
    scratch += [pltpu.VMEM((half, 2, *w), BF16) for w in w_shapes]
    scratch += [pltpu.VMEM((n * w[0], w[1]) if w[0] % 16 else (8, 128), F32) for w in w_shapes]
    scratch += [pltpu.VMEM((half, 2, *t), BF16) for t in t_shapes]
    scratch += [pltpu.VMEM((half, *t), BF16) for t in t_shapes]
    scratch += [pltpu.VMEM((half - 1, *t), BF16) for _ in range(2) for t in t_shapes]
    scratch += [pltpu.VMEM(layered(t), F32) for t in t_shapes]
    scratch += [pltpu.VMEM(lower(t), BF16) for _ in range(2) for t in t_shapes]
    steps, deep = Halving(half).steps, Halving(depth).steps
    scratch += [dma((4,)) for _ in range(2)]
    scratch += [dma((half - 1, count)) for _ in range(2)]
    scratch += [dma((half, count)) for _ in range(2)]
    scratch += [dma((items,)) for _ in range(2)]
    scratch += [dma((steps, items)) for _ in range(2)]
    scratch += [dma((deep, items)) for _ in range(2)]
    scratch += [dma((depth, items)) for _ in range(2)]
    return pl.pallas_call(
        partial(slab_kernel, n, depth, sizes),
        out_shape=tuple(out_shape),
        in_specs=[vmem] * (7 + count),
        out_specs=[vmem] * (2 + items),
        scratch_shapes=scratch,
        compiler_params=pltpu.CompilerParams(
            collective_id=0, has_side_effects=True, vmem_limit_bytes=60 * 2**20),
        name="slab",
    )(features, cotangent, rotation, src, tgt, send_left, send_right, *weights)


def finish_kernel(items, hidden, *refs):
    att_ref, grad_ref = refs[:2]
    final = refs[2:2 + items]
    out_att, out_grad = refs[2 + items:4 + items]
    gz_ref, g1r_ref, g1i_ref, g2r_ref, g2i_ref, gt_ref, ga_ref = refs[4 + items:]
    out_att[...] = att_ref[...]
    out_grad[...] = grad_ref[...]

    def unfold(source, grad, begin):
        depth, size, wide = source.shape
        part = slice(begin, begin + wide)
        if size == grad.shape[0]:
            value = source[0].astype(F32)
            for k in range(1, depth):
                value = value + source[k].astype(F32)
            grad[:, part] = value
        else:
            for k in range(depth):
                grad[k * size:(k + 1) * size, part] = source[k].astype(F32)

    unfold(final[0], g1r_ref, 0)
    unfold(final[1], g1i_ref, 0)
    unfold(final[2], g2r_ref, 0)
    unfold(final[3], g2i_ref, 0)
    unfold(final[4], gz_ref, 0)
    unfold(final[5], gz_ref, 5 * hidden)
    unfold(final[6], gt_ref, 0)
    unfold(final[7], ga_ref, 0)


def finish(attended, grad, final, weights, hidden):
    items = len(final)
    vmem = pl.BlockSpec(memory_space=pltpu.VMEM)
    shapes = [jax.ShapeDtypeStruct(attended.shape, BF16), jax.ShapeDtypeStruct(grad.shape, F32)]
    shapes += [jax.ShapeDtypeStruct(w.shape, F32) for w in weights]
    return pl.pallas_call(
        partial(finish_kernel, items, hidden),
        out_shape=tuple(shapes),
        in_specs=[vmem] * (2 + items),
        out_specs=[vmem] * len(shapes),
        name="finish",
    )(attended, grad, *final)


def body(n, depth, features, cotangent, rotation, send_left, send_right, edge_src, edge_tgt,
         *weights):
    turned_rotation = jnp.swapaxes(rotation[0], 0, 1)
    attended, grad_features, *final = slab(
        n, depth, features[0], cotangent[0], turned_rotation, edge_src, edge_tgt,
        send_left, send_right, weights)
    attended, grad_features, *grads = finish(
        attended, grad_features, final, weights, weights[1].shape[1] // 4)
    return (attended[None], grad_features[None], *grads)


def solution(mesh):
    cell = P("dp", "graph", None)
    lists = P("dp", "graph")
    shard = P("graph", None)
    in_specs = (cell, cell, P("dp", None, "graph")) + (lists,) * 4 + (shard,) * 7
    out_specs = (cell, cell) + (shard,) * 7
    return jax.shard_map(
        partial(body, mesh.shape["graph"], mesh.shape["dp"]), mesh=mesh,
        in_specs=in_specs, out_specs=out_specs, check_vma=False)
```

```python
from functools import partial

import jax
import jax.numpy as jnp
from jax import lax
from jax.experimental import pallas as pl
from jax.experimental.pallas import tpu as pltpu
from jax.sharding import PartitionSpec as P

F32 = jnp.float32
BF16 = jnp.bfloat16
OFFSETS = {1: 0, 2: 9, 3: 34, 4: 69}
DEGREES = (1, 2, 3, 4)
BLOCK_C = 32
BLOCK_H = 16
MESH = pl.DeviceIdType.MESH
EXACT = lax.Precision.HIGHEST
ORDER = (
    "g1r", "s0", "g1i", "s1", "gzv", "s3", "ds0", "s4", "x0", "ds1", "s5", "x1", "g2", "s2",
    "x3", "gwt", "s6", "s7", "dt0", "dt1", "dt2", "x4", "tb0", "y0", "y1", "tb1", "eg", "y3",
    "x5", "y4", "a0", "x2", "a1", "x6", "a3", "x7", "y5", "b0", "a4", "b1", "y2", "y6", "y7",
    "ghost", "att", "a5", "b3", "c0", "b4", "a2", "c1", "a6", "a7", "b5", "d0", "c3", "b2",
    "d1", "b6", "c4", "b7", "c5", "c2", "d3", "c6", "c7", "d4", "d5", "d2", "d6", "d7",
)


def slot(degree, azimuth):
    return {0: degree, 1: 4 + degree, -1: 8 + degree, 2: 11 + degree, -2: 14 + degree}[azimuth]


def orders(degree):
    kept = min(degree, 2)
    return range(-kept, kept + 1)


def rot_row(degree, azimuth, column):
    return OFFSETS[degree] + (azimuth + min(degree, 2)) * (2 * degree + 1) + column


def dot(a, b, ca, cb, precision=None):
    return lax.dot_general(
        a, b, (((ca,), (cb,)), ((), ())), preferred_element_type=F32, precision=precision
    )


def flip(index, power):
    bit = lax.rem(lax.div(index, power), 2)
    return index + (1 - 2 * bit) * power


def flips(index, powers, chosen):
    for j in chosen:
        index = flip(index, powers[j])
    return index


def subsets(steps):
    found = [()]
    for j in steps:
        found = found + [s + (j,) for s in found]
    return found


class Halving:
    def __init__(self, count):
        self.steps = count.bit_length() - 1
        self.rest = [subsets(range(j + 1, self.steps)) for j in range(self.steps)]
        self.base = [0]
        for found in self.rest:
            self.base.append(self.base[-1] + len(found))

    def spot(self, step, chosen):
        return self.base[step] + self.rest[step].index(chosen)


def slab_kernel(n, depth, sizes, *refs):
    take = iter(refs)
    feat_ref, cot_ref, rot_ref, src_ref, tgt_ref, left_ref, right_ref = [next(take) for _ in range(7)]
    count = len(sizes["weights"])
    items = len(sizes["terms"])
    shards = [next(take) for _ in range(count)]
    att_ref, grad_ref = next(take), next(take)
    final = [next(take) for _ in range(items)]
    (ext_ref, alphas, d_alphas, rotf, xs, turned, hid, msg, dmsg, scores, dhid, dmixed, dturned,
     dxs, small, spreads) = [next(take) for _ in range(16)]
    outgoing, near, ghost, back = [next(take) for _ in range(4)]
    full = [next(take) for _ in range(count)]
    mats = [next(take) for _ in range(count)]
    terms = [next(take) for _ in range(items)]
    landed = [next(take) for _ in range(items)]
    out_xy = [next(take) for _ in range(items)]
    in_xy = [next(take) for _ in range(items)]
    layers = [next(take) for _ in range(items)]
    out_z = [next(take) for _ in range(items)]
    in_z = [next(take) for _ in range(items)]
    (side_send, side_recv, hop_send, hop_recv, core_send, core_recv, sib_send, sib_recv,
     xy_send, xy_recv, z_send, z_recv) = list(take)

    edges = src_ref.shape[1]
    rows = ext_ref.shape[0]
    atoms = att_ref.shape[0]
    channels = n * sizes["weights"][5][0]
    hidden = sizes["weights"][1][1] // 4
    heads = small.shape[1]
    width = alphas.shape[0]
    slots = left_ref.shape[1]

    me = lax.axis_index("graph")
    row = lax.axis_index("dp")
    half = n // 2
    chip = lax.div(me, 2)
    parity = lax.rem(me, 2)
    sibling = me + 1 - 2 * parity
    right, left = lax.rem(me + 1, n), lax.rem(me + n - 1, n)
    plan = Halving(half)
    steps = plan.steps
    powers = [2 ** j + parity * (2 ** ((j + 1) % steps) - 2 ** j) for j in range(steps)]

    upper = lax.div(row, depth // 2)
    inward = row + 1 - 2 * upper
    outward = row - 1 + 2 * upper
    from_end = row + upper * (depth - 1 - 2 * row)
    at_middle = lax.div(from_end + 1, depth // 2)
    is_end = from_end == 0
    is_middle = at_middle == 1

    barrier = pltpu.get_barrier_semaphore()
    partners = [(row, sibling), (row, right), (row, left)]
    partners += [(row, 2 * flip(chip, p) + parity) for p in powers]
    for partner in partners:
        pl.semaphore_signal(barrier, inc=1, device_id=partner, device_id_type=MESH)
    for z in (-1, 1):
        other = row + z

        @pl.when((other >= 0) & (other < depth))
        def _():
            pl.semaphore_signal(barrier, inc=1, device_id=(other, me), device_id_type=MESH)

    def remote(src, dst, send, recv, target):
        copy = pltpu.make_async_remote_copy(
            src_ref=src, dst_ref=dst, send_sem=send, recv_sem=recv,
            device_id=target, device_id_type=MESH)
        copy.start()
        return copy

    started = []

    own = feat_ref[...].astype(BF16)
    ext_ref[:atoms, :] = own
    for side, list_ref in ((0, left_ref), (1, right_ref)):
        ids = lax.broadcasted_iota(jnp.int32, (atoms, slots), 0)
        pick = (ids == list_ref[...]).astype(F32).astype(BF16)
        outgoing[side] = dot(pick, own, 0, 0).astype(BF16)
    for w in range(count):
        full[w][chip, parity] = shards[w][...]
    src_hot = (
        lax.broadcasted_iota(jnp.int32, (rows, edges), 0) == src_ref[...]
    ).astype(F32).astype(BF16)
    member = (lax.broadcasted_iota(jnp.int32, (atoms, edges), 0) == tgt_ref[...]).astype(F32)
    member_b = member.astype(BF16)

    pl.semaphore_wait(barrier, len(partners) + 1 + lax.div(from_end + depth - 1, depth))

    sides = []
    for side, target in ((1, left), (0, right)):
        sides.append(remote(outgoing.at[1 - side], near.at[side], side_send.at[side],
                            side_recv.at[side], (row, target)))
    arrivals = {}

    def hop(j, w):
        target = (row, 2 * flip(chip, powers[j]) + parity)
        for t, chosen in enumerate(subsets(range(j))):
            unit = flips(chip, powers, chosen)
            source = shards[w] if j == 0 else full[w].at[unit, parity]
            copy = remote(source, full[w].at[unit, parity], hop_send.at[2 ** j + t - 1, w],
                          hop_recv.at[2 ** j + t - 1, w], target)
            arrivals[j, t, w] = copy
            started.append(copy)

    crossing = {}

    def cross(spot, unit, w, source=None):
        copy = remote(full[w].at[unit, parity] if source is None else source,
                      full[w].at[unit, parity], core_send.at[spot, w], core_recv.at[spot, w],
                      (row, sibling))
        crossing[spot, w] = copy
        started.append(copy)

    def land(j, w):
        partner = flip(chip, powers[j])
        for t, chosen in enumerate(subsets(range(j))):
            arrivals[j, t, w].wait_recv()
            cross(2 ** j + t, flips(partner, powers, chosen), w)

    weight_order = (0, 5, 6, 1, 2, 3, 4)
    for w in weight_order:
        hop(0, w)
    for w in weight_order:
        cross(0, chip, w, shards[w])

    edge_eye = (
        lax.broadcasted_iota(jnp.int32, (rot_ref.shape[1], rot_ref.shape[1]), 0)
        == lax.broadcasted_iota(jnp.int32, (rot_ref.shape[1], rot_ref.shape[1]), 1)
    ).astype(F32).astype(BF16)
    rotf[...] = dot(edge_eye, rot_ref[...], 1, 1)
    for k in range(25):
        dmsg[k] = dot(
            cot_ref[:, k * hidden:(k + 1) * hidden].astype(BF16), member_b, 0, 0
        )
    for copy in sides:
        copy.wait_recv()
    ext_ref[atoms:, :] = near[...].astype(F32).reshape(rows - atoms, -1).astype(BF16)
    for k in range(25):
        xs[k] = dot(ext_ref[:, k * channels:(k + 1) * channels], src_hot, 0, 0)

    for j in range(1, steps):
        for w in weight_order:
            land(j - 1, w)
            hop(j, w)

    def turn(i, carry):
        part = pl.ds(pl.multiple_of(i * BLOCK_C, BLOCK_C), BLOCK_C)
        turned[0, part, :] = xs[0, part, :].astype(BF16)
        for degree in DEGREES:
            for azimuth in orders(degree):
                total = None
                for m in range(2 * degree + 1):
                    k = rot_row(degree, azimuth, m)
                    term = rotf[k:k + 1, :] * xs[degree * degree + m, part, :]
                    total = term if total is None else total + term
                turned[slot(degree, azimuth), part, :] = total.astype(BF16)
        return carry

    lax.fori_loop(0, channels // BLOCK_C, turn, 0)

    zero_in = turned[0:5].reshape(5 * channels, edges)
    one_pos = turned[5:9].reshape(4 * channels, edges)
    one_neg = turned[9:13].reshape(4 * channels, edges)
    two_pos = turned[13:16].reshape(3 * channels, edges)
    two_neg = turned[16:19].reshape(3 * channels, edges)

    def settle(w):
        for spot in range(half):
            crossing[spot, w].wait_recv()
        block = sizes["weights"][w][0]
        if block % 16:
            for u in range(half):
                for c in range(2):
                    at = (2 * u + c) * block
                    mats[w][at:at + block, :] = full[w][u, c].astype(mats[w].dtype)

    def weight(w, begin=0, end=None):
        block, wide = sizes["weights"][w]
        end = wide if end is None else end
        if block % 16:
            return mats[w][:, begin:end].astype(BF16)
        return full[w][:, :, :, begin:end].reshape(n * block, end - begin)

    for w in (0, 5, 6):
        land(steps - 1, w)
    for w in (1, 2):
        land(steps - 1, w)
    for w in (0, 5, 6):
        settle(w)
    alpha_rows = sizes["weights"][6][0]
    for u in range(half):
        for c in range(2):
            at = (2 * u + c) * alpha_rows
            alphas[at:at + alpha_rows, :] = full[6][u, c].astype(F32)

    per_atom = dot(ext_ref[:atoms, :channels], weight(5), 1, 0)
    high = per_atom.astype(BF16)
    low = (per_atom - high.astype(F32)).astype(BF16)
    scores[...] = (
        dot(weight(0, 5 * hidden), zero_in, 0, 0)
        + dot(high, member_b, 0, 0)
        + dot(low, member_b, 0, 0)
    )
    hid[0:5] = dot(weight(0, 0, 5 * hidden), zero_in, 0, 0).reshape(5, hidden, edges)

    for w in (3, 4):
        land(steps - 1, w)

    for h in range(heads):
        part = slice(h * width, (h + 1) * width)
        value = scores[part, :]
        centre = value - jnp.mean(value, axis=0, keepdims=True)
        scale = lax.rsqrt(jnp.mean(centre * centre, axis=0, keepdims=True) + 1e-05)
        normed = centre * scale
        scores[part, :] = normed
        gate = 0.2 + 0.8 * jax.nn.sigmoid(normed)
        small[0, h:h + 1, :] = jnp.sum(
            normed * gate * alphas[:, h:h + 1], axis=0, keepdims=True
        )
        small[1, h:h + 1, :] = scale

    raised = jnp.exp(small[0])
    totals = dot(dot(raised, member, 1, 1, EXACT), member, 1, 0, EXACT)
    weights = raised / totals
    spreads[0] = jnp.broadcast_to(
        weights[:, None, :], (heads, hidden // heads, edges)
    ).reshape(hidden, edges)

    settle(1)
    settle(2)
    hid[5:9] = (dot(weight(1), one_pos, 0, 0) - dot(weight(2), one_neg, 0, 0)).reshape(
        4, hidden, edges)
    hid[9:13] = (dot(weight(1), one_neg, 0, 0) + dot(weight(2), one_pos, 0, 0)).reshape(
        4, hidden, edges)
    settle(3)
    settle(4)
    hid[13:16] = (dot(weight(3), two_pos, 0, 0) - dot(weight(4), two_neg, 0, 0)).reshape(
        3, hidden, edges)
    hid[16:19] = (dot(weight(3), two_neg, 0, 0) + dot(weight(4), two_pos, 0, 0)).reshape(
        3, hidden, edges)

    def mix(i, carry):
        part = pl.ds(pl.multiple_of(i * BLOCK_H, BLOCK_H), BLOCK_H)
        spread = spreads[0, part, :]
        scalar = hid[0, part, :]
        gating = jax.nn.sigmoid(scalar)
        silu = scalar * gating
        both = gating * spread
        msg[0, part, :] = (silu * spread).astype(BF16)
        d_first = dmsg[0, part, :]
        inner = jnp.zeros_like(scalar)
        for degree in DEGREES:
            size = 2 * degree + 1
            sums = [None] * size
            for azimuth in orders(degree):
                raw = hid[slot(degree, azimuth), part, :]
                value = raw * both
                back_sum = None
                for m in range(size):
                    k = rot_row(degree, azimuth, m)
                    line = rotf[k:k + 1, :]
                    term = line * value
                    sums[m] = term if sums[m] is None else sums[m] + term
                    other = line * dmsg[degree * degree + m, part, :]
                    back_sum = other if back_sum is None else back_sum + other
                inner = inner + back_sum * raw
                dhid[slot(degree, azimuth), part, :] = (back_sum * both).astype(BF16)
            for m in range(size):
                msg[degree * degree + m, part, :] = sums[m].astype(BF16)
        spreads[1, part, :] = inner * gating + d_first * silu
        d_scalar = d_first * spread * gating * (1.0 + scalar * (1.0 - gating)) + (
            inner * spread * gating * (1.0 - gating)
        )
        dhid[0, part, :] = d_scalar.astype(BF16)
        return carry

    lax.fori_loop(0, hidden // BLOCK_H, mix, 0)

    def put(i, value, begin=0):
        block = sizes["terms"][i][0]
        wide = value.shape[1]
        if block % 16:
            for u in range(half):
                for c in range(2):
                    at = (2 * u + c) * block
                    terms[i][u, c, :, begin:begin + wide] = value[at:at + block, :].astype(BF16)
        else:
            terms[i][:, :, :, begin:begin + wide] = value.astype(BF16).reshape(
                half, 2, block, wide)

    flights = {}

    def launch(key, src, dst, send, recv, target):
        copy = remote(src, dst, send, recv, target)
        flights[key] = copy
        started.append(copy)

    def to_sibling(i):
        launch(("core", i), terms[i].at[:, 1 - parity], landed[i], sib_send.at[i], sib_recv.at[i],
               (row, sibling))

    def chip_sum(i, step, chosen):
        unit = flips(chip, powers, chosen)
        total = terms[i][unit, parity].astype(F32) + landed[i][unit].astype(F32)
        for s in range(step):
            total = total + in_xy[i][plan.spot(s, chosen)].astype(F32)
        return total

    def to_chip(i, step):
        if step == 0:
            flights["core", i].wait_recv()
        else:
            flights["xy", step - 1, i].wait_recv()
        begin, end = plan.base[step], plan.base[step + 1]
        for t, rest in enumerate(plan.rest[step]):
            out_xy[i][begin + t] = chip_sum(i, step, (step,) + rest).astype(BF16)
        target = (row, 2 * flip(chip, powers[step]) + parity)
        launch(("xy", step, i), out_xy[i].at[begin:end], in_xy[i].at[begin:end],
               xy_send.at[step, i], xy_recv.at[step, i], target)

    def inward_copy(i):
        return pltpu.make_async_remote_copy(
            src_ref=out_z[i], dst_ref=in_z[i].at[at_middle],
            send_sem=z_send.at[0, i], recv_sem=z_recv.at[at_middle, i],
            device_id=(inward, me), device_id_type=MESH)

    def arrival(i, spot):
        return pltpu.make_async_remote_copy(
            src_ref=out_z[i], dst_ref=in_z[i].at[spot],
            send_sem=z_send.at[0, i], recv_sem=z_recv.at[spot, i],
            device_id=(inward, me), device_id_type=MESH)

    def outward_copy(i):
        return pltpu.make_async_remote_copy(
            src_ref=final[i], dst_ref=final[i],
            send_sem=z_send.at[1, i], recv_sem=z_recv.at[2, i],
            device_id=(outward, me), device_id_type=MESH)

    def on_line(i, stage):
        if stage == 0:
            flights["xy", steps - 1, i].wait_recv()
            total = chip_sum(i, steps, ())
            layers[i][...] = total
            out_z[i][...] = total.astype(BF16)

            @pl.when(is_end)
            def _():
                inward_copy(i).start()
        elif stage == 1:
            @pl.when(jnp.logical_not(is_end))
            def _():
                arrival(i, 0).wait_recv()
                out_z[i][...] = (layers[i][...] + in_z[i][0].astype(F32)).astype(BF16)
                inward_copy(i).start()
        elif stage == 2:
            @pl.when(is_middle)
            def _():
                arrival(i, 1).wait_recv()
                final[i][...] = (out_z[i][...].astype(F32) + in_z[i][1].astype(F32)).astype(BF16)
                if depth > 2:
                    outward_copy(i).start()
        else:
            @pl.when(jnp.logical_not(is_middle))
            def _():
                outward_copy(i).wait_recv()
                if depth > 4:
                    @pl.when(jnp.logical_not(is_end))
                    def _():
                        outward_copy(i).start()

    def advance(i, stage):
        if stage == 0:
            to_sibling(i)
        elif stage <= steps:
            to_chip(i, stage - 1)
        else:
            on_line(i, stage - 1 - steps)

    def bands(first, number):
        middle = first + number
        last = middle + number
        return (dhid[first:middle].reshape(number * hidden, edges),
                dhid[middle:last].reshape(number * hidden, edges))

    def one_re():
        up, down = bands(5, 4)
        put(0, dot(one_pos, up, 1, 1) + dot(one_neg, down, 1, 1))

    def one_im():
        up, down = bands(5, 4)
        put(1, dot(one_pos, down, 1, 1) - dot(one_neg, up, 1, 1))

    def two():
        up, down = bands(13, 3)
        put(2, dot(two_pos, up, 1, 1) + dot(two_neg, down, 1, 1))
        put(2, dot(two_pos, down, 1, 1) - dot(two_neg, up, 1, 1), 3 * hidden)

    def values():
        d_values = dhid[0:5].reshape(5 * hidden, edges)
        dmixed[:5 * hidden, :] = d_values
        put(3, dot(zero_in, d_values, 1, 1))

    def score_grads(which):
        if which == 0:
            d_weights = jnp.sum(
                spreads[1].reshape(heads, hidden // heads, edges), axis=1
            )
            product = weights * d_weights
            small[0] = product - weights * dot(
                dot(product, member, 1, 1, EXACT), member, 1, 0, EXACT
            )
        group = heads // 2
        for h in range(which * group, (which + 1) * group):
            part = slice(h * width, (h + 1) * width)
            normed = scores[part, :]
            sig = jax.nn.sigmoid(normed)
            gate = 0.2 + 0.8 * sig
            d_logit = small[0, h:h + 1, :]
            d_alphas[:, h:h + 1] = jnp.sum(normed * gate * d_logit, axis=1, keepdims=True)
            d_norm = d_logit * alphas[:, h:h + 1] * (gate + 0.8 * normed * sig * (1.0 - sig))
            first = jnp.mean(d_norm, axis=0, keepdims=True)
            second = jnp.mean(d_norm * normed, axis=0, keepdims=True)
            d_score = small[1, h:h + 1, :] * (d_norm - first - normed * second)
            dmixed[5 * hidden + h * width:5 * hidden + (h + 1) * width, :] = d_score.astype(BF16)
            scores[part, :] = d_score
        begin = 5 * hidden + which * group * width
        put(4 + which, dot(zero_in, dmixed[begin:begin + group * width, :], 1, 1))

    held = {}

    def target_alpha():
        held["atom"] = dot(member, scores[...], 1, 1, EXACT).astype(BF16)
        put(6, dot(ext_ref[:atoms, :channels], held["atom"], 0, 0))
        for u in range(half):
            for c in range(2):
                at = (2 * u + c) * alpha_rows
                terms[7][u, c] = d_alphas[at:at + alpha_rows, :].astype(BF16)

    def turn_zero():
        dturned[0:5] = dot(weight(0), dmixed[...], 1, 0).reshape(5, channels, edges)

    def turn_pair(first, number, re_item, im_item):
        up, down = bands(first, number)
        middle = first + number
        last = middle + number
        dturned[first:middle] = (
            dot(weight(re_item), up, 1, 0) + dot(weight(im_item), down, 1, 0)
        ).reshape(number, channels, edges)
        dturned[middle:last] = (
            dot(weight(re_item), down, 1, 0) - dot(weight(im_item), up, 1, 0)
        ).reshape(number, channels, edges)

    def turn_back(i, carry):
        part = pl.ds(pl.multiple_of(i * BLOCK_C, BLOCK_C), BLOCK_C)
        dxs[0, part, :] = dturned[0, part, :].astype(BF16)
        for degree in DEGREES:
            for m in range(2 * degree + 1):
                total = None
                for azimuth in orders(degree):
                    k = rot_row(degree, azimuth, m)
                    term = rotf[k:k + 1, :] * dturned[slot(degree, azimuth), part, :]
                    total = term if total is None else total + term
                dxs[degree * degree + m, part, :] = total.astype(BF16)
        return carry

    blocks = channels // BLOCK_C

    def source_grads():
        d_target = dot(held["atom"], weight(5), 1, 1)
        ext_grad = dot(src_hot, dxs[...].reshape(25 * channels, edges), 1, 1)
        grad_ref[...] = ext_grad[:atoms]
        grad_ref[:, :channels] = ext_grad[:atoms, :channels] + d_target
        for side in range(2):
            begin = atoms + side * slots
            ghost[side] = ext_grad[begin:begin + slots].astype(BF16)

    returns = []

    def return_ghosts():
        for side, target in ((0, left), (1, right)):
            returns.append(remote(ghost.at[side], back.at[side], side_send.at[2 + side],
                                  side_recv.at[2 + side], (row, target)))

    def attend():
        att_ref[...] = dot(member_b, msg[...].reshape(25 * hidden, edges), 1, 1).astype(BF16)

    work = {
        "g1r": one_re, "g1i": one_im, "g2": two, "gzv": values,
        "ds0": partial(score_grads, 0), "ds1": partial(score_grads, 1), "gwt": target_alpha,
        "dt0": turn_zero, "dt1": partial(turn_pair, 5, 4, 1, 2),
        "dt2": partial(turn_pair, 13, 3, 3, 4),
        "tb0": lambda: lax.fori_loop(0, blocks // 2, turn_back, 0),
        "tb1": lambda: lax.fori_loop(blocks // 2, blocks, turn_back, 0),
        "eg": source_grads, "ghost": return_ghosts, "att": attend,
    }
    for step in ORDER:
        if step in work:
            work[step]()
        else:
            first, last = {
                "s": (0, 1), "x": (1, 2), "y": (2, 1 + steps), "a": (1 + steps, 2 + steps),
                "b": (2 + steps, 3 + steps), "c": (3 + steps, 4 + steps),
                "d": (4 + steps, 5 + steps)}[step[0]]
            for stage in range(first, last):
                for i in step[1:]:
                    advance(int(i), stage)

    for copy in returns:
        copy.wait_recv()
    total = grad_ref[...]
    for side, list_ref in ((0, right_ref), (1, left_ref)):
        ids = lax.broadcasted_iota(jnp.int32, (atoms, slots), 0)
        place = (ids == list_ref[...]).astype(F32).astype(BF16)
        total = total + dot(place, back[side], 1, 0)
    grad_ref[...] = total
    for i in range(items):
        inward_copy(i).wait_send()
        if depth > 2:
            @pl.when(jnp.logical_not(is_end))
            def _():
                outward_copy(i).wait_send()
    for copy in sides + returns + started:
        copy.wait_send()


def slab(n, depth, features, cotangent, rotation, src, tgt, send_left, send_right, weights):
    atoms = features.shape[0]
    edges = src.shape[1]
    slots = send_left.shape[1]
    heads = weights[6].shape[1]
    head_width = n * weights[6].shape[0]
    channels = n * weights[5].shape[0]
    hidden = weights[1].shape[1] // 4
    half = n // 2
    w_shapes = [tuple(w.shape) for w in weights]
    block = w_shapes[0][0]
    logits = (w_shapes[0][1] - 5 * hidden) // 2
    t_shapes = w_shapes[1:3] + [(w_shapes[3][0], 6 * hidden), (block, 5 * hidden)]
    t_shapes += [(block, logits)] * 2 + w_shapes[5:]
    sizes = {"weights": w_shapes, "terms": t_shapes}
    count, items = len(w_shapes), len(t_shapes)

    shape = jax.ShapeDtypeStruct
    vmem = pl.BlockSpec(memory_space=pltpu.VMEM)
    out_shape = [shape((atoms, 25 * hidden), BF16), shape((atoms, 25 * channels), F32)]
    out_shape += [shape(t, BF16) for t in t_shapes]
    rows = atoms + 2 * slots
    mixed = w_shapes[0][1]
    rots = rotation.shape[1]
    dma = pltpu.SemaphoreType.DMA
    scratch = [
        pltpu.VMEM((rows, 25 * channels), BF16),
        pltpu.VMEM((head_width, heads), F32),
        pltpu.VMEM((head_width, heads), F32),
        pltpu.VMEM((rots, edges), F32),
        pltpu.VMEM((25, channels, edges), F32),
        pltpu.VMEM((19, channels, edges), BF16),
        pltpu.VMEM((19, hidden, edges), F32),
        pltpu.VMEM((25, hidden, edges), BF16),
        pltpu.VMEM((25, hidden, edges), F32),
        pltpu.VMEM((head_width * heads, edges), F32),
        pltpu.VMEM((19, hidden, edges), BF16),
        pltpu.VMEM((mixed, edges), BF16),
        pltpu.VMEM((19, channels, edges), F32),
        pltpu.VMEM((25, channels, edges), BF16),
        pltpu.VMEM((2, heads, edges), F32),
        pltpu.VMEM((2, hidden, edges), F32),
    ]
    scratch += [pltpu.VMEM((2, slots, 25 * channels), BF16) for _ in range(4)]
    scratch += [pltpu.VMEM((half, 2, *w), BF16) for w in w_shapes]
    scratch += [pltpu.VMEM((n * w[0], w[1]) if w[0] % 16 else (8, 128), F32) for w in w_shapes]
    scratch += [pltpu.VMEM((half, 2, *t), BF16) for t in t_shapes]
    scratch += [pltpu.VMEM((half, *t), BF16) for t in t_shapes]
    scratch += [pltpu.VMEM((half - 1, *t), BF16) for _ in range(2) for t in t_shapes]
    scratch += [pltpu.VMEM(t, F32) for t in t_shapes]
    scratch += [pltpu.VMEM(t, BF16) for t in t_shapes]
    scratch += [pltpu.VMEM((2, *t), BF16) for t in t_shapes]
    steps = Halving(half).steps
    scratch += [dma((4,)) for _ in range(2)]
    scratch += [dma((half - 1, count)) for _ in range(2)]
    scratch += [dma((half, count)) for _ in range(2)]
    scratch += [dma((items,)) for _ in range(2)]
    scratch += [dma((steps, items)) for _ in range(2)]
    scratch += [dma((2, items)), dma((3, items))]
    return pl.pallas_call(
        partial(slab_kernel, n, depth, sizes),
        out_shape=tuple(out_shape),
        in_specs=[vmem] * (7 + count),
        out_specs=[vmem] * (2 + items),
        scratch_shapes=scratch,
        compiler_params=pltpu.CompilerParams(
            collective_id=0, has_side_effects=True, vmem_limit_bytes=60 * 2**20),
        name="slab",
    )(features, cotangent, rotation, src, tgt, send_left, send_right, *weights)


def finish_kernel(items, hidden, *refs):
    att_ref, grad_ref = refs[:2]
    final = refs[2:2 + items]
    out_att, out_grad = refs[2 + items:4 + items]
    gz_ref, g1r_ref, g1i_ref, g2r_ref, g2i_ref, gt_ref, ga_ref = refs[4 + items:]
    out_att[...] = att_ref[...]
    out_grad[...] = grad_ref[...]

    wide = 3 * hidden
    g1r_ref[...] = final[0][...].astype(F32)
    g1i_ref[...] = final[1][...].astype(F32)
    g2r_ref[...] = final[2][:, :wide].astype(F32)
    g2i_ref[...] = final[2][:, wide:].astype(F32)
    begin = 0
    for source in final[3:6]:
        end = begin + source.shape[1]
        gz_ref[:, begin:end] = source[...].astype(F32)
        begin = end
    gt_ref[...] = final[6][...].astype(F32)
    ga_ref[...] = final[7][...].astype(F32)


def finish(attended, grad, final, weights, hidden):
    items = len(final)
    vmem = pl.BlockSpec(memory_space=pltpu.VMEM)
    shapes = [jax.ShapeDtypeStruct(attended.shape, BF16), jax.ShapeDtypeStruct(grad.shape, F32)]
    shapes += [jax.ShapeDtypeStruct(w.shape, F32) for w in weights]
    return pl.pallas_call(
        partial(finish_kernel, items, hidden),
        out_shape=tuple(shapes),
        in_specs=[vmem] * (2 + items),
        out_specs=[vmem] * len(shapes),
        name="finish",
    )(attended, grad, *final)


def body(n, depth, features, cotangent, rotation, send_left, send_right, edge_src, edge_tgt,
         *weights):
    turned_rotation = jnp.swapaxes(rotation[0], 0, 1)
    attended, grad_features, *final = slab(
        n, depth, features[0], cotangent[0], turned_rotation, edge_src, edge_tgt,
        send_left, send_right, weights)
    attended, grad_features, *grads = finish(
        attended, grad_features, final, weights, weights[1].shape[1] // 4)
    return (attended[None], grad_features[None], *grads)


def solution(mesh):
    cell = P("dp", "graph", None)
    lists = P("dp", "graph")
    shard = P("graph", None)
    in_specs = (cell, cell, P("dp", None, "graph")) + (lists,) * 4 + (shard,) * 7
    out_specs = (cell, cell) + (shard,) * 7
    return jax.shard_map(
        partial(body, mesh.shape["graph"], mesh.shape["dp"]), mesh=mesh,
        in_specs=in_specs, out_specs=out_specs, check_vma=False)
```

```python
from functools import partial

import jax
import jax.numpy as jnp
from jax import lax
from jax.experimental import pallas as pl
from jax.experimental.pallas import tpu as pltpu
from jax.sharding import PartitionSpec as P

F32 = jnp.float32
BF16 = jnp.bfloat16
OFFSETS = {1: 0, 2: 9, 3: 34, 4: 69}
DEGREES = (1, 2, 3, 4)
BLOCK_C = 32
BLOCK_H = 16
MESH = pl.DeviceIdType.MESH
EXACT = lax.Precision.HIGHEST
ORDER = (
    "g1r", "s0", "g1i", "s1", "gzv", "s3", "ds0", "s4", "x0", "ds1", "s5", "x1", "g2", "s2",
    "x3", "gwt", "s6", "s7", "dt0", "dt1", "dt2", "x4", "tb0", "y0", "y1", "tb1", "eg", "y3",
    "x5", "y4", "a0", "x2", "a1", "x6", "a3", "x7", "y5", "b0", "a4", "b1", "y2", "y6", "y7",
    "ghost", "att", "a5", "b3", "c0", "b4", "a2", "c1", "a6", "a7", "b5", "d0", "c3", "b2",
    "d1", "b6", "c4", "b7", "c5", "c2", "d3", "c6", "c7", "d4", "d5", "d2", "d6", "d7",
)


def slot(degree, azimuth):
    return {0: degree, 1: 4 + degree, -1: 8 + degree, 2: 11 + degree, -2: 14 + degree}[azimuth]


def orders(degree):
    kept = min(degree, 2)
    return range(-kept, kept + 1)


def rot_row(degree, azimuth, column):
    return OFFSETS[degree] + (azimuth + min(degree, 2)) * (2 * degree + 1) + column


def dot(a, b, ca, cb, precision=None):
    return lax.dot_general(
        a, b, (((ca,), (cb,)), ((), ())), preferred_element_type=F32, precision=precision
    )


def flip(index, power):
    bit = lax.rem(lax.div(index, power), 2)
    return index + (1 - 2 * bit) * power


def flips(index, powers, chosen):
    for j in chosen:
        index = flip(index, powers[j])
    return index


def subsets(steps):
    found = [()]
    for j in steps:
        found = found + [s + (j,) for s in found]
    return found


class Halving:
    def __init__(self, count):
        self.steps = count.bit_length() - 1
        self.rest = [subsets(range(j + 1, self.steps)) for j in range(self.steps)]
        self.base = [0]
        for found in self.rest:
            self.base.append(self.base[-1] + len(found))

    def spot(self, step, chosen):
        return self.base[step] + self.rest[step].index(chosen)


def slab_kernel(n, depth, sizes, *refs):
    take = iter(refs)
    placed = [next(take) for _ in range(7)]
    count = len(sizes["weights"])
    items = len(sizes["terms"])
    shards = [next(take) for _ in range(count)]
    att_ref, grad_ref = next(take), next(take)
    final = [next(take) for _ in range(items)]
    (ext_ref, alphas, d_alphas, rotf, xs, turned, hid, msg, dmsg, scores, dhid, dmixed, dturned,
     dxs, small, spreads) = [next(take) for _ in range(16)]
    outgoing, near, ghost, back = [next(take) for _ in range(4)]
    full = [next(take) for _ in range(count)]
    mats = [next(take) for _ in range(count)]
    terms = [next(take) for _ in range(items)]
    landed = [next(take) for _ in range(items)]
    out_xy = [next(take) for _ in range(items)]
    in_xy = [next(take) for _ in range(items)]
    layers = [next(take) for _ in range(items)]
    out_z = [next(take) for _ in range(items)]
    in_z = [next(take) for _ in range(items)]
    (side_send, side_recv, hop_send, hop_recv, core_send, core_recv, sib_send, sib_recv,
     xy_send, xy_recv, z_send, z_recv, in_sem) = [next(take) for _ in range(13)]
    local = list(take)
    feat_ref, cot_ref, rot_ref, src_ref, tgt_ref, left_ref, right_ref = local

    edges = src_ref.shape[1]
    rows = ext_ref.shape[0]
    atoms = att_ref.shape[0]
    channels = n * sizes["weights"][5][0]
    hidden = sizes["weights"][1][1] // 4
    heads = small.shape[1]
    width = alphas.shape[0]
    slots = left_ref.shape[1]

    me = lax.axis_index("graph")
    row = lax.axis_index("dp")
    half = n // 2
    chip = lax.div(me, 2)
    parity = lax.rem(me, 2)
    sibling = me + 1 - 2 * parity
    right, left = lax.rem(me + 1, n), lax.rem(me + n - 1, n)
    plan = Halving(half)
    steps = plan.steps
    powers = [2 ** j + parity * (2 ** ((j + 1) % steps) - 2 ** j) for j in range(steps)]

    upper = lax.div(row, depth // 2)
    inward = row + 1 - 2 * upper
    outward = row - 1 + 2 * upper
    from_end = row + upper * (depth - 1 - 2 * row)
    at_middle = lax.div(from_end + 1, depth // 2)
    is_end = from_end == 0
    is_middle = at_middle == 1

    barrier = pltpu.get_barrier_semaphore()
    partners = [(row, sibling), (row, right), (row, left)]
    partners += [(row, 2 * flip(chip, p) + parity) for p in powers]
    for partner in partners:
        pl.semaphore_signal(barrier, inc=1, device_id=partner, device_id_type=MESH)
    for z in (-1, 1):
        other = row + z

        @pl.when((other >= 0) & (other < depth))
        def _():
            pl.semaphore_signal(barrier, inc=1, device_id=(other, me), device_id_type=MESH)

    def remote(src, dst, send, recv, target):
        copy = pltpu.make_async_remote_copy(
            src_ref=src, dst_ref=dst, send_sem=send, recv_sem=recv,
            device_id=target, device_id_type=MESH)
        copy.start()
        return copy

    started = []

    loads = {}

    def load(key, src, dst, spot):
        copy = pltpu.make_async_copy(src, dst, in_sem.at[spot])
        copy.start()
        loads[key] = copy

    for k in (0, 5, 6):
        load(k, placed[k], local[k], k)
    for w in range(count):
        load(("w", w), shards[w], full[w].at[chip, parity], 7 + w)
    for k in (3, 4, 2, 1):
        load(k, placed[k], local[k], k)
    for k in (0, 5, 6):
        loads[k].wait()
    own = feat_ref[...].astype(BF16)
    ext_ref[:atoms, :] = own
    for side, list_ref in ((0, left_ref), (1, right_ref)):
        ids = lax.broadcasted_iota(jnp.int32, (atoms, slots), 0)
        pick = (ids == list_ref[...]).astype(F32).astype(BF16)
        outgoing[side] = dot(pick, own, 0, 0).astype(BF16)
    for w in range(count):
        loads["w", w].wait()

    pl.semaphore_wait(barrier, len(partners) + 1 + lax.div(from_end + depth - 1, depth))

    sides = []
    for side, target in ((1, left), (0, right)):
        sides.append(remote(outgoing.at[1 - side], near.at[side], side_send.at[side],
                            side_recv.at[side], (row, target)))
    arrivals = {}

    def hop(j, w, part):
        target = (row, 2 * flip(chip, powers[j]) + parity)
        for t, chosen in enumerate(subsets(range(j))):
            if (t > 0) != part:
                continue
            unit = flips(chip, powers, chosen)
            copy = remote(full[w].at[unit, parity], full[w].at[unit, parity],
                          hop_send.at[2 ** j + t - 1, w], hop_recv.at[2 ** j + t - 1, w], target)
            arrivals[j, t, w] = copy
            started.append(copy)

    crossing = {}

    def cross(spot, unit, w):
        copy = remote(full[w].at[unit, parity], full[w].at[unit, parity],
                      core_send.at[spot, w], core_recv.at[spot, w], (row, sibling))
        crossing[spot, w] = copy
        started.append(copy)

    def land(j, w, part):
        partner = flip(chip, powers[j])
        for t, chosen in enumerate(subsets(range(j))):
            if (t > 0) == part:
                arrivals[j, t, w].wait_recv()
                cross(2 ** j + t, flips(partner, powers, chosen), w)

    weight_order = (0, 5, 6, 1, 2, 3, 4)
    for j in range(steps):
        for w in weight_order:
            hop(j, w, False)
    for w in weight_order:
        cross(0, chip, w)

    for k in (3, 4, 2, 1):
        loads[k].wait()
    src_hot = (
        lax.broadcasted_iota(jnp.int32, (rows, edges), 0) == src_ref[...]
    ).astype(F32).astype(BF16)
    member = (lax.broadcasted_iota(jnp.int32, (atoms, edges), 0) == tgt_ref[...]).astype(F32)
    member_b = member.astype(BF16)

    edge_eye = (
        lax.broadcasted_iota(jnp.int32, (rot_ref.shape[1], rot_ref.shape[1]), 0)
        == lax.broadcasted_iota(jnp.int32, (rot_ref.shape[1], rot_ref.shape[1]), 1)
    ).astype(F32).astype(BF16)
    rotf[...] = dot(edge_eye, rot_ref[...], 1, 1)
    for k in range(25):
        dmsg[k] = dot(
            cot_ref[:, k * hidden:(k + 1) * hidden].astype(BF16), member_b, 0, 0
        )
    for copy in sides:
        copy.wait_recv()
    ext_ref[atoms:, :] = near[...].astype(F32).reshape(rows - atoms, -1).astype(BF16)
    for k in range(25):
        xs[k] = dot(ext_ref[:, k * channels:(k + 1) * channels], src_hot, 0, 0)

    for j in range(1, steps):
        for w in weight_order:
            land(j - 1, w, False)
            land(j - 1, w, True)
            hop(j, w, True)

    def turn(i, carry):
        part = pl.ds(pl.multiple_of(i * BLOCK_C, BLOCK_C), BLOCK_C)
        turned[0, part, :] = xs[0, part, :].astype(BF16)
        for degree in DEGREES:
            for azimuth in orders(degree):
                total = None
                for m in range(2 * degree + 1):
                    k = rot_row(degree, azimuth, m)
                    term = rotf[k:k + 1, :] * xs[degree * degree + m, part, :]
                    total = term if total is None else total + term
                turned[slot(degree, azimuth), part, :] = total.astype(BF16)
        return carry

    lax.fori_loop(0, channels // BLOCK_C, turn, 0)

    zero_in = turned[0:5].reshape(5 * channels, edges)
    one_pos = turned[5:9].reshape(4 * channels, edges)
    one_neg = turned[9:13].reshape(4 * channels, edges)
    two_pos = turned[13:16].reshape(3 * channels, edges)
    two_neg = turned[16:19].reshape(3 * channels, edges)

    def settle(w):
        for spot in range(half):
            crossing[spot, w].wait_recv()
        block = sizes["weights"][w][0]
        if block % 16:
            for u in range(half):
                for c in range(2):
                    at = (2 * u + c) * block
                    mats[w][at:at + block, :] = full[w][u, c].astype(mats[w].dtype)

    def weight(w, begin=0, end=None):
        block, wide = sizes["weights"][w]
        end = wide if end is None else end
        if block % 16:
            return mats[w][:, begin:end].astype(BF16)
        return full[w][:, :, :, begin:end].reshape(n * block, end - begin)

    for w in weight_order:
        land(steps - 1, w, False)
    for w in (0, 5, 6, 1, 2):
        land(steps - 1, w, True)
    for w in (0, 5, 6):
        settle(w)
    alpha_rows = sizes["weights"][6][0]
    for u in range(half):
        for c in range(2):
            at = (2 * u + c) * alpha_rows
            alphas[at:at + alpha_rows, :] = full[6][u, c].astype(F32)

    per_atom = dot(ext_ref[:atoms, :channels], weight(5), 1, 0)
    high = per_atom.astype(BF16)
    low = (per_atom - high.astype(F32)).astype(BF16)
    scores[...] = (
        dot(weight(0, 5 * hidden), zero_in, 0, 0)
        + dot(high, member_b, 0, 0)
        + dot(low, member_b, 0, 0)
    )
    hid[0:5] = dot(weight(0, 0, 5 * hidden), zero_in, 0, 0).reshape(5, hidden, edges)

    for w in (3, 4):
        land(steps - 1, w, True)

    for h in range(heads):
        part = slice(h * width, (h + 1) * width)
        value = scores[part, :]
        centre = value - jnp.mean(value, axis=0, keepdims=True)
        scale = lax.rsqrt(jnp.mean(centre * centre, axis=0, keepdims=True) + 1e-05)
        normed = centre * scale
        scores[part, :] = normed
        gate = 0.2 + 0.8 * jax.nn.sigmoid(normed)
        small[0, h:h + 1, :] = jnp.sum(
            normed * gate * alphas[:, h:h + 1], axis=0, keepdims=True
        )
        small[1, h:h + 1, :] = scale

    raised = jnp.exp(small[0])
    totals = dot(dot(raised, member, 1, 1, EXACT), member, 1, 0, EXACT)
    weights = raised / totals
    spreads[0] = jnp.broadcast_to(
        weights[:, None, :], (heads, hidden // heads, edges)
    ).reshape(hidden, edges)

    settle(1)
    settle(2)
    hid[5:9] = (dot(weight(1), one_pos, 0, 0) - dot(weight(2), one_neg, 0, 0)).reshape(
        4, hidden, edges)
    hid[9:13] = (dot(weight(1), one_neg, 0, 0) + dot(weight(2), one_pos, 0, 0)).reshape(
        4, hidden, edges)
    settle(3)
    settle(4)
    hid[13:16] = (dot(weight(3), two_pos, 0, 0) - dot(weight(4), two_neg, 0, 0)).reshape(
        3, hidden, edges)
    hid[16:19] = (dot(weight(3), two_neg, 0, 0) + dot(weight(4), two_pos, 0, 0)).reshape(
        3, hidden, edges)

    def mix(i, carry):
        part = pl.ds(pl.multiple_of(i * BLOCK_H, BLOCK_H), BLOCK_H)
        spread = spreads[0, part, :]
        scalar = hid[0, part, :]
        gating = jax.nn.sigmoid(scalar)
        silu = scalar * gating
        both = gating * spread
        msg[0, part, :] = (silu * spread).astype(BF16)
        d_first = dmsg[0, part, :]
        inner = jnp.zeros_like(scalar)
        for degree in DEGREES:
            size = 2 * degree + 1
            sums = [None] * size
            for azimuth in orders(degree):
                raw = hid[slot(degree, azimuth), part, :]
                value = raw * both
                back_sum = None
                for m in range(size):
                    k = rot_row(degree, azimuth, m)
                    line = rotf[k:k + 1, :]
                    term = line * value
                    sums[m] = term if sums[m] is None else sums[m] + term
                    other = line * dmsg[degree * degree + m, part, :]
                    back_sum = other if back_sum is None else back_sum + other
                inner = inner + back_sum * raw
                dhid[slot(degree, azimuth), part, :] = (back_sum * both).astype(BF16)
            for m in range(size):
                msg[degree * degree + m, part, :] = sums[m].astype(BF16)
        spreads[1, part, :] = inner * gating + d_first * silu
        d_scalar = d_first * spread * gating * (1.0 + scalar * (1.0 - gating)) + (
            inner * spread * gating * (1.0 - gating)
        )
        dhid[0, part, :] = d_scalar.astype(BF16)
        return carry

    lax.fori_loop(0, hidden // BLOCK_H, mix, 0)

    def put(i, value, begin=0):
        block = sizes["terms"][i][0]
        wide = value.shape[1]
        if block % 16:
            for u in range(half):
                for c in range(2):
                    at = (2 * u + c) * block
                    terms[i][u, c, :, begin:begin + wide] = value[at:at + block, :].astype(BF16)
        else:
            terms[i][:, :, :, begin:begin + wide] = value.astype(BF16).reshape(
                half, 2, block, wide)

    flights = {}

    def launch(key, src, dst, send, recv, target):
        copy = remote(src, dst, send, recv, target)
        flights[key] = copy
        started.append(copy)

    def to_sibling(i):
        launch(("core", i), terms[i].at[:, 1 - parity], landed[i], sib_send.at[i], sib_recv.at[i],
               (row, sibling))

    def chip_sum(i, step, chosen):
        unit = flips(chip, powers, chosen)
        total = terms[i][unit, parity].astype(F32) + landed[i][unit].astype(F32)
        for s in range(step):
            total = total + in_xy[i][plan.spot(s, chosen)].astype(F32)
        return total

    def to_chip(i, step):
        if step == 0:
            flights["core", i].wait_recv()
        else:
            flights["xy", step - 1, i].wait_recv()
        begin, end = plan.base[step], plan.base[step + 1]
        for t, rest in enumerate(plan.rest[step]):
            out_xy[i][begin + t] = chip_sum(i, step, (step,) + rest).astype(BF16)
        target = (row, 2 * flip(chip, powers[step]) + parity)
        launch(("xy", step, i), out_xy[i].at[begin:end], in_xy[i].at[begin:end],
               xy_send.at[step, i], xy_recv.at[step, i], target)

    def inward_copy(i):
        return pltpu.make_async_remote_copy(
            src_ref=out_z[i], dst_ref=in_z[i].at[at_middle],
            send_sem=z_send.at[0, i], recv_sem=z_recv.at[at_middle, i],
            device_id=(inward, me), device_id_type=MESH)

    def arrival(i, spot):
        return pltpu.make_async_remote_copy(
            src_ref=out_z[i], dst_ref=in_z[i].at[spot],
            send_sem=z_send.at[0, i], recv_sem=z_recv.at[spot, i],
            device_id=(inward, me), device_id_type=MESH)

    def outward_copy(i):
        return pltpu.make_async_remote_copy(
            src_ref=final[i], dst_ref=final[i],
            send_sem=z_send.at[1, i], recv_sem=z_recv.at[2, i],
            device_id=(outward, me), device_id_type=MESH)

    def on_line(i, stage):
        if stage == 0:
            flights["xy", steps - 1, i].wait_recv()
            total = chip_sum(i, steps, ())
            layers[i][...] = total
            out_z[i][...] = total.astype(BF16)

            @pl.when(is_end)
            def _():
                inward_copy(i).start()
        elif stage == 1:
            @pl.when(jnp.logical_not(is_end))
            def _():
                arrival(i, 0).wait_recv()
                out_z[i][...] = (layers[i][...] + in_z[i][0].astype(F32)).astype(BF16)
                inward_copy(i).start()
        elif stage == 2:
            @pl.when(is_middle)
            def _():
                arrival(i, 1).wait_recv()
                final[i][...] = (out_z[i][...].astype(F32) + in_z[i][1].astype(F32)).astype(BF16)
                if depth > 2:
                    outward_copy(i).start()
        else:
            @pl.when(jnp.logical_not(is_middle))
            def _():
                outward_copy(i).wait_recv()
                if depth > 4:
                    @pl.when(jnp.logical_not(is_end))
                    def _():
                        outward_copy(i).start()

    def advance(i, stage):
        if stage == 0:
            to_sibling(i)
        elif stage <= steps:
            to_chip(i, stage - 1)
        else:
            on_line(i, stage - 1 - steps)

    def bands(first, number):
        middle = first + number
        last = middle + number
        return (dhid[first:middle].reshape(number * hidden, edges),
                dhid[middle:last].reshape(number * hidden, edges))

    def one_re():
        up, down = bands(5, 4)
        put(0, dot(one_pos, up, 1, 1) + dot(one_neg, down, 1, 1))

    def one_im():
        up, down = bands(5, 4)
        put(1, dot(one_pos, down, 1, 1) - dot(one_neg, up, 1, 1))

    def two():
        up, down = bands(13, 3)
        put(2, dot(two_pos, up, 1, 1) + dot(two_neg, down, 1, 1))
        put(2, dot(two_pos, down, 1, 1) - dot(two_neg, up, 1, 1), 3 * hidden)

    def values():
        d_values = dhid[0:5].reshape(5 * hidden, edges)
        dmixed[:5 * hidden, :] = d_values
        put(3, dot(zero_in, d_values, 1, 1))

    def score_grads(which):
        if which == 0:
            d_weights = jnp.sum(
                spreads[1].reshape(heads, hidden // heads, edges), axis=1
            )
            product = weights * d_weights
            small[0] = product - weights * dot(
                dot(product, member, 1, 1, EXACT), member, 1, 0, EXACT
            )
        group = heads // 2
        for h in range(which * group, (which + 1) * group):
            part = slice(h * width, (h + 1) * width)
            normed = scores[part, :]
            sig = jax.nn.sigmoid(normed)
            gate = 0.2 + 0.8 * sig
            d_logit = small[0, h:h + 1, :]
            d_alphas[:, h:h + 1] = jnp.sum(normed * gate * d_logit, axis=1, keepdims=True)
            d_norm = d_logit * alphas[:, h:h + 1] * (gate + 0.8 * normed * sig * (1.0 - sig))
            first = jnp.mean(d_norm, axis=0, keepdims=True)
            second = jnp.mean(d_norm * normed, axis=0, keepdims=True)
            d_score = small[1, h:h + 1, :] * (d_norm - first - normed * second)
            dmixed[5 * hidden + h * width:5 * hidden + (h + 1) * width, :] = d_score.astype(BF16)
            scores[part, :] = d_score
        begin = 5 * hidden + which * group * width
        put(4 + which, dot(zero_in, dmixed[begin:begin + group * width, :], 1, 1))

    held = {}

    def target_alpha():
        held["atom"] = dot(member, scores[...], 1, 1, EXACT).astype(BF16)
        put(6, dot(ext_ref[:atoms, :channels], held["atom"], 0, 0))
        for u in range(half):
            for c in range(2):
                at = (2 * u + c) * alpha_rows
                terms[7][u, c] = d_alphas[at:at + alpha_rows, :].astype(BF16)

    def turn_zero():
        dturned[0:5] = dot(weight(0), dmixed[...], 1, 0).reshape(5, channels, edges)

    def turn_pair(first, number, re_item, im_item):
        up, down = bands(first, number)
        middle = first + number
        last = middle + number
        dturned[first:middle] = (
            dot(weight(re_item), up, 1, 0) + dot(weight(im_item), down, 1, 0)
        ).reshape(number, channels, edges)
        dturned[middle:last] = (
            dot(weight(re_item), down, 1, 0) - dot(weight(im_item), up, 1, 0)
        ).reshape(number, channels, edges)

    def turn_back(i, carry):
        part = pl.ds(pl.multiple_of(i * BLOCK_C, BLOCK_C), BLOCK_C)
        dxs[0, part, :] = dturned[0, part, :].astype(BF16)
        for degree in DEGREES:
            for m in range(2 * degree + 1):
                total = None
                for azimuth in orders(degree):
                    k = rot_row(degree, azimuth, m)
                    term = rotf[k:k + 1, :] * dturned[slot(degree, azimuth), part, :]
                    total = term if total is None else total + term
                dxs[degree * degree + m, part, :] = total.astype(BF16)
        return carry

    blocks = channels // BLOCK_C

    def source_grads():
        d_target = dot(held["atom"], weight(5), 1, 1)
        ext_grad = dot(src_hot, dxs[...].reshape(25 * channels, edges), 1, 1)
        grad_ref[...] = ext_grad[:atoms]
        grad_ref[:, :channels] = ext_grad[:atoms, :channels] + d_target
        for side in range(2):
            begin = atoms + side * slots
            ghost[side] = ext_grad[begin:begin + slots].astype(BF16)

    returns = []

    def return_ghosts():
        for side, target in ((0, left), (1, right)):
            returns.append(remote(ghost.at[side], back.at[side], side_send.at[2 + side],
                                  side_recv.at[2 + side], (row, target)))

    def attend():
        att_ref[...] = dot(member_b, msg[...].reshape(25 * hidden, edges), 1, 1).astype(BF16)

    work = {
        "g1r": one_re, "g1i": one_im, "g2": two, "gzv": values,
        "ds0": partial(score_grads, 0), "ds1": partial(score_grads, 1), "gwt": target_alpha,
        "dt0": turn_zero, "dt1": partial(turn_pair, 5, 4, 1, 2),
        "dt2": partial(turn_pair, 13, 3, 3, 4),
        "tb0": lambda: lax.fori_loop(0, blocks // 2, turn_back, 0),
        "tb1": lambda: lax.fori_loop(blocks // 2, blocks, turn_back, 0),
        "eg": source_grads, "ghost": return_ghosts, "att": attend,
    }
    for step in ORDER:
        if step in work:
            work[step]()
        else:
            first, last = {
                "s": (0, 1), "x": (1, 2), "y": (2, 1 + steps), "a": (1 + steps, 2 + steps),
                "b": (2 + steps, 3 + steps), "c": (3 + steps, 4 + steps),
                "d": (4 + steps, 5 + steps)}[step[0]]
            for stage in range(first, last):
                for i in step[1:]:
                    advance(int(i), stage)

    for copy in returns:
        copy.wait_recv()
    total = grad_ref[...]
    for side, list_ref in ((0, right_ref), (1, left_ref)):
        ids = lax.broadcasted_iota(jnp.int32, (atoms, slots), 0)
        place = (ids == list_ref[...]).astype(F32).astype(BF16)
        total = total + dot(place, back[side], 1, 0)
    grad_ref[...] = total
    for i in range(items):
        inward_copy(i).wait_send()
        if depth > 2:
            @pl.when(jnp.logical_not(is_end))
            def _():
                outward_copy(i).wait_send()
    for copy in sides + returns + started:
        copy.wait_send()


def slab(n, depth, features, cotangent, rotation, src, tgt, send_left, send_right, weights):
    atoms = features.shape[0]
    edges = src.shape[1]
    slots = send_left.shape[1]
    heads = weights[6].shape[1]
    head_width = n * weights[6].shape[0]
    channels = n * weights[5].shape[0]
    hidden = weights[1].shape[1] // 4
    half = n // 2
    w_shapes = [tuple(w.shape) for w in weights]
    block = w_shapes[0][0]
    logits = (w_shapes[0][1] - 5 * hidden) // 2
    t_shapes = w_shapes[1:3] + [(w_shapes[3][0], 6 * hidden), (block, 5 * hidden)]
    t_shapes += [(block, logits)] * 2 + w_shapes[5:]
    sizes = {"weights": w_shapes, "terms": t_shapes}
    count, items = len(w_shapes), len(t_shapes)

    shape = jax.ShapeDtypeStruct
    vmem = pl.BlockSpec(memory_space=pltpu.VMEM)
    out_shape = [shape((atoms, 25 * hidden), BF16), shape((atoms, 25 * channels), F32)]
    out_shape += [shape(t, BF16) for t in t_shapes]
    rows = atoms + 2 * slots
    mixed = w_shapes[0][1]
    rots = rotation.shape[1]
    dma = pltpu.SemaphoreType.DMA
    scratch = [
        pltpu.VMEM((rows, 25 * channels), BF16),
        pltpu.VMEM((head_width, heads), F32),
        pltpu.VMEM((head_width, heads), F32),
        pltpu.VMEM((rots, edges), F32),
        pltpu.VMEM((25, channels, edges), F32),
        pltpu.VMEM((19, channels, edges), BF16),
        pltpu.VMEM((19, hidden, edges), F32),
        pltpu.VMEM((25, hidden, edges), BF16),
        pltpu.VMEM((25, hidden, edges), F32),
        pltpu.VMEM((head_width * heads, edges), F32),
        pltpu.VMEM((19, hidden, edges), BF16),
        pltpu.VMEM((mixed, edges), BF16),
        pltpu.VMEM((19, channels, edges), F32),
        pltpu.VMEM((25, channels, edges), BF16),
        pltpu.VMEM((2, heads, edges), F32),
        pltpu.VMEM((2, hidden, edges), F32),
    ]
    scratch += [pltpu.VMEM((2, slots, 25 * channels), BF16) for _ in range(4)]
    scratch += [pltpu.VMEM((half, 2, *w), BF16) for w in w_shapes]
    scratch += [pltpu.VMEM((n * w[0], w[1]) if w[0] % 16 else (8, 128), F32) for w in w_shapes]
    scratch += [pltpu.VMEM((half, 2, *t), BF16) for t in t_shapes]
    scratch += [pltpu.VMEM((half, *t), BF16) for t in t_shapes]
    scratch += [pltpu.VMEM((half - 1, *t), BF16) for _ in range(2) for t in t_shapes]
    scratch += [pltpu.VMEM(t, F32) for t in t_shapes]
    scratch += [pltpu.VMEM(t, BF16) for t in t_shapes]
    scratch += [pltpu.VMEM((2, *t), BF16) for t in t_shapes]
    steps = Halving(half).steps
    scratch += [dma((4,)) for _ in range(2)]
    scratch += [dma((half - 1, count)) for _ in range(2)]
    scratch += [dma((half, count)) for _ in range(2)]
    scratch += [dma((items,)) for _ in range(2)]
    scratch += [dma((steps, items)) for _ in range(2)]
    scratch += [dma((2, items)), dma((3, items)), dma((7 + count,))]
    given = (features, cotangent, rotation, src, tgt, send_left, send_right)
    scratch += [pltpu.VMEM(g.shape, g.dtype) for g in given]
    return pl.pallas_call(
        partial(slab_kernel, n, depth, sizes),
        out_shape=tuple(out_shape),
        in_specs=[pl.BlockSpec(memory_space=pl.ANY)] * (7 + count),
        out_specs=[vmem] * (2 + items),
        scratch_shapes=scratch,
        compiler_params=pltpu.CompilerParams(
            collective_id=0, has_side_effects=True, vmem_limit_bytes=60 * 2**20),
        name="slab",
    )(features, cotangent, rotation, src, tgt, send_left, send_right, *weights)


def finish_kernel(items, hidden, *refs):
    att_ref, grad_ref = refs[:2]
    final = refs[2:2 + items]
    out_att, out_grad = refs[2 + items:4 + items]
    gz_ref, g1r_ref, g1i_ref, g2r_ref, g2i_ref, gt_ref, ga_ref = refs[4 + items:]
    out_att[...] = att_ref[...]
    out_grad[...] = grad_ref[...]

    wide = 3 * hidden
    g1r_ref[...] = final[0][...].astype(F32)
    g1i_ref[...] = final[1][...].astype(F32)
    g2r_ref[...] = final[2][:, :wide].astype(F32)
    g2i_ref[...] = final[2][:, wide:].astype(F32)
    begin = 0
    for source in final[3:6]:
        end = begin + source.shape[1]
        gz_ref[:, begin:end] = source[...].astype(F32)
        begin = end
    gt_ref[...] = final[6][...].astype(F32)
    ga_ref[...] = final[7][...].astype(F32)


def finish(attended, grad, final, weights, hidden):
    items = len(final)
    vmem = pl.BlockSpec(memory_space=pltpu.VMEM)
    shapes = [jax.ShapeDtypeStruct(attended.shape, BF16), jax.ShapeDtypeStruct(grad.shape, F32)]
    shapes += [jax.ShapeDtypeStruct(w.shape, F32) for w in weights]
    return pl.pallas_call(
        partial(finish_kernel, items, hidden),
        out_shape=tuple(shapes),
        in_specs=[vmem] * (2 + items),
        out_specs=[vmem] * len(shapes),
        name="finish",
    )(attended, grad, *final)


def body(n, depth, features, cotangent, rotation, send_left, send_right, edge_src, edge_tgt,
         *weights):
    turned_rotation = jnp.swapaxes(rotation[0], 0, 1)
    attended, grad_features, *final = slab(
        n, depth, features[0], cotangent[0], turned_rotation, edge_src, edge_tgt,
        send_left, send_right, weights)
    attended, grad_features, *grads = finish(
        attended, grad_features, final, weights, weights[1].shape[1] // 4)
    return (attended[None], grad_features[None], *grads)


def solution(mesh):
    cell = P("dp", "graph", None)
    lists = P("dp", "graph")
    shard = P("graph", None)
    in_specs = (cell, cell, P("dp", None, "graph")) + (lists,) * 4 + (shard,) * 7
    out_specs = (cell, cell) + (shard,) * 7
    return jax.shard_map(
        partial(body, mesh.shape["graph"], mesh.shape["dp"]), mesh=mesh,
        in_specs=in_specs, out_specs=out_specs, check_vma=False)
```

```python
from functools import partial

import jax
import jax.numpy as jnp
from jax import lax
from jax.experimental import pallas as pl
from jax.experimental.pallas import tpu as pltpu
from jax.sharding import PartitionSpec as P

F32 = jnp.float32
BF16 = jnp.bfloat16
OFFSETS = {1: 0, 2: 9, 3: 34, 4: 69}
DEGREES = (1, 2, 3, 4)
BLOCK_C = 32
BLOCK_H = 16
MESH = pl.DeviceIdType.MESH
EXACT = lax.Precision.HIGHEST
ORDER = (
    "g1r", "s0", "g1i", "s1", "gzv", "s3", "ds0", "s4", "x0", "ds1", "s5", "x1", "g2", "s2",
    "x3", "gwt", "s6", "s7", "dt0", "dt1", "dt2", "x4", "tb0", "y0", "y1", "tb1", "tb2", "tb3", "eg0", "eg1", "eg2", "eg3", "eg4", "y3",
    "x5", "y4", "a0", "x2", "a1", "x6", "a3", "x7", "y5", "b0", "a4", "b1", "y2", "y6", "y7",
    "ghost", "att", "a5", "b3", "c0", "b4", "a2", "c1", "a6", "a7", "b5", "d0", "c3", "b2",
    "d1", "b6", "c4", "b7", "c5", "c2", "d3", "c6", "c7", "d4", "d5", "d2", "d6", "d7",
)
TURN = (0, 1, 0, 0, 1, 1, 1, 1)


def slot(degree, azimuth):
    return {0: degree, 1: 4 + degree, -1: 8 + degree, 2: 11 + degree, -2: 14 + degree}[azimuth]


def orders(degree):
    kept = min(degree, 2)
    return range(-kept, kept + 1)


def rot_row(degree, azimuth, column):
    return OFFSETS[degree] + (azimuth + min(degree, 2)) * (2 * degree + 1) + column


def dot(a, b, ca, cb, precision=None):
    return lax.dot_general(
        a, b, (((ca,), (cb,)), ((), ())), preferred_element_type=F32, precision=precision
    )


def flip(index, power):
    bit = lax.rem(lax.div(index, power), 2)
    return index + (1 - 2 * bit) * power


def flips(index, powers, chosen):
    for j in chosen:
        index = flip(index, powers[j])
    return index


def subsets(steps):
    found = [()]
    for j in steps:
        found = found + [s + (j,) for s in found]
    return found


class Halving:
    def __init__(self, count):
        self.steps = count.bit_length() - 1
        self.rest = [subsets(range(j + 1, self.steps)) for j in range(self.steps)]
        self.base = [0]
        for found in self.rest:
            self.base.append(self.base[-1] + len(found))

    def spot(self, step, chosen):
        return self.base[step] + self.rest[step].index(chosen)


def slab_kernel(n, depth, sizes, *refs):
    take = iter(refs)
    placed = [next(take) for _ in range(7)]
    count = len(sizes["weights"])
    items = len(sizes["terms"])
    shards = [next(take) for _ in range(count)]
    att_ref, grad_ref = next(take), next(take)
    final = [next(take) for _ in range(items)]
    (ext_ref, alphas, d_alphas, rotf, xs, turned, hid, msg, dmsg, scores, dhid, dmixed, dturned,
     dxs, small, spreads) = [next(take) for _ in range(16)]
    outgoing, near, ghost, back = [next(take) for _ in range(4)]
    full = [next(take) for _ in range(count)]
    mats = [next(take) for _ in range(count)]
    terms = [next(take) for _ in range(items)]
    landed = [next(take) for _ in range(items)]
    out_xy = [next(take) for _ in range(items)]
    in_xy = [next(take) for _ in range(items)]
    layers = [next(take) for _ in range(items)]
    out_z = [next(take) for _ in range(items)]
    in_z = [next(take) for _ in range(items)]
    whole = [next(take) for _ in range(items)]
    (side_send, side_recv, hop_send, hop_recv, core_send, core_recv, sib_send, sib_recv,
     xy_send, xy_recv, z_send, z_recv, end_send, end_recv, in_sem) = [next(take) for _ in range(15)]
    local = list(take)
    feat_ref, cot_ref, rot_ref, src_ref, tgt_ref, left_ref, right_ref = local

    edges = src_ref.shape[1]
    rows = ext_ref.shape[0]
    atoms = att_ref.shape[0]
    channels = n * sizes["weights"][5][0]
    hidden = sizes["weights"][1][1] // 4
    heads = small.shape[1]
    width = alphas.shape[0]
    slots = left_ref.shape[1]

    me = lax.axis_index("graph")
    row = lax.axis_index("dp")
    half = n // 2
    chip = lax.div(me, 2)
    parity = lax.rem(me, 2)
    sibling = me + 1 - 2 * parity
    right, left = lax.rem(me + 1, n), lax.rem(me + n - 1, n)
    plan = Halving(half)
    steps = plan.steps
    powers = [2 ** j + parity * (2 ** ((j + 1) % steps) - 2 ** j) for j in range(steps)]

    upper = lax.div(row, depth // 2)
    inward = row + 1 - 2 * upper
    outward = row - 1 + 2 * upper
    from_end = row + upper * (depth - 1 - 2 * row)
    at_middle = lax.div(from_end + 1, depth // 2)
    is_end = from_end == 0
    is_middle = at_middle == 1
    odd = parity == 1
    even = parity == 0

    barrier = pltpu.get_barrier_semaphore()
    partners = [(row, sibling), (row, right), (row, left)]
    partners += [(row, 2 * flip(chip, p) + parity) for p in powers]
    for partner in partners:
        pl.semaphore_signal(barrier, inc=1, device_id=partner, device_id_type=MESH)
    for z in (-1, 1):
        other = row + z

        @pl.when(odd & (other >= 0) & (other < depth))
        def _():
            pl.semaphore_signal(barrier, inc=1, device_id=(other, me), device_id_type=MESH)

    def remote(src, dst, send, recv, target):
        copy = pltpu.make_async_remote_copy(
            src_ref=src, dst_ref=dst, send_sem=send, recv_sem=recv,
            device_id=target, device_id_type=MESH)
        copy.start()
        return copy

    started = []

    loads = {}

    def load(key, src, dst, spot):
        copy = pltpu.make_async_copy(src, dst, in_sem.at[spot])
        copy.start()
        loads[key] = copy

    for k in (0, 5, 6):
        load(k, placed[k], local[k], k)
    for w in range(count):
        load(("w", w), shards[w], full[w].at[chip, parity], 7 + w)
    for k in (3, 4, 2, 1):
        load(k, placed[k], local[k], k)
    for k in (0, 5, 6):
        loads[k].wait()
    own = feat_ref[...].astype(BF16)
    ext_ref[:atoms, :] = own
    for side, list_ref in ((0, left_ref), (1, right_ref)):
        ids = lax.broadcasted_iota(jnp.int32, (atoms, slots), 0)
        pick = (ids == list_ref[...]).astype(F32).astype(BF16)
        outgoing[side] = dot(pick, own, 0, 0).astype(BF16)
    for w in range(count):
        loads["w", w].wait()

    pl.semaphore_wait(
        barrier, len(partners) + parity * (1 + lax.div(from_end + depth - 1, depth)))

    sides = []
    for side, target in ((1, left), (0, right)):
        sides.append(remote(outgoing.at[1 - side], near.at[side], side_send.at[side],
                            side_recv.at[side], (row, target)))
    arrivals = {}

    def hop(j, w, part):
        target = (row, 2 * flip(chip, powers[j]) + parity)
        for t, chosen in enumerate(subsets(range(j))):
            if (t > 0) != part:
                continue
            unit = flips(chip, powers, chosen)
            copy = remote(full[w].at[unit, parity], full[w].at[unit, parity],
                          hop_send.at[2 ** j + t - 1, w], hop_recv.at[2 ** j + t - 1, w], target)
            arrivals[j, t, w] = copy
            started.append(copy)

    crossing = {}

    def cross(spot, unit, w):
        copy = remote(full[w].at[unit, parity], full[w].at[unit, parity],
                      core_send.at[spot, w], core_recv.at[spot, w], (row, sibling))
        crossing[spot, w] = copy
        started.append(copy)

    def land(j, w, part):
        partner = flip(chip, powers[j])
        for t, chosen in enumerate(subsets(range(j))):
            if (t > 0) == part:
                arrivals[j, t, w].wait_recv()
                cross(2 ** j + t, flips(partner, powers, chosen), w)

    weight_order = (0, 5, 6, 1, 2, 3, 4)
    for j in range(steps):
        for w in weight_order:
            hop(j, w, False)
    for w in weight_order:
        cross(0, chip, w)

    for k in (3, 4, 2, 1):
        loads[k].wait()
    src_hot = (
        lax.broadcasted_iota(jnp.int32, (rows, edges), 0) == src_ref[...]
    ).astype(F32).astype(BF16)
    member = (lax.broadcasted_iota(jnp.int32, (atoms, edges), 0) == tgt_ref[...]).astype(F32)
    member_b = member.astype(BF16)

    edge_eye = (
        lax.broadcasted_iota(jnp.int32, (rot_ref.shape[1], rot_ref.shape[1]), 0)
        == lax.broadcasted_iota(jnp.int32, (rot_ref.shape[1], rot_ref.shape[1]), 1)
    ).astype(F32).astype(BF16)
    rotf[...] = dot(edge_eye, rot_ref[...], 1, 1)
    for k in range(25):
        dmsg[k] = dot(
            cot_ref[:, k * hidden:(k + 1) * hidden].astype(BF16), member_b, 0, 0
        )
    for copy in sides:
        copy.wait_recv()
    ext_ref[atoms:, :] = near[...].astype(F32).reshape(rows - atoms, -1).astype(BF16)
    for k in range(25):
        xs[k] = dot(ext_ref[:, k * channels:(k + 1) * channels], src_hot, 0, 0)

    for j in range(1, steps):
        for w in weight_order:
            land(j - 1, w, False)
            land(j - 1, w, True)
            hop(j, w, True)

    def turn(i, carry):
        part = pl.ds(pl.multiple_of(i * BLOCK_C, BLOCK_C), BLOCK_C)
        turned[0, part, :] = xs[0, part, :].astype(BF16)
        for degree in DEGREES:
            for azimuth in orders(degree):
                total = None
                for m in range(2 * degree + 1):
                    k = rot_row(degree, azimuth, m)
                    term = rotf[k:k + 1, :] * xs[degree * degree + m, part, :]
                    total = term if total is None else total + term
                turned[slot(degree, azimuth), part, :] = total.astype(BF16)
        return carry

    lax.fori_loop(0, channels // BLOCK_C, turn, 0)

    zero_in = turned[0:5].reshape(5 * channels, edges)
    one_pos = turned[5:9].reshape(4 * channels, edges)
    one_neg = turned[9:13].reshape(4 * channels, edges)
    two_pos = turned[13:16].reshape(3 * channels, edges)
    two_neg = turned[16:19].reshape(3 * channels, edges)

    def settle(w):
        for spot in range(half):
            crossing[spot, w].wait_recv()
        block = sizes["weights"][w][0]
        if block % 16:
            for u in range(half):
                for c in range(2):
                    at = (2 * u + c) * block
                    mats[w][at:at + block, :] = full[w][u, c].astype(mats[w].dtype)

    def weight(w, begin=0, end=None):
        block, wide = sizes["weights"][w]
        end = wide if end is None else end
        if block % 16:
            return mats[w][:, begin:end].astype(BF16)
        return full[w][:, :, :, begin:end].reshape(n * block, end - begin)

    for w in weight_order:
        land(steps - 1, w, False)
    for w in (0, 5, 6, 1, 2):
        land(steps - 1, w, True)
    for w in (0, 5, 6):
        settle(w)
    alpha_rows = sizes["weights"][6][0]
    for u in range(half):
        for c in range(2):
            at = (2 * u + c) * alpha_rows
            alphas[at:at + alpha_rows, :] = full[6][u, c].astype(F32)

    per_atom = dot(ext_ref[:atoms, :channels], weight(5), 1, 0)
    high = per_atom.astype(BF16)
    low = (per_atom - high.astype(F32)).astype(BF16)
    scores[...] = (
        dot(weight(0, 5 * hidden), zero_in, 0, 0)
        + dot(high, member_b, 0, 0)
        + dot(low, member_b, 0, 0)
    )
    hid[0:5] = dot(weight(0, 0, 5 * hidden), zero_in, 0, 0).reshape(5, hidden, edges)

    for w in (3, 4):
        land(steps - 1, w, True)

    for h in range(heads):
        part = slice(h * width, (h + 1) * width)
        value = scores[part, :]
        centre = value - jnp.mean(value, axis=0, keepdims=True)
        scale = lax.rsqrt(jnp.mean(centre * centre, axis=0, keepdims=True) + 1e-05)
        normed = centre * scale
        scores[part, :] = normed
        gate = 0.2 + 0.8 * jax.nn.sigmoid(normed)
        small[0, h:h + 1, :] = jnp.sum(
            normed * gate * alphas[:, h:h + 1], axis=0, keepdims=True
        )
        small[1, h:h + 1, :] = scale

    raised = jnp.exp(small[0])
    totals = dot(dot(raised, member, 1, 1, EXACT), member, 1, 0, EXACT)
    weights = raised / totals
    spreads[0] = jnp.broadcast_to(
        weights[:, None, :], (heads, hidden // heads, edges)
    ).reshape(hidden, edges)

    settle(1)
    settle(2)
    hid[5:9] = (dot(weight(1), one_pos, 0, 0) - dot(weight(2), one_neg, 0, 0)).reshape(
        4, hidden, edges)
    hid[9:13] = (dot(weight(1), one_neg, 0, 0) + dot(weight(2), one_pos, 0, 0)).reshape(
        4, hidden, edges)
    settle(3)
    settle(4)
    hid[13:16] = (dot(weight(3), two_pos, 0, 0) - dot(weight(4), two_neg, 0, 0)).reshape(
        3, hidden, edges)
    hid[16:19] = (dot(weight(3), two_neg, 0, 0) + dot(weight(4), two_pos, 0, 0)).reshape(
        3, hidden, edges)

    def mix(i, carry):
        part = pl.ds(pl.multiple_of(i * BLOCK_H, BLOCK_H), BLOCK_H)
        spread = spreads[0, part, :]
        scalar = hid[0, part, :]
        gating = jax.nn.sigmoid(scalar)
        silu = scalar * gating
        both = gating * spread
        msg[0, part, :] = (silu * spread).astype(BF16)
        d_first = dmsg[0, part, :]
        inner = jnp.zeros_like(scalar)
        for degree in DEGREES:
            size = 2 * degree + 1
            sums = [None] * size
            for azimuth in orders(degree):
                raw = hid[slot(degree, azimuth), part, :]
                value = raw * both
                back_sum = None
                for m in range(size):
                    k = rot_row(degree, azimuth, m)
                    line = rotf[k:k + 1, :]
                    term = line * value
                    sums[m] = term if sums[m] is None else sums[m] + term
                    other = line * dmsg[degree * degree + m, part, :]
                    back_sum = other if back_sum is None else back_sum + other
                inner = inner + back_sum * raw
                dhid[slot(degree, azimuth), part, :] = (back_sum * both).astype(BF16)
            for m in range(size):
                msg[degree * degree + m, part, :] = sums[m].astype(BF16)
        spreads[1, part, :] = inner * gating + d_first * silu
        d_scalar = d_first * spread * gating * (1.0 + scalar * (1.0 - gating)) + (
            inner * spread * gating * (1.0 - gating)
        )
        dhid[0, part, :] = d_scalar.astype(BF16)
        return carry

    lax.fori_loop(0, hidden // BLOCK_H, mix, 0)

    def put(i, value, begin=0):
        block = sizes["terms"][i][0]
        wide = value.shape[1]
        if block % 16:
            for u in range(half):
                for c in range(2):
                    at = (2 * u + c) * block
                    terms[i][u, c, :, begin:begin + wide] = value[at:at + block, :].astype(BF16)
        else:
            terms[i][:, :, :, begin:begin + wide] = value.astype(BF16).reshape(
                half, 2, block, wide)

    def copy_to(src, dst, send, recv, target):
        return pltpu.make_async_remote_copy(
            src_ref=src, dst_ref=dst, send_sem=send, recv_sem=recv,
            device_id=target, device_id_type=MESH)

    def handed(i):
        return copy_to(terms[i], landed[i], sib_send.at[i], sib_recv.at[i], (row, sibling))

    def crossed(i, step):
        begin, end = plan.base[step], plan.base[step + 1]
        target = (row, 2 * flip(chip, order_of(i)[step]) + parity)
        return copy_to(out_xy[i].at[begin:end], in_xy[i].at[begin:end],
                       xy_send.at[step, i], xy_recv.at[step, i], target)

    def inward_copy(i, spot):
        return copy_to(out_z[i], in_z[i].at[spot], z_send.at[0, i], z_recv.at[spot, i],
                       (inward, me))

    def outward_copy(i):
        return copy_to(whole[i], whole[i], z_send.at[1, i], z_recv.at[2, i], (outward, me))

    def returned(i):
        return copy_to(whole[i].at[0], final[i], end_send.at[i], end_recv.at[i], (row, sibling))

    def order_of(i):
        return [2 ** ((j + TURN[i]) % steps) for j in range(steps)]

    def chip_sum(i, step, chosen):
        unit = flips(chip, order_of(i), chosen)
        total = terms[i][unit].astype(F32) + landed[i][unit].astype(F32)
        for s in range(step):
            total = total + in_xy[i][plan.spot(s, chosen)].astype(F32)
        return total

    def to_chip(i, step):
        @pl.when(odd)
        def _():
            if step == 0:
                handed(i).wait_recv()
            else:
                crossed(i, step - 1).wait_recv()
            for t, rest in enumerate(plan.rest[step]):
                out_xy[i][plan.base[step] + t] = chip_sum(i, step, (step,) + rest).astype(BF16)
            crossed(i, step).start()

    def finished(i):
        returned(i).start()
        final[i][...] = whole[i][1]

    def on_line(i, stage):
        if stage == 0:
            @pl.when(odd)
            def _():
                crossed(i, steps - 1).wait_recv()
                total = chip_sum(i, steps, ())
                layers[i][...] = total
                out_z[i][...] = total.astype(BF16)

                @pl.when(is_end)
                def _():
                    inward_copy(i, at_middle).start()
        elif stage == 1:
            @pl.when(odd & jnp.logical_not(is_end))
            def _():
                inward_copy(i, 0).wait_recv()
                out_z[i][...] = (layers[i][...] + in_z[i][0].astype(F32)).astype(BF16)
                inward_copy(i, at_middle).start()
        elif stage == 2:
            @pl.when(odd & is_middle)
            def _():
                inward_copy(i, 1).wait_recv()
                whole[i][...] = (out_z[i][...].astype(F32) + in_z[i][1].astype(F32)).astype(BF16)
                if depth > 2:
                    outward_copy(i).start()
                finished(i)
        else:
            @pl.when(odd & jnp.logical_not(is_middle))
            def _():
                outward_copy(i).wait_recv()
                if depth > 4:
                    @pl.when(jnp.logical_not(is_end))
                    def _():
                        outward_copy(i).start()
                finished(i)

    def advance(i, stage):
        if stage == 0:
            @pl.when(even)
            def _():
                handed(i).start()
        elif stage <= steps:
            to_chip(i, stage - 1)
        else:
            on_line(i, stage - 1 - steps)

    def bands(first, number):
        middle = first + number
        last = middle + number
        return (dhid[first:middle].reshape(number * hidden, edges),
                dhid[middle:last].reshape(number * hidden, edges))

    def one_re():
        up, down = bands(5, 4)
        put(0, dot(one_pos, up, 1, 1) + dot(one_neg, down, 1, 1))

    def one_im():
        up, down = bands(5, 4)
        put(1, dot(one_pos, down, 1, 1) - dot(one_neg, up, 1, 1))

    def two():
        up, down = bands(13, 3)
        put(2, dot(two_pos, up, 1, 1) + dot(two_neg, down, 1, 1))
        put(2, dot(two_pos, down, 1, 1) - dot(two_neg, up, 1, 1), 3 * hidden)

    def values():
        d_values = dhid[0:5].reshape(5 * hidden, edges)
        dmixed[:5 * hidden, :] = d_values
        put(3, dot(zero_in, d_values, 1, 1))

    def score_grads(which):
        if which == 0:
            d_weights = jnp.sum(
                spreads[1].reshape(heads, hidden // heads, edges), axis=1
            )
            product = weights * d_weights
            small[0] = product - weights * dot(
                dot(product, member, 1, 1, EXACT), member, 1, 0, EXACT
            )
        group = heads // 2
        for h in range(which * group, (which + 1) * group):
            part = slice(h * width, (h + 1) * width)
            normed = scores[part, :]
            sig = jax.nn.sigmoid(normed)
            gate = 0.2 + 0.8 * sig
            d_logit = small[0, h:h + 1, :]
            d_alphas[:, h:h + 1] = jnp.sum(normed * gate * d_logit, axis=1, keepdims=True)
            d_norm = d_logit * alphas[:, h:h + 1] * (gate + 0.8 * normed * sig * (1.0 - sig))
            first = jnp.mean(d_norm, axis=0, keepdims=True)
            second = jnp.mean(d_norm * normed, axis=0, keepdims=True)
            d_score = small[1, h:h + 1, :] * (d_norm - first - normed * second)
            dmixed[5 * hidden + h * width:5 * hidden + (h + 1) * width, :] = d_score.astype(BF16)
            scores[part, :] = d_score
        begin = 5 * hidden + which * group * width
        put(4 + which, dot(zero_in, dmixed[begin:begin + group * width, :], 1, 1))

    held = {}

    def target_alpha():
        held["atom"] = dot(member, scores[...], 1, 1, EXACT).astype(BF16)
        put(6, dot(ext_ref[:atoms, :channels], held["atom"], 0, 0))
        for u in range(half):
            for c in range(2):
                at = (2 * u + c) * alpha_rows
                terms[7][u, c] = d_alphas[at:at + alpha_rows, :].astype(BF16)

    def turn_zero():
        dturned[0:5] = dot(weight(0), dmixed[...], 1, 0).reshape(5, channels, edges)

    def turn_pair(first, number, re_item, im_item):
        up, down = bands(first, number)
        middle = first + number
        last = middle + number
        dturned[first:middle] = (
            dot(weight(re_item), up, 1, 0) + dot(weight(im_item), down, 1, 0)
        ).reshape(number, channels, edges)
        dturned[middle:last] = (
            dot(weight(re_item), down, 1, 0) - dot(weight(im_item), up, 1, 0)
        ).reshape(number, channels, edges)

    def turn_back(i, carry):
        part = pl.ds(pl.multiple_of(i * BLOCK_C, BLOCK_C), BLOCK_C)
        dxs[0, part, :] = dturned[0, part, :].astype(BF16)
        for degree in DEGREES:
            for m in range(2 * degree + 1):
                total = None
                for azimuth in orders(degree):
                    k = rot_row(degree, azimuth, m)
                    term = rotf[k:k + 1, :] * dturned[slot(degree, azimuth), part, :]
                    total = term if total is None else total + term
                dxs[degree * degree + m, part, :] = total.astype(BF16)
        return carry

    blocks = channels // BLOCK_C

    def source_grads(k):
        part = slice(5 * k * channels, 5 * (k + 1) * channels)
        ext_grad = dot(src_hot, dxs[5 * k:5 * k + 5].reshape(5 * channels, edges), 1, 1)
        grad_ref[:, part] = ext_grad[:atoms]
        if k == 0:
            grad_ref[:, :channels] = ext_grad[:atoms, :channels] + dot(
                held["atom"], weight(5), 1, 1)
        for side in range(2):
            begin = atoms + side * slots
            ghost[side, :, part] = ext_grad[begin:begin + slots].astype(BF16)

    returns = []

    def return_ghosts():
        for side, target in ((0, left), (1, right)):
            returns.append(remote(ghost.at[side], back.at[side], side_send.at[2 + side],
                                  side_recv.at[2 + side], (row, target)))

    def attend():
        att_ref[...] = dot(member_b, msg[...].reshape(25 * hidden, edges), 1, 1).astype(BF16)

    work = {
        "g1r": one_re, "g1i": one_im, "g2": two, "gzv": values,
        "ds0": partial(score_grads, 0), "ds1": partial(score_grads, 1), "gwt": target_alpha,
        "dt0": turn_zero, "dt1": partial(turn_pair, 5, 4, 1, 2),
        "dt2": partial(turn_pair, 13, 3, 3, 4),
        "ghost": return_ghosts, "att": attend,
    }
    for k in range(4):
        work["tb%d" % k] = partial(
            lax.fori_loop, k * blocks // 4, (k + 1) * blocks // 4, turn_back, 0)
    for k in range(5):
        work["eg%d" % k] = partial(source_grads, k)
    for step in ORDER:
        if step in work:
            work[step]()
        else:
            first, last = {
                "s": (0, 1), "x": (1, 2), "y": (2, 1 + steps), "a": (1 + steps, 2 + steps),
                "b": (2 + steps, 3 + steps), "c": (3 + steps, 4 + steps),
                "d": (4 + steps, 5 + steps)}[step[0]]
            for stage in range(first, last):
                for i in step[1:]:
                    advance(int(i), stage)

    for copy in returns:
        copy.wait_recv()
    total = grad_ref[...]
    for side, list_ref in ((0, right_ref), (1, left_ref)):
        ids = lax.broadcasted_iota(jnp.int32, (atoms, slots), 0)
        place = (ids == list_ref[...]).astype(F32).astype(BF16)
        total = total + dot(place, back[side], 1, 0)
    grad_ref[...] = total
    @pl.when(even)
    def _():
        for i in range(items):
            handed(i).wait_send()
            returned(i).wait_recv()

    @pl.when(odd)
    def _():
        for i in range(items):
            for step in range(steps):
                crossed(i, step).wait_send()
            inward_copy(i, at_middle).wait_send()
            if depth > 2:
                @pl.when(jnp.logical_not(is_end))
                def _():
                    outward_copy(i).wait_send()
            returned(i).wait_send()

    for copy in sides + returns + started:
        copy.wait_send()


def slab(n, depth, features, cotangent, rotation, src, tgt, send_left, send_right, weights):
    atoms = features.shape[0]
    edges = src.shape[1]
    slots = send_left.shape[1]
    heads = weights[6].shape[1]
    head_width = n * weights[6].shape[0]
    channels = n * weights[5].shape[0]
    hidden = weights[1].shape[1] // 4
    half = n // 2
    w_shapes = [tuple(w.shape) for w in weights]
    block = w_shapes[0][0]
    logits = (w_shapes[0][1] - 5 * hidden) // 2
    t_shapes = w_shapes[1:3] + [(w_shapes[3][0], 6 * hidden), (block, 5 * hidden)]
    t_shapes += [(block, logits)] * 2 + w_shapes[5:]
    sizes = {"weights": w_shapes, "terms": t_shapes}
    count, items = len(w_shapes), len(t_shapes)

    shape = jax.ShapeDtypeStruct
    vmem = pl.BlockSpec(memory_space=pltpu.VMEM)
    out_shape = [shape((atoms, 25 * hidden), BF16), shape((atoms, 25 * channels), F32)]
    out_shape += [shape(t, BF16) for t in t_shapes]
    rows = atoms + 2 * slots
    mixed = w_shapes[0][1]
    rots = rotation.shape[1]
    dma = pltpu.SemaphoreType.DMA
    scratch = [
        pltpu.VMEM((rows, 25 * channels), BF16),
        pltpu.VMEM((head_width, heads), F32),
        pltpu.VMEM((head_width, heads), F32),
        pltpu.VMEM((rots, edges), F32),
        pltpu.VMEM((25, channels, edges), F32),
        pltpu.VMEM((19, channels, edges), BF16),
        pltpu.VMEM((19, hidden, edges), F32),
        pltpu.VMEM((25, hidden, edges), BF16),
        pltpu.VMEM((25, hidden, edges), F32),
        pltpu.VMEM((head_width * heads, edges), F32),
        pltpu.VMEM((19, hidden, edges), BF16),
        pltpu.VMEM((mixed, edges), BF16),
        pltpu.VMEM((19, channels, edges), F32),
        pltpu.VMEM((25, channels, edges), BF16),
        pltpu.VMEM((2, heads, edges), F32),
        pltpu.VMEM((2, hidden, edges), F32),
    ]
    scratch += [pltpu.VMEM((2, slots, 25 * channels), BF16) for _ in range(4)]
    scratch += [pltpu.VMEM((half, 2, *w), BF16) for w in w_shapes]
    scratch += [pltpu.VMEM((n * w[0], w[1]) if w[0] % 16 else (8, 128), F32) for w in w_shapes]
    scratch += [pltpu.VMEM((half, 2, *t), BF16) for t in t_shapes]
    scratch += [pltpu.VMEM((half, 2, *t), BF16) for t in t_shapes]
    scratch += [pltpu.VMEM((half - 1, 2, *t), BF16) for _ in range(2) for t in t_shapes]
    scratch += [pltpu.VMEM((2, *t), F32) for t in t_shapes]
    scratch += [pltpu.VMEM((2, *t), BF16) for t in t_shapes]
    scratch += [pltpu.VMEM((2, 2, *t), BF16) for t in t_shapes]
    scratch += [pltpu.VMEM((2, *t), BF16) for t in t_shapes]
    steps = Halving(half).steps
    scratch += [dma((4,)) for _ in range(2)]
    scratch += [dma((half - 1, count)) for _ in range(2)]
    scratch += [dma((half, count)) for _ in range(2)]
    scratch += [dma((items,)) for _ in range(2)]
    scratch += [dma((steps, items)) for _ in range(2)]
    scratch += [dma((2, items)), dma((3, items)), dma((items,)), dma((items,)), dma((7 + count,))]
    given = (features, cotangent, rotation, src, tgt, send_left, send_right)
    scratch += [pltpu.VMEM(g.shape, g.dtype) for g in given]
    return pl.pallas_call(
        partial(slab_kernel, n, depth, sizes),
        out_shape=tuple(out_shape),
        in_specs=[pl.BlockSpec(memory_space=pl.ANY)] * (7 + count),
        out_specs=[vmem] * (2 + items),
        scratch_shapes=scratch,
        compiler_params=pltpu.CompilerParams(
            collective_id=0, has_side_effects=True, vmem_limit_bytes=60 * 2**20),
        name="slab",
    )(features, cotangent, rotation, src, tgt, send_left, send_right, *weights)


def finish_kernel(items, hidden, *refs):
    att_ref, grad_ref = refs[:2]
    final = refs[2:2 + items]
    out_att, out_grad = refs[2 + items:4 + items]
    gz_ref, g1r_ref, g1i_ref, g2r_ref, g2i_ref, gt_ref, ga_ref = refs[4 + items:]
    out_att[...] = att_ref[...]
    out_grad[...] = grad_ref[...]

    wide = 3 * hidden
    g1r_ref[...] = final[0][...].astype(F32)
    g1i_ref[...] = final[1][...].astype(F32)
    g2r_ref[...] = final[2][:, :wide].astype(F32)
    g2i_ref[...] = final[2][:, wide:].astype(F32)
    begin = 0
    for source in final[3:6]:
        end = begin + source.shape[1]
        gz_ref[:, begin:end] = source[...].astype(F32)
        begin = end
    gt_ref[...] = final[6][...].astype(F32)
    ga_ref[...] = final[7][...].astype(F32)


def finish(attended, grad, final, weights, hidden):
    items = len(final)
    vmem = pl.BlockSpec(memory_space=pltpu.VMEM)
    shapes = [jax.ShapeDtypeStruct(attended.shape, BF16), jax.ShapeDtypeStruct(grad.shape, F32)]
    shapes += [jax.ShapeDtypeStruct(w.shape, F32) for w in weights]
    return pl.pallas_call(
        partial(finish_kernel, items, hidden),
        out_shape=tuple(shapes),
        in_specs=[vmem] * (2 + items),
        out_specs=[vmem] * len(shapes),
        name="finish",
    )(attended, grad, *final)


def body(n, depth, features, cotangent, rotation, send_left, send_right, edge_src, edge_tgt,
         *weights):
    turned_rotation = jnp.swapaxes(rotation[0], 0, 1)
    attended, grad_features, *final = slab(
        n, depth, features[0], cotangent[0], turned_rotation, edge_src, edge_tgt,
        send_left, send_right, weights)
    attended, grad_features, *grads = finish(
        attended, grad_features, final, weights, weights[1].shape[1] // 4)
    return (attended[None], grad_features[None], *grads)


def solution(mesh):
    cell = P("dp", "graph", None)
    lists = P("dp", "graph")
    shard = P("graph", None)
    in_specs = (cell, cell, P("dp", None, "graph")) + (lists,) * 4 + (shard,) * 7
    out_specs = (cell, cell) + (shard,) * 7
    return jax.shard_map(
        partial(body, mesh.shape["graph"], mesh.shape["dp"]), mesh=mesh,
        in_specs=in_specs, out_specs=out_specs, check_vma=False)
```

```python
from functools import partial

import jax
import jax.numpy as jnp
from jax import lax
from jax.experimental import pallas as pl
from jax.experimental.pallas import tpu as pltpu
from jax.sharding import PartitionSpec as P

F32 = jnp.float32
BF16 = jnp.bfloat16
OFFSETS = {1: 0, 2: 9, 3: 34, 4: 69}
DEGREES = (1, 2, 3, 4)
BLOCK_C = 32
BLOCK_H = 16
MESH = pl.DeviceIdType.MESH
EXACT = lax.Precision.HIGHEST
ORDER = (
    "g1r", "s0", "g2", "s2", "ds0", "x0", "gzv", "s3", "x2", "g1i", "ds1", "s4", "s1", "x3",
    "dt0", "gwt", "x4", "s7", "dt2", "y0", "s5", "dt1", "y2", "x1", "tb0", "s6", "y3", "x6",
    "x5", "x7", "a0", "y4", "a2", "y1", "tb1", "tb2", "a3", "y6", "b0", "y5", "y7", "a4", "b2",
    "tb3", "a6", "att", "b3", "a1", "a5", "b4", "c0", "eg0", "c2", "eg1", "a7", "b1", "b6",
    "eg2", "eg3", "c3", "eg4", "b5", "ghost", "c4", "b7", "c1", "c6", "d3", "c5", "c7", "d0",
    "d1",
)
CUBE = (2, 4, 5, 6, 7)


def slot(degree, azimuth):
    return {0: degree, 1: 4 + degree, -1: 8 + degree, 2: 11 + degree, -2: 14 + degree}[azimuth]


def orders(degree):
    kept = min(degree, 2)
    return range(-kept, kept + 1)


def rot_row(degree, azimuth, column):
    return OFFSETS[degree] + (azimuth + min(degree, 2)) * (2 * degree + 1) + column


def dot(a, b, ca, cb, precision=None):
    return lax.dot_general(
        a, b, (((ca,), (cb,)), ((), ())), preferred_element_type=F32, precision=precision
    )


def flip(index, power):
    bit = lax.rem(lax.div(index, power), 2)
    return index + (1 - 2 * bit) * power


def flips(index, powers, chosen):
    for j in chosen:
        index = flip(index, powers[j])
    return index


def subsets(steps):
    found = [()]
    for j in steps:
        found = found + [s + (j,) for s in found]
    return found


class Halving:
    def __init__(self, count):
        self.steps = count.bit_length() - 1
        self.rest = [subsets(range(j + 1, self.steps)) for j in range(self.steps)]
        self.base = [0]
        for found in self.rest:
            self.base.append(self.base[-1] + len(found))

    def spot(self, step, chosen):
        return self.base[step] + self.rest[step].index(chosen)


def slab_kernel(n, depth, sizes, *refs):
    take = iter(refs)
    placed = [next(take) for _ in range(7)]
    count = len(sizes["weights"])
    items = len(sizes["terms"])
    shards = [next(take) for _ in range(count)]
    att_ref, grad_ref = next(take), next(take)
    final = [next(take) for _ in range(items)]
    (ext_ref, alphas, d_alphas, rotf, xs, turned, hid, msg, dmsg, scores, dhid, dmixed, dturned,
     dxs, small, spreads) = [next(take) for _ in range(16)]
    outgoing, near, ghost, back = [next(take) for _ in range(4)]
    full = [next(take) for _ in range(count)]
    mats = [next(take) for _ in range(count)]
    terms = [next(take) for _ in range(items)]
    landed = [next(take) for _ in range(items)]
    out_xy = [next(take) for _ in range(items)]
    in_xy = [next(take) for _ in range(items)]
    out_z = [next(take) for _ in range(items)]
    in_z = [next(take) for _ in range(items)]
    (side_send, side_recv, hop_send, hop_recv, core_send, core_recv, sib_send, sib_recv,
     xy_send, xy_recv, z_send, z_recv, in_sem) = [next(take) for _ in range(13)]
    local = list(take)
    feat_ref, cot_ref, rot_ref, src_ref, tgt_ref, left_ref, right_ref = local

    edges = src_ref.shape[1]
    rows = ext_ref.shape[0]
    atoms = att_ref.shape[0]
    channels = n * sizes["weights"][5][0]
    hidden = sizes["weights"][1][1] // 4
    heads = small.shape[1]
    width = alphas.shape[0]
    slots = left_ref.shape[1]

    me = lax.axis_index("graph")
    row = lax.axis_index("dp")
    half = n // 2
    chip = lax.div(me, 2)
    parity = lax.rem(me, 2)
    sibling = me + 1 - 2 * parity
    right, left = lax.rem(me + 1, n), lax.rem(me + n - 1, n)
    plan = Halving(half)
    steps = plan.steps
    deep = Halving(depth).steps
    z_spots = max(deep, 2)
    powers = [2 ** j + parity * (2 ** ((j + 1) % steps) - 2 ** j) for j in range(steps)]

    upper = lax.div(row, depth // 2)
    inward = row + 1 - 2 * upper
    outward = row - 1 + 2 * upper
    from_end = row + upper * (depth - 1 - 2 * row)
    at_middle = lax.div(from_end + 1, depth // 2)
    is_end = from_end == 0
    is_middle = at_middle == 1

    barrier = pltpu.get_barrier_semaphore()
    partners = [(row, sibling), (row, right), (row, left)]
    partners += [(row, 2 * flip(chip, p) + parity) for p in powers]
    partners += [(flip(row, 2 ** j), me) for j in range(deep)]
    for partner in partners:
        pl.semaphore_signal(barrier, inc=1, device_id=partner, device_id_type=MESH)
    for z in (-1, 1):
        other = row + z

        @pl.when((other >= 0) & (other < depth))
        def _():
            pl.semaphore_signal(barrier, inc=1, device_id=(other, me), device_id_type=MESH)

    def remote(src, dst, send, recv, target):
        copy = pltpu.make_async_remote_copy(
            src_ref=src, dst_ref=dst, send_sem=send, recv_sem=recv,
            device_id=target, device_id_type=MESH)
        copy.start()
        return copy

    started = []

    loads = {}

    def load(key, src, dst, spot):
        copy = pltpu.make_async_copy(src, dst, in_sem.at[spot])
        copy.start()
        loads[key] = copy

    for k in (0, 5, 6):
        load(k, placed[k], local[k], k)
    for w in range(count):
        load(("w", w), shards[w], full[w].at[chip, parity], 7 + w)
    for k in (3, 4, 2, 1):
        load(k, placed[k], local[k], k)
    for k in (0, 5, 6):
        loads[k].wait()
    own = feat_ref[...].astype(BF16)
    ext_ref[:atoms, :] = own
    for side, list_ref in ((0, left_ref), (1, right_ref)):
        ids = lax.broadcasted_iota(jnp.int32, (atoms, slots), 0)
        pick = (ids == list_ref[...]).astype(F32).astype(BF16)
        outgoing[side] = dot(pick, own, 0, 0).astype(BF16)
    for w in range(count):
        loads["w", w].wait()

    pl.semaphore_wait(barrier, len(partners) + 1 + lax.div(from_end + depth - 1, depth))

    sides = []
    for side, target in ((1, left), (0, right)):
        sides.append(remote(outgoing.at[1 - side], near.at[side], side_send.at[side],
                            side_recv.at[side], (row, target)))
    arrivals = {}

    def hop(j, w, part):
        target = (row, 2 * flip(chip, powers[j]) + parity)
        for t, chosen in enumerate(subsets(range(j))):
            if (t > 0) != part:
                continue
            unit = flips(chip, powers, chosen)
            copy = remote(full[w].at[unit, parity], full[w].at[unit, parity],
                          hop_send.at[2 ** j + t - 1, w], hop_recv.at[2 ** j + t - 1, w], target)
            arrivals[j, t, w] = copy
            started.append(copy)

    crossing = {}

    def cross(spot, unit, w):
        copy = remote(full[w].at[unit, parity], full[w].at[unit, parity],
                      core_send.at[spot, w], core_recv.at[spot, w], (row, sibling))
        crossing[spot, w] = copy
        started.append(copy)

    def land(j, w, part):
        partner = flip(chip, powers[j])
        for t, chosen in enumerate(subsets(range(j))):
            if (t > 0) == part:
                arrivals[j, t, w].wait_recv()
                cross(2 ** j + t, flips(partner, powers, chosen), w)

    weight_order = (0, 5, 6, 1, 2, 3, 4)
    for j in range(steps):
        for w in weight_order:
            hop(j, w, False)
    for w in weight_order:
        cross(0, chip, w)

    for k in (3, 4, 2, 1):
        loads[k].wait()
    src_hot = (
        lax.broadcasted_iota(jnp.int32, (rows, edges), 0) == src_ref[...]
    ).astype(F32).astype(BF16)
    member = (lax.broadcasted_iota(jnp.int32, (atoms, edges), 0) == tgt_ref[...]).astype(F32)
    member_b = member.astype(BF16)

    edge_eye = (
        lax.broadcasted_iota(jnp.int32, (rot_ref.shape[1], rot_ref.shape[1]), 0)
        == lax.broadcasted_iota(jnp.int32, (rot_ref.shape[1], rot_ref.shape[1]), 1)
    ).astype(F32).astype(BF16)
    rotf[...] = dot(edge_eye, rot_ref[...], 1, 1)
    for k in range(25):
        dmsg[k] = dot(
            cot_ref[:, k * hidden:(k + 1) * hidden].astype(BF16), member_b, 0, 0
        )
    for copy in sides:
        copy.wait_recv()
    ext_ref[atoms:, :] = near[...].astype(F32).reshape(rows - atoms, -1).astype(BF16)
    for k in range(25):
        xs[k] = dot(ext_ref[:, k * channels:(k + 1) * channels], src_hot, 0, 0)

    for j in range(1, steps):
        for w in weight_order:
            land(j - 1, w, False)
            land(j - 1, w, True)
            hop(j, w, True)

    def turn(i, carry):
        part = pl.ds(pl.multiple_of(i * BLOCK_C, BLOCK_C), BLOCK_C)
        turned[0, part, :] = xs[0, part, :].astype(BF16)
        for degree in DEGREES:
            for azimuth in orders(degree):
                total = None
                for m in range(2 * degree + 1):
                    k = rot_row(degree, azimuth, m)
                    term = rotf[k:k + 1, :] * xs[degree * degree + m, part, :]
                    total = term if total is None else total + term
                turned[slot(degree, azimuth), part, :] = total.astype(BF16)
        return carry

    lax.fori_loop(0, channels // BLOCK_C, turn, 0)

    zero_in = turned[0:5].reshape(5 * channels, edges)
    one_pos = turned[5:9].reshape(4 * channels, edges)
    one_neg = turned[9:13].reshape(4 * channels, edges)
    two_pos = turned[13:16].reshape(3 * channels, edges)
    two_neg = turned[16:19].reshape(3 * channels, edges)

    def settle(w):
        for spot in range(half):
            crossing[spot, w].wait_recv()
        block = sizes["weights"][w][0]
        if block % 16:
            for u in range(half):
                for c in range(2):
                    at = (2 * u + c) * block
                    mats[w][at:at + block, :] = full[w][u, c].astype(mats[w].dtype)

    def weight(w, begin=0, end=None):
        block, wide = sizes["weights"][w]
        end = wide if end is None else end
        if block % 16:
            return mats[w][:, begin:end].astype(BF16)
        return full[w][:, :, :, begin:end].reshape(n * block, end - begin)

    for w in weight_order:
        land(steps - 1, w, False)
    for w in (0, 5, 6, 1, 2):
        land(steps - 1, w, True)
    for w in (0, 5, 6):
        settle(w)
    alpha_rows = sizes["weights"][6][0]
    for u in range(half):
        for c in range(2):
            at = (2 * u + c) * alpha_rows
            alphas[at:at + alpha_rows, :] = full[6][u, c].astype(F32)

    per_atom = dot(ext_ref[:atoms, :channels], weight(5), 1, 0)
    high = per_atom.astype(BF16)
    low = (per_atom - high.astype(F32)).astype(BF16)
    scores[...] = (
        dot(weight(0, 5 * hidden), zero_in, 0, 0)
        + dot(high, member_b, 0, 0)
        + dot(low, member_b, 0, 0)
    )
    hid[0:5] = dot(weight(0, 0, 5 * hidden), zero_in, 0, 0).reshape(5, hidden, edges)

    for w in (3, 4):
        land(steps - 1, w, True)

    for h in range(heads):
        part = slice(h * width, (h + 1) * width)
        value = scores[part, :]
        centre = value - jnp.mean(value, axis=0, keepdims=True)
        scale = lax.rsqrt(jnp.mean(centre * centre, axis=0, keepdims=True) + 1e-05)
        normed = centre * scale
        scores[part, :] = normed
        gate = 0.2 + 0.8 * jax.nn.sigmoid(normed)
        small[0, h:h + 1, :] = jnp.sum(
            normed * gate * alphas[:, h:h + 1], axis=0, keepdims=True
        )
        small[1, h:h + 1, :] = scale

    raised = jnp.exp(small[0])
    totals = dot(dot(raised, member, 1, 1, EXACT), member, 1, 0, EXACT)
    weights = raised / totals
    spreads[0] = jnp.broadcast_to(
        weights[:, None, :], (heads, hidden // heads, edges)
    ).reshape(hidden, edges)

    settle(1)
    settle(2)
    hid[5:9] = (dot(weight(1), one_pos, 0, 0) - dot(weight(2), one_neg, 0, 0)).reshape(
        4, hidden, edges)
    hid[9:13] = (dot(weight(1), one_neg, 0, 0) + dot(weight(2), one_pos, 0, 0)).reshape(
        4, hidden, edges)
    settle(3)
    settle(4)
    hid[13:16] = (dot(weight(3), two_pos, 0, 0) - dot(weight(4), two_neg, 0, 0)).reshape(
        3, hidden, edges)
    hid[16:19] = (dot(weight(3), two_neg, 0, 0) + dot(weight(4), two_pos, 0, 0)).reshape(
        3, hidden, edges)

    def mix(i, carry):
        part = pl.ds(pl.multiple_of(i * BLOCK_H, BLOCK_H), BLOCK_H)
        spread = spreads[0, part, :]
        scalar = hid[0, part, :]
        gating = jax.nn.sigmoid(scalar)
        silu = scalar * gating
        both = gating * spread
        msg[0, part, :] = (silu * spread).astype(BF16)
        d_first = dmsg[0, part, :]
        inner = jnp.zeros_like(scalar)
        for degree in DEGREES:
            size = 2 * degree + 1
            sums = [None] * size
            for azimuth in orders(degree):
                raw = hid[slot(degree, azimuth), part, :]
                value = raw * both
                back_sum = None
                for m in range(size):
                    k = rot_row(degree, azimuth, m)
                    line = rotf[k:k + 1, :]
                    term = line * value
                    sums[m] = term if sums[m] is None else sums[m] + term
                    other = line * dmsg[degree * degree + m, part, :]
                    back_sum = other if back_sum is None else back_sum + other
                inner = inner + back_sum * raw
                dhid[slot(degree, azimuth), part, :] = (back_sum * both).astype(BF16)
            for m in range(size):
                msg[degree * degree + m, part, :] = sums[m].astype(BF16)
        spreads[1, part, :] = inner * gating + d_first * silu
        d_scalar = d_first * spread * gating * (1.0 + scalar * (1.0 - gating)) + (
            inner * spread * gating * (1.0 - gating)
        )
        dhid[0, part, :] = d_scalar.astype(BF16)
        return carry

    lax.fori_loop(0, hidden // BLOCK_H, mix, 0)

    def put(i, value, begin=0):
        block = sizes["terms"][i][0]
        wide = value.shape[1]
        if block % 16:
            for u in range(half):
                for c in range(2):
                    at = (2 * u + c) * block
                    terms[i][u, c, :, begin:begin + wide] = value[at:at + block, :].astype(BF16)
        else:
            terms[i][:, :, :, begin:begin + wide] = value.astype(BF16).reshape(
                half, 2, block, wide)

    flights = {}

    def launch(key, src, dst, send, recv, target):
        copy = remote(src, dst, send, recv, target)
        flights[key] = copy
        started.append(copy)

    def to_sibling(i):
        launch(("core", i), terms[i].at[:, 1 - parity], landed[i], sib_send.at[i], sib_recv.at[i],
               (row, sibling))

    def chip_sum(i, step, chosen):
        unit = flips(chip, powers, chosen)
        total = terms[i][unit, parity] + landed[i][unit]
        for s in range(step):
            total = total + in_xy[i][plan.spot(s, chosen)]
        return total

    def to_chip(i, step):
        if step == 0:
            flights["core", i].wait_recv()
        else:
            flights["xy", step - 1, i].wait_recv()
        begin, end = plan.base[step], plan.base[step + 1]
        for t, rest in enumerate(plan.rest[step]):
            out_xy[i][begin + t] = chip_sum(i, step, (step,) + rest)
        target = (row, 2 * flip(chip, powers[step]) + parity)
        launch(("xy", step, i), out_xy[i].at[begin:end], in_xy[i].at[begin:end],
               xy_send.at[step, i], xy_recv.at[step, i], target)

    def z_copy(i, out, spot, target):
        return pltpu.make_async_remote_copy(
            src_ref=out_z[i].at[out], dst_ref=in_z[i].at[spot],
            send_sem=z_send.at[out, i], recv_sem=z_recv.at[spot, i],
            device_id=(target, me), device_id_type=MESH)

    def inward_copy(i, spot):
        return z_copy(i, 0, spot, inward)

    def swap_copy(i, step):
        return z_copy(i, step, step, flip(row, 2 ** step))

    def outward_copy(i):
        return pltpu.make_async_remote_copy(
            src_ref=final[i], dst_ref=final[i],
            send_sem=z_send.at[deep, i], recv_sem=z_recv.at[z_spots, i],
            device_id=(outward, me), device_id_type=MESH)

    def layer_total(i):
        flights["xy", steps - 1, i].wait_recv()
        out_z[i][0] = chip_sum(i, steps, ())

    def on_line(i, stage):
        if stage == 0:
            layer_total(i)

            @pl.when(is_end)
            def _():
                inward_copy(i, at_middle).start()
        elif stage == 1:
            @pl.when(jnp.logical_not(is_end))
            def _():
                inward_copy(i, 0).wait_recv()
                out_z[i][0] = out_z[i][0] + in_z[i][0]
                inward_copy(i, at_middle).start()
        elif stage == 2:
            @pl.when(is_middle)
            def _():
                inward_copy(i, 1).wait_recv()
                final[i][...] = out_z[i][0] + in_z[i][1]
                if depth > 2:
                    outward_copy(i).start()
        else:
            @pl.when(jnp.logical_not(is_middle))
            def _():
                outward_copy(i).wait_recv()
                if depth > 4:
                    @pl.when(jnp.logical_not(is_end))
                    def _():
                        outward_copy(i).start()

    def on_cube(i, stage):
        if stage == 0:
            layer_total(i)
            swap_copy(i, 0).start()
        elif stage == 1:
            for step in range(1, deep):
                swap_copy(i, step - 1).wait_recv()
                out_z[i][step] = out_z[i][step - 1] + in_z[i][step - 1]
                swap_copy(i, step).start()
        elif stage == 2:
            swap_copy(i, deep - 1).wait_recv()
            final[i][...] = out_z[i][deep - 1] + in_z[i][deep - 1]

    def advance(i, stage):
        if stage == 0:
            to_sibling(i)
        elif stage <= steps:
            to_chip(i, stage - 1)
        else:
            (on_cube if i in CUBE else on_line)(i, stage - 1 - steps)

    def bands(first, number):
        middle = first + number
        last = middle + number
        return (dhid[first:middle].reshape(number * hidden, edges),
                dhid[middle:last].reshape(number * hidden, edges))

    def one_re():
        up, down = bands(5, 4)
        put(0, dot(one_pos, up, 1, 1) + dot(one_neg, down, 1, 1))

    def one_im():
        up, down = bands(5, 4)
        put(1, dot(one_pos, down, 1, 1) - dot(one_neg, up, 1, 1))

    def two():
        up, down = bands(13, 3)
        put(2, dot(two_pos, up, 1, 1) + dot(two_neg, down, 1, 1))
        put(2, dot(two_pos, down, 1, 1) - dot(two_neg, up, 1, 1), 3 * hidden)

    def values():
        d_values = dhid[0:5].reshape(5 * hidden, edges)
        dmixed[:5 * hidden, :] = d_values
        put(3, dot(zero_in, d_values, 1, 1))

    def score_grads(which):
        if which == 0:
            d_weights = jnp.sum(
                spreads[1].reshape(heads, hidden // heads, edges), axis=1
            )
            product = weights * d_weights
            small[0] = product - weights * dot(
                dot(product, member, 1, 1, EXACT), member, 1, 0, EXACT
            )
        group = heads // 2
        for h in range(which * group, (which + 1) * group):
            part = slice(h * width, (h + 1) * width)
            normed = scores[part, :]
            sig = jax.nn.sigmoid(normed)
            gate = 0.2 + 0.8 * sig
            d_logit = small[0, h:h + 1, :]
            d_alphas[:, h:h + 1] = jnp.sum(normed * gate * d_logit, axis=1, keepdims=True)
            d_norm = d_logit * alphas[:, h:h + 1] * (gate + 0.8 * normed * sig * (1.0 - sig))
            first = jnp.mean(d_norm, axis=0, keepdims=True)
            second = jnp.mean(d_norm * normed, axis=0, keepdims=True)
            d_score = small[1, h:h + 1, :] * (d_norm - first - normed * second)
            dmixed[5 * hidden + h * width:5 * hidden + (h + 1) * width, :] = d_score.astype(BF16)
            scores[part, :] = d_score
        begin = 5 * hidden + which * group * width
        put(4 + which, dot(zero_in, dmixed[begin:begin + group * width, :], 1, 1))

    held = {}

    def target_alpha():
        held["atom"] = dot(member, scores[...], 1, 1, EXACT).astype(BF16)
        put(6, dot(ext_ref[:atoms, :channels], held["atom"], 0, 0))
        for u in range(half):
            for c in range(2):
                at = (2 * u + c) * alpha_rows
                terms[7][u, c] = d_alphas[at:at + alpha_rows, :].astype(BF16)

    def turn_zero():
        dturned[0:5] = dot(weight(0), dmixed[...], 1, 0).reshape(5, channels, edges)

    def turn_pair(first, number, re_item, im_item):
        up, down = bands(first, number)
        middle = first + number
        last = middle + number
        dturned[first:middle] = (
            dot(weight(re_item), up, 1, 0) + dot(weight(im_item), down, 1, 0)
        ).reshape(number, channels, edges)
        dturned[middle:last] = (
            dot(weight(re_item), down, 1, 0) - dot(weight(im_item), up, 1, 0)
        ).reshape(number, channels, edges)

    def turn_back(i, carry):
        part = pl.ds(pl.multiple_of(i * BLOCK_C, BLOCK_C), BLOCK_C)
        dxs[0, part, :] = dturned[0, part, :].astype(BF16)
        for degree in DEGREES:
            for m in range(2 * degree + 1):
                total = None
                for azimuth in orders(degree):
                    k = rot_row(degree, azimuth, m)
                    term = rotf[k:k + 1, :] * dturned[slot(degree, azimuth), part, :]
                    total = term if total is None else total + term
                dxs[degree * degree + m, part, :] = total.astype(BF16)
        return carry

    blocks = channels // BLOCK_C

    def source_grads(k):
        part = slice(5 * k * channels, 5 * (k + 1) * channels)
        ext_grad = dot(src_hot, dxs[5 * k:5 * k + 5].reshape(5 * channels, edges), 1, 1)
        grad_ref[:, part] = ext_grad[:atoms]
        if k == 0:
            grad_ref[:, :channels] = ext_grad[:atoms, :channels] + dot(
                held["atom"], weight(5), 1, 1)
        for side in range(2):
            begin = atoms + side * slots
            ghost[side, :, part] = ext_grad[begin:begin + slots].astype(BF16)

    returns = []

    def return_ghosts():
        for side, target in ((0, left), (1, right)):
            returns.append(remote(ghost.at[side], back.at[side], side_send.at[2 + side],
                                  side_recv.at[2 + side], (row, target)))

    def attend():
        att_ref[...] = dot(member_b, msg[...].reshape(25 * hidden, edges), 1, 1).astype(BF16)

    work = {
        "g1r": one_re, "g1i": one_im, "g2": two, "gzv": values,
        "ds0": partial(score_grads, 0), "ds1": partial(score_grads, 1), "gwt": target_alpha,
        "dt0": turn_zero, "dt1": partial(turn_pair, 5, 4, 1, 2),
        "dt2": partial(turn_pair, 13, 3, 3, 4),
        "ghost": return_ghosts, "att": attend,
    }
    for k in range(4):
        work["tb%d" % k] = partial(
            lax.fori_loop, k * blocks // 4, (k + 1) * blocks // 4, turn_back, 0)
    for k in range(5):
        work["eg%d" % k] = partial(source_grads, k)
    for step in ORDER:
        if step in work:
            work[step]()
        else:
            first, last = {
                "s": (0, 1), "x": (1, 2), "y": (2, 1 + steps), "a": (1 + steps, 2 + steps),
                "b": (2 + steps, 3 + steps), "c": (3 + steps, 4 + steps),
                "d": (4 + steps, 5 + steps)}[step[0]]
            for stage in range(first, last):
                for i in step[1:]:
                    advance(int(i), stage)

    for copy in returns:
        copy.wait_recv()
    total = grad_ref[...]
    for side, list_ref in ((0, right_ref), (1, left_ref)):
        ids = lax.broadcasted_iota(jnp.int32, (atoms, slots), 0)
        place = (ids == list_ref[...]).astype(F32).astype(BF16)
        total = total + dot(place, back[side], 1, 0)
    grad_ref[...] = total
    for i in range(items):
        if i in CUBE:
            for step in range(deep):
                swap_copy(i, step).wait_send()
            continue
        inward_copy(i, at_middle).wait_send()
        if depth > 2:
            @pl.when(jnp.logical_not(is_end))
            def _():
                outward_copy(i).wait_send()
    for copy in sides + returns + started:
        copy.wait_send()


def slab(n, depth, features, cotangent, rotation, src, tgt, send_left, send_right, weights):
    atoms = features.shape[0]
    edges = src.shape[1]
    slots = send_left.shape[1]
    heads = weights[6].shape[1]
    head_width = n * weights[6].shape[0]
    channels = n * weights[5].shape[0]
    hidden = weights[1].shape[1] // 4
    half = n // 2
    w_shapes = [tuple(w.shape) for w in weights]
    block = w_shapes[0][0]
    logits = (w_shapes[0][1] - 5 * hidden) // 2
    t_shapes = w_shapes[1:3] + [(w_shapes[3][0], 6 * hidden), (block, 5 * hidden)]
    t_shapes += [(block, logits)] * 2 + w_shapes[5:]
    sizes = {"weights": w_shapes, "terms": t_shapes}
    count, items = len(w_shapes), len(t_shapes)

    shape = jax.ShapeDtypeStruct
    vmem = pl.BlockSpec(memory_space=pltpu.VMEM)
    out_shape = [shape((atoms, 25 * hidden), BF16), shape((atoms, 25 * channels), F32)]
    out_shape += [shape(t, BF16) for t in t_shapes]
    rows = atoms + 2 * slots
    mixed = w_shapes[0][1]
    rots = rotation.shape[1]
    dma = pltpu.SemaphoreType.DMA
    scratch = [
        pltpu.VMEM((rows, 25 * channels), BF16),
        pltpu.VMEM((head_width, heads), F32),
        pltpu.VMEM((head_width, heads), F32),
        pltpu.VMEM((rots, edges), F32),
        pltpu.VMEM((25, channels, edges), F32),
        pltpu.VMEM((19, channels, edges), BF16),
        pltpu.VMEM((19, hidden, edges), F32),
        pltpu.VMEM((25, hidden, edges), BF16),
        pltpu.VMEM((25, hidden, edges), F32),
        pltpu.VMEM((head_width * heads, edges), F32),
        pltpu.VMEM((19, hidden, edges), BF16),
        pltpu.VMEM((mixed, edges), BF16),
        pltpu.VMEM((19, channels, edges), F32),
        pltpu.VMEM((25, channels, edges), BF16),
        pltpu.VMEM((2, heads, edges), F32),
        pltpu.VMEM((2, hidden, edges), F32),
    ]
    scratch += [pltpu.VMEM((2, slots, 25 * channels), BF16) for _ in range(4)]
    scratch += [pltpu.VMEM((half, 2, *w), BF16) for w in w_shapes]
    scratch += [pltpu.VMEM((n * w[0], w[1]) if w[0] % 16 else (8, 128), F32) for w in w_shapes]
    scratch += [pltpu.VMEM((half, 2, *t), BF16) for t in t_shapes]
    scratch += [pltpu.VMEM((half, *t), BF16) for t in t_shapes]
    scratch += [pltpu.VMEM((half - 1, *t), BF16) for _ in range(2) for t in t_shapes]
    steps, deep = Halving(half).steps, Halving(depth).steps
    scratch += [pltpu.VMEM((deep, *t), BF16) for t in t_shapes]
    scratch += [pltpu.VMEM((max(deep, 2), *t), BF16) for t in t_shapes]
    scratch += [dma((4,)) for _ in range(2)]
    scratch += [dma((half - 1, count)) for _ in range(2)]
    scratch += [dma((half, count)) for _ in range(2)]
    scratch += [dma((items,)) for _ in range(2)]
    scratch += [dma((steps, items)) for _ in range(2)]
    scratch += [dma((deep + 1, items)), dma((max(deep, 2) + 1, items)), dma((7 + count,))]
    given = (features, cotangent, rotation, src, tgt, send_left, send_right)
    scratch += [pltpu.VMEM(g.shape, g.dtype) for g in given]
    return pl.pallas_call(
        partial(slab_kernel, n, depth, sizes),
        out_shape=tuple(out_shape),
        in_specs=[pl.BlockSpec(memory_space=pl.ANY)] * (7 + count),
        out_specs=[vmem] * (2 + items),
        scratch_shapes=scratch,
        compiler_params=pltpu.CompilerParams(
            collective_id=0, has_side_effects=True, vmem_limit_bytes=60 * 2**20),
        name="slab",
    )(features, cotangent, rotation, src, tgt, send_left, send_right, *weights)


def finish_kernel(items, hidden, *refs):
    att_ref, grad_ref = refs[:2]
    final = refs[2:2 + items]
    out_att, out_grad = refs[2 + items:4 + items]
    gz_ref, g1r_ref, g1i_ref, g2r_ref, g2i_ref, gt_ref, ga_ref = refs[4 + items:]
    out_att[...] = att_ref[...]
    out_grad[...] = grad_ref[...]

    wide = 3 * hidden
    g1r_ref[...] = final[0][...].astype(F32)
    g1i_ref[...] = final[1][...].astype(F32)
    g2r_ref[...] = final[2][:, :wide].astype(F32)
    g2i_ref[...] = final[2][:, wide:].astype(F32)
    begin = 0
    for source in final[3:6]:
        end = begin + source.shape[1]
        gz_ref[:, begin:end] = source[...].astype(F32)
        begin = end
    gt_ref[...] = final[6][...].astype(F32)
    ga_ref[...] = final[7][...].astype(F32)


def finish(attended, grad, final, weights, hidden):
    items = len(final)
    vmem = pl.BlockSpec(memory_space=pltpu.VMEM)
    shapes = [jax.ShapeDtypeStruct(attended.shape, BF16), jax.ShapeDtypeStruct(grad.shape, F32)]
    shapes += [jax.ShapeDtypeStruct(w.shape, F32) for w in weights]
    return pl.pallas_call(
        partial(finish_kernel, items, hidden),
        out_shape=tuple(shapes),
        in_specs=[vmem] * (2 + items),
        out_specs=[vmem] * len(shapes),
        name="finish",
    )(attended, grad, *final)


def body(n, depth, features, cotangent, rotation, send_left, send_right, edge_src, edge_tgt,
         *weights):
    turned_rotation = jnp.swapaxes(rotation[0], 0, 1)
    attended, grad_features, *final = slab(
        n, depth, features[0], cotangent[0], turned_rotation, edge_src, edge_tgt,
        send_left, send_right, weights)
    attended, grad_features, *grads = finish(
        attended, grad_features, final, weights, weights[1].shape[1] // 4)
    return (attended[None], grad_features[None], *grads)


def solution(mesh):
    cell = P("dp", "graph", None)
    lists = P("dp", "graph")
    shard = P("graph", None)
    in_specs = (cell, cell, P("dp", None, "graph")) + (lists,) * 4 + (shard,) * 7
    out_specs = (cell, cell) + (shard,) * 7
    return jax.shard_map(
        partial(body, mesh.shape["graph"], mesh.shape["dp"]), mesh=mesh,
        in_specs=in_specs, out_specs=out_specs, check_vma=False)
```

```python
from functools import partial

import jax
import jax.numpy as jnp
from jax import lax
from jax.experimental import pallas as pl
from jax.experimental.pallas import tpu as pltpu
from jax.sharding import PartitionSpec as P

F32 = jnp.float32
BF16 = jnp.bfloat16
OFFSETS = {1: 0, 2: 9, 3: 34, 4: 69}
DEGREES = (1, 2, 3, 4)
BLOCK_C = 32
BLOCK_H = 16
MESH = pl.DeviceIdType.MESH
EXACT = lax.Precision.HIGHEST
ORDER = (
    "g1r", "s0", "g2", "s2", "ds0", "x0", "gzv", "s3", "x2", "g1i", "ds1", "s4", "s1", "x3",
    "dt0", "gwt", "x4", "s7", "dt2", "y0", "s5", "dt1", "y2", "x1", "tb0", "s6", "y3", "x6",
    "x5", "x7", "a0", "y4", "a2", "y1", "tb1", "tb2", "a3", "y6", "b0", "y5", "y7", "a4", "b2",
    "tb3", "a6", "att", "b3", "a1", "a5", "b4", "c0", "eg0", "c2", "eg1", "a7", "b1", "b6",
    "eg2", "eg3", "c3", "eg4", "b5", "ghost", "c4", "b7", "c1", "c6", "d3", "add", "c5", "c7",
    "d0", "d1",
)
CUBE = (2, 4, 5, 6, 7)


def slot(degree, azimuth):
    return {0: degree, 1: 4 + degree, -1: 8 + degree, 2: 11 + degree, -2: 14 + degree}[azimuth]


def orders(degree):
    kept = min(degree, 2)
    return range(-kept, kept + 1)


def rot_row(degree, azimuth, column):
    return OFFSETS[degree] + (azimuth + min(degree, 2)) * (2 * degree + 1) + column


def dot(a, b, ca, cb, precision=None):
    return lax.dot_general(
        a, b, (((ca,), (cb,)), ((), ())), preferred_element_type=F32, precision=precision
    )


def flip(index, power):
    bit = lax.rem(lax.div(index, power), 2)
    return index + (1 - 2 * bit) * power


def flips(index, powers, chosen):
    for j in chosen:
        index = flip(index, powers[j])
    return index


def subsets(steps):
    found = [()]
    for j in steps:
        found = found + [s + (j,) for s in found]
    return found


class Halving:
    def __init__(self, count):
        self.steps = count.bit_length() - 1
        self.rest = [subsets(range(j + 1, self.steps)) for j in range(self.steps)]
        self.base = [0]
        for found in self.rest:
            self.base.append(self.base[-1] + len(found))

    def spot(self, step, chosen):
        return self.base[step] + self.rest[step].index(chosen)


def slab_kernel(n, depth, sizes, *refs):
    take = iter(refs)
    placed = [next(take) for _ in range(7)]
    count = len(sizes["weights"])
    items = len(sizes["terms"])
    shards = [next(take) for _ in range(count)]
    results = [next(take) for _ in range(2 + items)]
    (ext_ref, alphas, d_alphas, rotf, xs, turned, hid, msg, dmsg, scores, dhid, dmixed, dturned,
     dxs, small, spreads) = [next(take) for _ in range(16)]
    outgoing, near, ghost, back = [next(take) for _ in range(4)]
    full = [next(take) for _ in range(count)]
    mats = [next(take) for _ in range(count)]
    terms = [next(take) for _ in range(items)]
    landed = [next(take) for _ in range(items)]
    out_xy = [next(take) for _ in range(items)]
    in_xy = [next(take) for _ in range(items)]
    out_z = [next(take) for _ in range(items)]
    in_z = [next(take) for _ in range(items)]
    (side_send, side_recv, hop_send, hop_recv, core_send, core_recv, sib_send, sib_recv,
     xy_send, xy_recv, z_send, z_recv, in_sem, out_sem) = [next(take) for _ in range(14)]
    local = [next(take) for _ in range(7)]
    leaving = list(take)
    att_ref, grad_ref = leaving[:2]
    final = leaving[2:]
    feat_ref, cot_ref, rot_ref, src_ref, tgt_ref, left_ref, right_ref = local

    edges = src_ref.shape[1]
    rows = ext_ref.shape[0]
    atoms = att_ref.shape[0]
    channels = n * sizes["weights"][5][0]
    hidden = sizes["weights"][1][1] // 4
    heads = small.shape[1]
    width = alphas.shape[0]
    slots = left_ref.shape[1]

    me = lax.axis_index("graph")
    row = lax.axis_index("dp")
    half = n // 2
    chip = lax.div(me, 2)
    parity = lax.rem(me, 2)
    sibling = me + 1 - 2 * parity
    right, left = lax.rem(me + 1, n), lax.rem(me + n - 1, n)
    plan = Halving(half)
    steps = plan.steps
    deep = Halving(depth).steps
    z_spots = max(deep, 2)
    powers = [2 ** j + parity * (2 ** ((j + 1) % steps) - 2 ** j) for j in range(steps)]

    upper = lax.div(row, depth // 2)
    inward = row + 1 - 2 * upper
    outward = row - 1 + 2 * upper
    from_end = row + upper * (depth - 1 - 2 * row)
    at_middle = lax.div(from_end + 1, depth // 2)
    is_end = from_end == 0
    is_middle = at_middle == 1

    barrier = pltpu.get_barrier_semaphore()
    partners = [(row, sibling), (row, right), (row, left)]
    partners += [(row, 2 * flip(chip, p) + parity) for p in powers]
    partners += [(flip(row, 2 ** j), me) for j in range(deep)]
    for partner in partners:
        pl.semaphore_signal(barrier, inc=1, device_id=partner, device_id_type=MESH)
    for z in (-1, 1):
        other = row + z

        @pl.when((other >= 0) & (other < depth))
        def _():
            pl.semaphore_signal(barrier, inc=1, device_id=(other, me), device_id_type=MESH)

    def remote(src, dst, send, recv, target):
        copy = pltpu.make_async_remote_copy(
            src_ref=src, dst_ref=dst, send_sem=send, recv_sem=recv,
            device_id=target, device_id_type=MESH)
        copy.start()
        return copy

    started = []

    loads = {}

    def load(key, src, dst, spot):
        copy = pltpu.make_async_copy(src, dst, in_sem.at[spot])
        copy.start()
        loads[key] = copy

    for k in (0, 5, 6):
        load(k, placed[k], local[k], k)
    for w in range(count):
        load(("w", w), shards[w], full[w].at[chip, parity], 7 + w)
    for k in (3, 4, 2, 1):
        load(k, placed[k], local[k], k)
    for k in (0, 5, 6):
        loads[k].wait()
    own = feat_ref[...].astype(BF16)
    ext_ref[:atoms, :] = own
    for side, list_ref in ((0, left_ref), (1, right_ref)):
        ids = lax.broadcasted_iota(jnp.int32, (atoms, slots), 0)
        pick = (ids == list_ref[...]).astype(F32).astype(BF16)
        outgoing[side] = dot(pick, own, 0, 0).astype(BF16)
    for w in range(count):
        loads["w", w].wait()

    pl.semaphore_wait(barrier, len(partners) + 1 + lax.div(from_end + depth - 1, depth))

    sides = []
    for side, target in ((1, left), (0, right)):
        sides.append(remote(outgoing.at[1 - side], near.at[side], side_send.at[side],
                            side_recv.at[side], (row, target)))
    arrivals = {}

    def hop(j, w, part):
        target = (row, 2 * flip(chip, powers[j]) + parity)
        for t, chosen in enumerate(subsets(range(j))):
            if (t > 0) != part:
                continue
            unit = flips(chip, powers, chosen)
            copy = remote(full[w].at[unit, parity], full[w].at[unit, parity],
                          hop_send.at[2 ** j + t - 1, w], hop_recv.at[2 ** j + t - 1, w], target)
            arrivals[j, t, w] = copy
            started.append(copy)

    crossing = {}

    def cross(spot, unit, w):
        copy = remote(full[w].at[unit, parity], full[w].at[unit, parity],
                      core_send.at[spot, w], core_recv.at[spot, w], (row, sibling))
        crossing[spot, w] = copy
        started.append(copy)

    def land(j, w, part):
        partner = flip(chip, powers[j])
        for t, chosen in enumerate(subsets(range(j))):
            if (t > 0) == part:
                arrivals[j, t, w].wait_recv()
                cross(2 ** j + t, flips(partner, powers, chosen), w)

    weight_order = (0, 5, 6, 1, 2, 3, 4)
    for j in range(steps):
        for w in weight_order:
            hop(j, w, False)
    for w in weight_order:
        cross(0, chip, w)

    for k in (3, 4, 2, 1):
        loads[k].wait()
    src_hot = (
        lax.broadcasted_iota(jnp.int32, (rows, edges), 0) == src_ref[...]
    ).astype(F32).astype(BF16)
    member = (lax.broadcasted_iota(jnp.int32, (atoms, edges), 0) == tgt_ref[...]).astype(F32)
    member_b = member.astype(BF16)

    edge_eye = (
        lax.broadcasted_iota(jnp.int32, (rot_ref.shape[1], rot_ref.shape[1]), 0)
        == lax.broadcasted_iota(jnp.int32, (rot_ref.shape[1], rot_ref.shape[1]), 1)
    ).astype(F32).astype(BF16)
    rotf[...] = dot(edge_eye, rot_ref[...], 1, 1)
    for k in range(25):
        dmsg[k] = dot(
            cot_ref[:, k * hidden:(k + 1) * hidden].astype(BF16), member_b, 0, 0
        )
    for copy in sides:
        copy.wait_recv()
    ext_ref[atoms:, :] = near[...].astype(F32).reshape(rows - atoms, -1).astype(BF16)
    for k in range(25):
        xs[k] = dot(ext_ref[:, k * channels:(k + 1) * channels], src_hot, 0, 0)

    for j in range(1, steps):
        for w in weight_order:
            land(j - 1, w, False)
            land(j - 1, w, True)
            hop(j, w, True)

    def turn(i, carry):
        part = pl.ds(pl.multiple_of(i * BLOCK_C, BLOCK_C), BLOCK_C)
        turned[0, part, :] = xs[0, part, :].astype(BF16)
        for degree in DEGREES:
            for azimuth in orders(degree):
                total = None
                for m in range(2 * degree + 1):
                    k = rot_row(degree, azimuth, m)
                    term = rotf[k:k + 1, :] * xs[degree * degree + m, part, :]
                    total = term if total is None else total + term
                turned[slot(degree, azimuth), part, :] = total.astype(BF16)
        return carry

    lax.fori_loop(0, channels // BLOCK_C, turn, 0)

    zero_in = turned[0:5].reshape(5 * channels, edges)
    one_pos = turned[5:9].reshape(4 * channels, edges)
    one_neg = turned[9:13].reshape(4 * channels, edges)
    two_pos = turned[13:16].reshape(3 * channels, edges)
    two_neg = turned[16:19].reshape(3 * channels, edges)

    def settle(w):
        for spot in range(half):
            crossing[spot, w].wait_recv()
        block = sizes["weights"][w][0]
        if block % 16:
            for u in range(half):
                for c in range(2):
                    at = (2 * u + c) * block
                    mats[w][at:at + block, :] = full[w][u, c].astype(mats[w].dtype)

    def weight(w, begin=0, end=None):
        block, wide = sizes["weights"][w]
        end = wide if end is None else end
        if block % 16:
            return mats[w][:, begin:end].astype(BF16)
        return full[w][:, :, :, begin:end].reshape(n * block, end - begin)

    for w in weight_order:
        land(steps - 1, w, False)
    for w in (0, 5, 6, 1, 2):
        land(steps - 1, w, True)
    for w in (0, 5, 6):
        settle(w)
    alpha_rows = sizes["weights"][6][0]
    for u in range(half):
        for c in range(2):
            at = (2 * u + c) * alpha_rows
            alphas[at:at + alpha_rows, :] = full[6][u, c].astype(F32)

    per_atom = dot(ext_ref[:atoms, :channels], weight(5), 1, 0)
    high = per_atom.astype(BF16)
    low = (per_atom - high.astype(F32)).astype(BF16)
    scores[...] = (
        dot(weight(0, 5 * hidden), zero_in, 0, 0)
        + dot(high, member_b, 0, 0)
        + dot(low, member_b, 0, 0)
    )
    hid[0:5] = dot(weight(0, 0, 5 * hidden), zero_in, 0, 0).reshape(5, hidden, edges)

    for w in (3, 4):
        land(steps - 1, w, True)

    for h in range(heads):
        part = slice(h * width, (h + 1) * width)
        value = scores[part, :]
        centre = value - jnp.mean(value, axis=0, keepdims=True)
        scale = lax.rsqrt(jnp.mean(centre * centre, axis=0, keepdims=True) + 1e-05)
        normed = centre * scale
        scores[part, :] = normed
        gate = 0.2 + 0.8 * jax.nn.sigmoid(normed)
        small[0, h:h + 1, :] = jnp.sum(
            normed * gate * alphas[:, h:h + 1], axis=0, keepdims=True
        )
        small[1, h:h + 1, :] = scale

    raised = jnp.exp(small[0])
    totals = dot(dot(raised, member, 1, 1, EXACT), member, 1, 0, EXACT)
    weights = raised / totals
    spreads[0] = jnp.broadcast_to(
        weights[:, None, :], (heads, hidden // heads, edges)
    ).reshape(hidden, edges)

    settle(1)
    settle(2)
    hid[5:9] = (dot(weight(1), one_pos, 0, 0) - dot(weight(2), one_neg, 0, 0)).reshape(
        4, hidden, edges)
    hid[9:13] = (dot(weight(1), one_neg, 0, 0) + dot(weight(2), one_pos, 0, 0)).reshape(
        4, hidden, edges)
    settle(3)
    settle(4)
    hid[13:16] = (dot(weight(3), two_pos, 0, 0) - dot(weight(4), two_neg, 0, 0)).reshape(
        3, hidden, edges)
    hid[16:19] = (dot(weight(3), two_neg, 0, 0) + dot(weight(4), two_pos, 0, 0)).reshape(
        3, hidden, edges)

    def mix(i, carry):
        part = pl.ds(pl.multiple_of(i * BLOCK_H, BLOCK_H), BLOCK_H)
        spread = spreads[0, part, :]
        scalar = hid[0, part, :]
        gating = jax.nn.sigmoid(scalar)
        silu = scalar * gating
        both = gating * spread
        msg[0, part, :] = (silu * spread).astype(BF16)
        d_first = dmsg[0, part, :]
        inner = jnp.zeros_like(scalar)
        for degree in DEGREES:
            size = 2 * degree + 1
            sums = [None] * size
            for azimuth in orders(degree):
                raw = hid[slot(degree, azimuth), part, :]
                value = raw * both
                back_sum = None
                for m in range(size):
                    k = rot_row(degree, azimuth, m)
                    line = rotf[k:k + 1, :]
                    term = line * value
                    sums[m] = term if sums[m] is None else sums[m] + term
                    other = line * dmsg[degree * degree + m, part, :]
                    back_sum = other if back_sum is None else back_sum + other
                inner = inner + back_sum * raw
                dhid[slot(degree, azimuth), part, :] = (back_sum * both).astype(BF16)
            for m in range(size):
                msg[degree * degree + m, part, :] = sums[m].astype(BF16)
        spreads[1, part, :] = inner * gating + d_first * silu
        d_scalar = d_first * spread * gating * (1.0 + scalar * (1.0 - gating)) + (
            inner * spread * gating * (1.0 - gating)
        )
        dhid[0, part, :] = d_scalar.astype(BF16)
        return carry

    lax.fori_loop(0, hidden // BLOCK_H, mix, 0)

    def put(i, value, begin=0):
        block = sizes["terms"][i][0]
        wide = value.shape[1]
        if block % 16:
            for u in range(half):
                for c in range(2):
                    at = (2 * u + c) * block
                    terms[i][u, c, :, begin:begin + wide] = value[at:at + block, :].astype(BF16)
        else:
            terms[i][:, :, :, begin:begin + wide] = value.astype(BF16).reshape(
                half, 2, block, wide)

    flights = {}

    def launch(key, src, dst, send, recv, target):
        copy = remote(src, dst, send, recv, target)
        flights[key] = copy
        started.append(copy)

    def to_sibling(i):
        launch(("core", i), terms[i].at[:, 1 - parity], landed[i], sib_send.at[i], sib_recv.at[i],
               (row, sibling))

    def chip_sum(i, step, chosen):
        unit = flips(chip, powers, chosen)
        total = terms[i][unit, parity] + landed[i][unit]
        for s in range(step):
            total = total + in_xy[i][plan.spot(s, chosen)]
        return total

    def to_chip(i, step):
        if step == 0:
            flights["core", i].wait_recv()
        else:
            flights["xy", step - 1, i].wait_recv()
        begin, end = plan.base[step], plan.base[step + 1]
        for t, rest in enumerate(plan.rest[step]):
            out_xy[i][begin + t] = chip_sum(i, step, (step,) + rest)
        target = (row, 2 * flip(chip, powers[step]) + parity)
        launch(("xy", step, i), out_xy[i].at[begin:end], in_xy[i].at[begin:end],
               xy_send.at[step, i], xy_recv.at[step, i], target)

    def z_copy(i, out, spot, target):
        return pltpu.make_async_remote_copy(
            src_ref=out_z[i].at[out], dst_ref=in_z[i].at[spot],
            send_sem=z_send.at[out, i], recv_sem=z_recv.at[spot, i],
            device_id=(target, me), device_id_type=MESH)

    def inward_copy(i, spot):
        return z_copy(i, 0, spot, inward)

    def swap_copy(i, step):
        return z_copy(i, step, step, flip(row, 2 ** step))

    def outward_copy(i):
        return pltpu.make_async_remote_copy(
            src_ref=final[i], dst_ref=final[i],
            send_sem=z_send.at[deep, i], recv_sem=z_recv.at[z_spots, i],
            device_id=(outward, me), device_id_type=MESH)

    def leave(k):
        return pltpu.make_async_copy(leaving[k], results[k], out_sem.at[k])

    def layer_total(i):
        flights["xy", steps - 1, i].wait_recv()
        out_z[i][0] = chip_sum(i, steps, ())

    def on_line(i, stage):
        if stage == 0:
            layer_total(i)

            @pl.when(is_end)
            def _():
                inward_copy(i, at_middle).start()
        elif stage == 1:
            @pl.when(jnp.logical_not(is_end))
            def _():
                inward_copy(i, 0).wait_recv()
                out_z[i][0] = out_z[i][0] + in_z[i][0]
                inward_copy(i, at_middle).start()
        elif stage == 2:
            @pl.when(is_middle)
            def _():
                inward_copy(i, 1).wait_recv()
                final[i][...] = out_z[i][0] + in_z[i][1]
                leave(2 + i).start()
                if depth > 2:
                    outward_copy(i).start()
        else:
            @pl.when(jnp.logical_not(is_middle))
            def _():
                outward_copy(i).wait_recv()
                if depth > 4:
                    @pl.when(jnp.logical_not(is_end))
                    def _():
                        outward_copy(i).start()
                leave(2 + i).start()

    def on_cube(i, stage):
        if stage == 0:
            layer_total(i)
            swap_copy(i, 0).start()
        elif stage == 1:
            for step in range(1, deep):
                swap_copy(i, step - 1).wait_recv()
                out_z[i][step] = out_z[i][step - 1] + in_z[i][step - 1]
                swap_copy(i, step).start()
        elif stage == 2:
            swap_copy(i, deep - 1).wait_recv()
            final[i][...] = out_z[i][deep - 1] + in_z[i][deep - 1]
            leave(2 + i).start()

    def advance(i, stage):
        if stage == 0:
            to_sibling(i)
        elif stage <= steps:
            to_chip(i, stage - 1)
        else:
            (on_cube if i in CUBE else on_line)(i, stage - 1 - steps)

    def bands(first, number):
        middle = first + number
        last = middle + number
        return (dhid[first:middle].reshape(number * hidden, edges),
                dhid[middle:last].reshape(number * hidden, edges))

    def one_re():
        up, down = bands(5, 4)
        put(0, dot(one_pos, up, 1, 1) + dot(one_neg, down, 1, 1))

    def one_im():
        up, down = bands(5, 4)
        put(1, dot(one_pos, down, 1, 1) - dot(one_neg, up, 1, 1))

    def two():
        up, down = bands(13, 3)
        put(2, dot(two_pos, up, 1, 1) + dot(two_neg, down, 1, 1))
        put(2, dot(two_pos, down, 1, 1) - dot(two_neg, up, 1, 1), 3 * hidden)

    def values():
        d_values = dhid[0:5].reshape(5 * hidden, edges)
        dmixed[:5 * hidden, :] = d_values
        put(3, dot(zero_in, d_values, 1, 1))

    def score_grads(which):
        if which == 0:
            d_weights = jnp.sum(
                spreads[1].reshape(heads, hidden // heads, edges), axis=1
            )
            product = weights * d_weights
            small[0] = product - weights * dot(
                dot(product, member, 1, 1, EXACT), member, 1, 0, EXACT
            )
        group = heads // 2
        for h in range(which * group, (which + 1) * group):
            part = slice(h * width, (h + 1) * width)
            normed = scores[part, :]
            sig = jax.nn.sigmoid(normed)
            gate = 0.2 + 0.8 * sig
            d_logit = small[0, h:h + 1, :]
            d_alphas[:, h:h + 1] = jnp.sum(normed * gate * d_logit, axis=1, keepdims=True)
            d_norm = d_logit * alphas[:, h:h + 1] * (gate + 0.8 * normed * sig * (1.0 - sig))
            first = jnp.mean(d_norm, axis=0, keepdims=True)
            second = jnp.mean(d_norm * normed, axis=0, keepdims=True)
            d_score = small[1, h:h + 1, :] * (d_norm - first - normed * second)
            dmixed[5 * hidden + h * width:5 * hidden + (h + 1) * width, :] = d_score.astype(BF16)
            scores[part, :] = d_score
        begin = 5 * hidden + which * group * width
        put(4 + which, dot(zero_in, dmixed[begin:begin + group * width, :], 1, 1))

    held = {}

    def target_alpha():
        held["atom"] = dot(member, scores[...], 1, 1, EXACT).astype(BF16)
        put(6, dot(ext_ref[:atoms, :channels], held["atom"], 0, 0))
        for u in range(half):
            for c in range(2):
                at = (2 * u + c) * alpha_rows
                terms[7][u, c] = d_alphas[at:at + alpha_rows, :].astype(BF16)

    def turn_zero():
        dturned[0:5] = dot(weight(0), dmixed[...], 1, 0).reshape(5, channels, edges)

    def turn_pair(first, number, re_item, im_item):
        up, down = bands(first, number)
        middle = first + number
        last = middle + number
        dturned[first:middle] = (
            dot(weight(re_item), up, 1, 0) + dot(weight(im_item), down, 1, 0)
        ).reshape(number, channels, edges)
        dturned[middle:last] = (
            dot(weight(re_item), down, 1, 0) - dot(weight(im_item), up, 1, 0)
        ).reshape(number, channels, edges)

    def turn_back(i, carry):
        part = pl.ds(pl.multiple_of(i * BLOCK_C, BLOCK_C), BLOCK_C)
        dxs[0, part, :] = dturned[0, part, :].astype(BF16)
        for degree in DEGREES:
            for m in range(2 * degree + 1):
                total = None
                for azimuth in orders(degree):
                    k = rot_row(degree, azimuth, m)
                    term = rotf[k:k + 1, :] * dturned[slot(degree, azimuth), part, :]
                    total = term if total is None else total + term
                dxs[degree * degree + m, part, :] = total.astype(BF16)
        return carry

    blocks = channels // BLOCK_C

    def source_grads(k):
        part = slice(5 * k * channels, 5 * (k + 1) * channels)
        ext_grad = dot(src_hot, dxs[5 * k:5 * k + 5].reshape(5 * channels, edges), 1, 1)
        grad_ref[:, part] = ext_grad[:atoms]
        if k == 0:
            grad_ref[:, :channels] = ext_grad[:atoms, :channels] + dot(
                held["atom"], weight(5), 1, 1)
        for side in range(2):
            begin = atoms + side * slots
            ghost[side, :, part] = ext_grad[begin:begin + slots].astype(BF16)

    returns = []

    def return_ghosts():
        for side, target in ((0, left), (1, right)):
            returns.append(remote(ghost.at[side], back.at[side], side_send.at[2 + side],
                                  side_recv.at[2 + side], (row, target)))

    def attend():
        att_ref[...] = dot(member_b, msg[...].reshape(25 * hidden, edges), 1, 1).astype(BF16)
        leave(0).start()

    def add_ghosts():
        for copy in returns:
            copy.wait_recv()
        total = grad_ref[...]
        for side, list_ref in ((0, right_ref), (1, left_ref)):
            ids = lax.broadcasted_iota(jnp.int32, (atoms, slots), 0)
            place = (ids == list_ref[...]).astype(F32).astype(BF16)
            total = total + dot(place, back[side], 1, 0)
        grad_ref[...] = total
        leave(1).start()

    work = {
        "g1r": one_re, "g1i": one_im, "g2": two, "gzv": values,
        "ds0": partial(score_grads, 0), "ds1": partial(score_grads, 1), "gwt": target_alpha,
        "dt0": turn_zero, "dt1": partial(turn_pair, 5, 4, 1, 2),
        "dt2": partial(turn_pair, 13, 3, 3, 4),
        "ghost": return_ghosts, "add": add_ghosts, "att": attend,
    }
    for k in range(4):
        work["tb%d" % k] = partial(
            lax.fori_loop, k * blocks // 4, (k + 1) * blocks // 4, turn_back, 0)
    for k in range(5):
        work["eg%d" % k] = partial(source_grads, k)
    for step in ORDER:
        if step in work:
            work[step]()
        else:
            first, last = {
                "s": (0, 1), "x": (1, 2), "y": (2, 1 + steps), "a": (1 + steps, 2 + steps),
                "b": (2 + steps, 3 + steps), "c": (3 + steps, 4 + steps),
                "d": (4 + steps, 5 + steps)}[step[0]]
            for stage in range(first, last):
                for i in step[1:]:
                    advance(int(i), stage)

    for i in range(items):
        if i in CUBE:
            for step in range(deep):
                swap_copy(i, step).wait_send()
            continue
        inward_copy(i, at_middle).wait_send()
        if depth > 2:
            @pl.when(jnp.logical_not(is_end))
            def _():
                outward_copy(i).wait_send()
    for copy in sides + returns + started:
        copy.wait_send()
    for k in range(2 + items):
        leave(k).wait()


def slab(n, depth, features, cotangent, rotation, src, tgt, send_left, send_right, weights):
    atoms = features.shape[0]
    edges = src.shape[1]
    slots = send_left.shape[1]
    heads = weights[6].shape[1]
    head_width = n * weights[6].shape[0]
    channels = n * weights[5].shape[0]
    hidden = weights[1].shape[1] // 4
    half = n // 2
    w_shapes = [tuple(w.shape) for w in weights]
    block = w_shapes[0][0]
    logits = (w_shapes[0][1] - 5 * hidden) // 2
    t_shapes = w_shapes[1:3] + [(w_shapes[3][0], 6 * hidden), (block, 5 * hidden)]
    t_shapes += [(block, logits)] * 2 + w_shapes[5:]
    sizes = {"weights": w_shapes, "terms": t_shapes}
    count, items = len(w_shapes), len(t_shapes)

    shape = jax.ShapeDtypeStruct
    vmem = pl.BlockSpec(memory_space=pltpu.VMEM)
    out_shape = [shape((atoms, 25 * hidden), BF16), shape((atoms, 25 * channels), F32)]
    out_shape += [shape(t, BF16) for t in t_shapes]
    rows = atoms + 2 * slots
    mixed = w_shapes[0][1]
    rots = rotation.shape[1]
    dma = pltpu.SemaphoreType.DMA
    scratch = [
        pltpu.VMEM((rows, 25 * channels), BF16),
        pltpu.VMEM((head_width, heads), F32),
        pltpu.VMEM((head_width, heads), F32),
        pltpu.VMEM((rots, edges), F32),
        pltpu.VMEM((25, channels, edges), F32),
        pltpu.VMEM((19, channels, edges), BF16),
        pltpu.VMEM((19, hidden, edges), F32),
        pltpu.VMEM((25, hidden, edges), BF16),
        pltpu.VMEM((25, hidden, edges), F32),
        pltpu.VMEM((head_width * heads, edges), F32),
        pltpu.VMEM((19, hidden, edges), BF16),
        pltpu.VMEM((mixed, edges), BF16),
        pltpu.VMEM((19, channels, edges), F32),
        pltpu.VMEM((25, channels, edges), BF16),
        pltpu.VMEM((2, heads, edges), F32),
        pltpu.VMEM((2, hidden, edges), F32),
    ]
    scratch += [pltpu.VMEM((2, slots, 25 * channels), BF16) for _ in range(4)]
    scratch += [pltpu.VMEM((half, 2, *w), BF16) for w in w_shapes]
    scratch += [pltpu.VMEM((n * w[0], w[1]) if w[0] % 16 else (8, 128), F32) for w in w_shapes]
    scratch += [pltpu.VMEM((half, 2, *t), BF16) for t in t_shapes]
    scratch += [pltpu.VMEM((half, *t), BF16) for t in t_shapes]
    scratch += [pltpu.VMEM((half - 1, *t), BF16) for _ in range(2) for t in t_shapes]
    steps, deep = Halving(half).steps, Halving(depth).steps
    scratch += [pltpu.VMEM((deep, *t), BF16) for t in t_shapes]
    scratch += [pltpu.VMEM((max(deep, 2), *t), BF16) for t in t_shapes]
    scratch += [dma((4,)) for _ in range(2)]
    scratch += [dma((half - 1, count)) for _ in range(2)]
    scratch += [dma((half, count)) for _ in range(2)]
    scratch += [dma((items,)) for _ in range(2)]
    scratch += [dma((steps, items)) for _ in range(2)]
    scratch += [dma((deep + 1, items)), dma((max(deep, 2) + 1, items)), dma((7 + count,))]
    given = (features, cotangent, rotation, src, tgt, send_left, send_right)
    scratch += [dma((2 + items,))]
    scratch += [pltpu.VMEM(g.shape, g.dtype) for g in (*given, *out_shape)]
    return pl.pallas_call(
        partial(slab_kernel, n, depth, sizes),
        out_shape=tuple(out_shape),
        in_specs=[pl.BlockSpec(memory_space=pl.ANY)] * (7 + count),
        out_specs=[pl.BlockSpec(memory_space=pl.ANY)] * (2 + items),
        scratch_shapes=scratch,
        compiler_params=pltpu.CompilerParams(
            collective_id=0, has_side_effects=True, vmem_limit_bytes=60 * 2**20),
        name="slab",
    )(features, cotangent, rotation, src, tgt, send_left, send_right, *weights)


def finish_kernel(items, hidden, *refs):
    att_ref, grad_ref = refs[:2]
    final = refs[2:2 + items]
    out_att, out_grad = refs[2 + items:4 + items]
    gz_ref, g1r_ref, g1i_ref, g2r_ref, g2i_ref, gt_ref, ga_ref = refs[4 + items:]
    out_att[...] = att_ref[...]
    out_grad[...] = grad_ref[...]

    wide = 3 * hidden
    g1r_ref[...] = final[0][...].astype(F32)
    g1i_ref[...] = final[1][...].astype(F32)
    g2r_ref[...] = final[2][:, :wide].astype(F32)
    g2i_ref[...] = final[2][:, wide:].astype(F32)
    begin = 0
    for source in final[3:6]:
        end = begin + source.shape[1]
        gz_ref[:, begin:end] = source[...].astype(F32)
        begin = end
    gt_ref[...] = final[6][...].astype(F32)
    ga_ref[...] = final[7][...].astype(F32)


def finish(attended, grad, final, weights, hidden):
    items = len(final)
    vmem = pl.BlockSpec(memory_space=pltpu.VMEM)
    shapes = [jax.ShapeDtypeStruct(attended.shape, BF16), jax.ShapeDtypeStruct(grad.shape, F32)]
    shapes += [jax.ShapeDtypeStruct(w.shape, F32) for w in weights]
    return pl.pallas_call(
        partial(finish_kernel, items, hidden),
        out_shape=tuple(shapes),
        in_specs=[vmem] * (2 + items),
        out_specs=[vmem] * len(shapes),
        name="finish",
    )(attended, grad, *final)


def body(n, depth, features, cotangent, rotation, send_left, send_right, edge_src, edge_tgt,
         *weights):
    turned_rotation = jnp.swapaxes(rotation[0], 0, 1)
    attended, grad_features, *final = slab(
        n, depth, features[0], cotangent[0], turned_rotation, edge_src, edge_tgt,
        send_left, send_right, weights)
    attended, grad_features, *grads = finish(
        attended, grad_features, final, weights, weights[1].shape[1] // 4)
    return (attended[None], grad_features[None], *grads)


def solution(mesh):
    cell = P("dp", "graph", None)
    lists = P("dp", "graph")
    shard = P("graph", None)
    in_specs = (cell, cell, P("dp", None, "graph")) + (lists,) * 4 + (shard,) * 7
    out_specs = (cell, cell) + (shard,) * 7
    return jax.shard_map(
        partial(body, mesh.shape["graph"], mesh.shape["dp"]), mesh=mesh,
        in_specs=in_specs, out_specs=out_specs, check_vma=False)
```

```python
from functools import partial

import jax
import jax.numpy as jnp
from jax import lax
from jax.experimental import pallas as pl
from jax.experimental.pallas import tpu as pltpu
from jax.sharding import PartitionSpec as P

F32 = jnp.float32
BF16 = jnp.bfloat16
OFFSETS = {1: 0, 2: 9, 3: 34, 4: 69}
DEGREES = (1, 2, 3, 4)
BLOCK_C = 16
BLOCK_H = 16
MESH = pl.DeviceIdType.MESH
EXACT = lax.Precision.HIGHEST
ORDER = (
    "g1r", "s0", "g2", "s2", "ds0", "x0", "gzv", "s3", "x2", "g1i", "ds1", "s4", "s1", "x3",
    "dt0", "gwt", "x4", "s7", "dt2", "y0", "s5", "dt1", "y2", "x1", "tb0", "s6", "y3", "x6",
    "x5", "x7", "a0", "y4", "a2", "y1", "tb1", "tb2", "a3", "y6", "b0", "y5", "y7", "a4", "b2",
    "tb3", "a6", "att", "b3", "a1", "a5", "b4", "c0", "eg0", "c2", "eg1", "a7", "b1", "b6",
    "eg2", "eg3", "c3", "eg4", "b5", "ghost", "c4", "b7", "c1", "c6", "d3", "add", "c5", "c7",
    "d0", "d1",
)
CUBE = (2, 4, 5, 6, 7)


def slot(degree, azimuth):
    return {0: degree, 1: 4 + degree, -1: 8 + degree, 2: 11 + degree, -2: 14 + degree}[azimuth]


def orders(degree):
    kept = min(degree, 2)
    return range(-kept, kept + 1)


def rot_row(degree, azimuth, column):
    return OFFSETS[degree] + (azimuth + min(degree, 2)) * (2 * degree + 1) + column


def dot(a, b, ca, cb, precision=None):
    return lax.dot_general(
        a, b, (((ca,), (cb,)), ((), ())), preferred_element_type=F32, precision=precision
    )


def flip(index, power):
    bit = lax.rem(lax.div(index, power), 2)
    return index + (1 - 2 * bit) * power


def flips(index, powers, chosen):
    for j in chosen:
        index = flip(index, powers[j])
    return index


def subsets(steps):
    found = [()]
    for j in steps:
        found = found + [s + (j,) for s in found]
    return found


class Halving:
    def __init__(self, count):
        self.steps = count.bit_length() - 1
        self.rest = [subsets(range(j + 1, self.steps)) for j in range(self.steps)]
        self.base = [0]
        for found in self.rest:
            self.base.append(self.base[-1] + len(found))

    def spot(self, step, chosen):
        return self.base[step] + self.rest[step].index(chosen)


def pieces_of(shapes):
    found = []
    for w, (block, _) in enumerate(shapes):
        cut = block // 32 * 16
        if w == 0 and block % 16 == 0 and cut:
            found += [(w, 0, cut), (w, cut, block)]
        else:
            found.append((w, 0, block))
    return found


def slab_kernel(n, depth, sizes, *refs):
    take = iter(refs)
    placed = [next(take) for _ in range(7)]
    count = len(sizes["weights"])
    items = len(sizes["terms"])
    shards = [next(take) for _ in range(count)]
    results = [next(take) for _ in range(2 + items)]
    (ext_ref, alphas, d_alphas, rotf, xs, turned, hid, msg, dmsg, scores, dhid, dmixed, dturned,
     dxs, small, spreads) = [next(take) for _ in range(16)]
    outgoing, near, ghost, back = [next(take) for _ in range(4)]
    full = [next(take) for _ in range(count)]
    mats = [next(take) for _ in range(count)]
    terms = [next(take) for _ in range(items)]
    landed = [next(take) for _ in range(items)]
    out_xy = [next(take) for _ in range(items)]
    in_xy = [next(take) for _ in range(items)]
    out_z = [next(take) for _ in range(items)]
    in_z = [next(take) for _ in range(items)]
    (side_send, side_recv, hop_send, hop_recv, core_send, core_recv, sib_send, sib_recv,
     xy_send, xy_recv, z_send, z_recv, in_sem, out_sem) = [next(take) for _ in range(14)]
    local = [next(take) for _ in range(7)]
    leaving = list(take)
    att_ref, grad_ref = leaving[:2]
    final = leaving[2:]
    feat_ref, cot_ref, rot_ref, src_ref, tgt_ref, left_ref, right_ref = local

    edges = src_ref.shape[1]
    rows = ext_ref.shape[0]
    atoms = att_ref.shape[0]
    channels = n * sizes["weights"][5][0]
    hidden = sizes["weights"][1][1] // 4
    heads = small.shape[1]
    width = alphas.shape[0]
    slots = left_ref.shape[1]

    me = lax.axis_index("graph")
    row = lax.axis_index("dp")
    half = n // 2
    chip = lax.div(me, 2)
    parity = lax.rem(me, 2)
    sibling = me + 1 - 2 * parity
    right, left = lax.rem(me + 1, n), lax.rem(me + n - 1, n)
    plan = Halving(half)
    steps = plan.steps
    deep = Halving(depth).steps
    z_spots = max(deep, 2)
    powers = [2 ** j + parity * (2 ** ((j + 1) % steps) - 2 ** j) for j in range(steps)]

    upper = lax.div(row, depth // 2)
    inward = row + 1 - 2 * upper
    outward = row - 1 + 2 * upper
    from_end = row + upper * (depth - 1 - 2 * row)
    at_middle = lax.div(from_end + 1, depth // 2)
    is_end = from_end == 0
    is_middle = at_middle == 1

    barrier = pltpu.get_barrier_semaphore()
    partners = [(row, sibling), (row, right), (row, left)]
    partners += [(row, 2 * flip(chip, p) + parity) for p in powers]
    partners += [(flip(row, 2 ** j), me) for j in range(deep)]
    for partner in partners:
        pl.semaphore_signal(barrier, inc=1, device_id=partner, device_id_type=MESH)
    for z in (-1, 1):
        other = row + z

        @pl.when((other >= 0) & (other < depth))
        def _():
            pl.semaphore_signal(barrier, inc=1, device_id=(other, me), device_id_type=MESH)

    def remote(src, dst, send, recv, target):
        copy = pltpu.make_async_remote_copy(
            src_ref=src, dst_ref=dst, send_sem=send, recv_sem=recv,
            device_id=target, device_id_type=MESH)
        copy.start()
        return copy

    started = []

    loads = {}

    def load(key, src, dst, spot):
        copy = pltpu.make_async_copy(src, dst, in_sem.at[spot])
        copy.start()
        loads[key] = copy

    for k in (0, 5, 6):
        load(k, placed[k], local[k], k)
    for w in range(count):
        load(("w", w), shards[w], full[w].at[chip, parity], 7 + w)
    for k in (3, 4, 2, 1):
        load(k, placed[k], local[k], k)
    for k in (0, 5, 6):
        loads[k].wait()
    own = feat_ref[...].astype(BF16)
    ext_ref[:atoms, :] = own
    for side, list_ref in ((0, left_ref), (1, right_ref)):
        ids = lax.broadcasted_iota(jnp.int32, (atoms, slots), 0)
        pick = (ids == list_ref[...]).astype(F32).astype(BF16)
        outgoing[side] = dot(pick, own, 0, 0).astype(BF16)
    for w in range(count):
        loads["w", w].wait()

    pl.semaphore_wait(barrier, len(partners) + 1 + lax.div(from_end + depth - 1, depth))

    sides = []
    for side, target in ((1, left), (0, right)):
        sides.append(remote(outgoing.at[1 - side], near.at[side], side_send.at[side],
                            side_recv.at[side], (row, target)))
    arrivals = {}

    pieces = pieces_of(sizes["weights"])

    def block_of(w, unit):
        own, begin, end = pieces[w]
        if end - begin == sizes["weights"][own][0]:
            return full[own].at[unit, parity]
        return full[own].at[unit, parity, begin:end]

    def hop(j, w, part):
        target = (row, 2 * flip(chip, powers[j]) + parity)
        for t, chosen in enumerate(subsets(range(j))):
            if (t > 0) != part:
                continue
            unit = flips(chip, powers, chosen)
            copy = remote(block_of(w, unit), block_of(w, unit),
                          hop_send.at[2 ** j + t - 1, w], hop_recv.at[2 ** j + t - 1, w], target)
            arrivals[j, t, w] = copy
            started.append(copy)

    crossing = {}

    def cross(spot, unit, w):
        copy = remote(block_of(w, unit), block_of(w, unit),
                      core_send.at[spot, w], core_recv.at[spot, w], (row, sibling))
        crossing[spot, w] = copy
        started.append(copy)

    def land(j, w, part):
        partner = flip(chip, powers[j])
        for t, chosen in enumerate(subsets(range(j))):
            if (t > 0) == part:
                arrivals[j, t, w].wait_recv()
                cross(2 ** j + t, flips(partner, powers, chosen), w)

    weight_order = [p for w in (0, 5, 6, 1, 2, 3, 4)
                    for p in range(len(pieces)) if pieces[p][0] == w]
    for j in range(steps):
        for w in weight_order:
            hop(j, w, False)
    for w in weight_order:
        cross(0, chip, w)

    for k in (3, 4, 2, 1):
        loads[k].wait()
    src_hot = (
        lax.broadcasted_iota(jnp.int32, (rows, edges), 0) == src_ref[...]
    ).astype(F32).astype(BF16)
    member = (lax.broadcasted_iota(jnp.int32, (atoms, edges), 0) == tgt_ref[...]).astype(F32)
    member_b = member.astype(BF16)

    edge_eye = (
        lax.broadcasted_iota(jnp.int32, (rot_ref.shape[1], rot_ref.shape[1]), 0)
        == lax.broadcasted_iota(jnp.int32, (rot_ref.shape[1], rot_ref.shape[1]), 1)
    ).astype(F32).astype(BF16)
    rotf[...] = dot(edge_eye, rot_ref[...], 1, 1)
    for k in range(25):
        dmsg[k] = dot(
            cot_ref[:, k * hidden:(k + 1) * hidden].astype(BF16), member_b, 0, 0
        )
    for copy in sides:
        copy.wait_recv()
    ext_ref[atoms:, :] = near[...].astype(F32).reshape(rows - atoms, -1).astype(BF16)
    for k in range(25):
        xs[k] = dot(ext_ref[:, k * channels:(k + 1) * channels], src_hot, 0, 0)

    for j in range(1, steps):
        for w in weight_order:
            land(j - 1, w, False)
            land(j - 1, w, True)
            hop(j, w, True)

    def turn(i, carry):
        part = pl.ds(pl.multiple_of(i * BLOCK_C, BLOCK_C), BLOCK_C)
        turned[0, part, :] = xs[0, part, :].astype(BF16)
        for degree in DEGREES:
            for azimuth in orders(degree):
                total = None
                for m in range(2 * degree + 1):
                    k = rot_row(degree, azimuth, m)
                    term = rotf[k:k + 1, :] * xs[degree * degree + m, part, :]
                    total = term if total is None else total + term
                turned[slot(degree, azimuth), part, :] = total.astype(BF16)
        return carry

    lax.fori_loop(0, channels // BLOCK_C, turn, 0)

    zero_in = turned[0:5].reshape(5 * channels, edges)
    one_pos = turned[5:9].reshape(4 * channels, edges)
    one_neg = turned[9:13].reshape(4 * channels, edges)
    two_pos = turned[13:16].reshape(3 * channels, edges)
    two_neg = turned[16:19].reshape(3 * channels, edges)

    def settle(w):
        for spot in range(half):
            for p in range(len(pieces)):
                if pieces[p][0] == w:
                    crossing[spot, p].wait_recv()
        block = sizes["weights"][w][0]
        if block % 16:
            for u in range(half):
                for c in range(2):
                    at = (2 * u + c) * block
                    mats[w][at:at + block, :] = full[w][u, c].astype(mats[w].dtype)

    def weight(w, begin=0, end=None):
        block, wide = sizes["weights"][w]
        end = wide if end is None else end
        if block % 16:
            return mats[w][:, begin:end].astype(BF16)
        return full[w][:, :, :, begin:end].reshape(n * block, end - begin)

    for w in weight_order:
        land(steps - 1, w, False)
    for w in weight_order:
        if pieces[w][0] not in (3, 4):
            land(steps - 1, w, True)
    for w in (0, 5, 6):
        settle(w)
    alpha_rows = sizes["weights"][6][0]
    for u in range(half):
        for c in range(2):
            at = (2 * u + c) * alpha_rows
            alphas[at:at + alpha_rows, :] = full[6][u, c].astype(F32)

    per_atom = dot(ext_ref[:atoms, :channels], weight(5), 1, 0)
    high = per_atom.astype(BF16)
    low = (per_atom - high.astype(F32)).astype(BF16)
    scores[...] = (
        dot(weight(0, 5 * hidden), zero_in, 0, 0)
        + dot(high, member_b, 0, 0)
        + dot(low, member_b, 0, 0)
    )
    hid[0:5] = dot(weight(0, 0, 5 * hidden), zero_in, 0, 0).reshape(5, hidden, edges)

    for w in weight_order:
        if pieces[w][0] in (3, 4):
            land(steps - 1, w, True)

    for h in range(heads):
        part = slice(h * width, (h + 1) * width)
        value = scores[part, :]
        centre = value - jnp.mean(value, axis=0, keepdims=True)
        scale = lax.rsqrt(jnp.mean(centre * centre, axis=0, keepdims=True) + 1e-05)
        normed = centre * scale
        scores[part, :] = normed
        gate = 0.2 + 0.8 * jax.nn.sigmoid(normed)
        small[0, h:h + 1, :] = jnp.sum(
            normed * gate * alphas[:, h:h + 1], axis=0, keepdims=True
        )
        small[1, h:h + 1, :] = scale

    raised = jnp.exp(small[0])
    totals = dot(dot(raised, member, 1, 1, EXACT), member, 1, 0, EXACT)
    weights = raised / totals
    spreads[0] = jnp.broadcast_to(
        weights[:, None, :], (heads, hidden // heads, edges)
    ).reshape(hidden, edges)

    settle(1)
    settle(2)
    hid[5:9] = (dot(weight(1), one_pos, 0, 0) - dot(weight(2), one_neg, 0, 0)).reshape(
        4, hidden, edges)
    hid[9:13] = (dot(weight(1), one_neg, 0, 0) + dot(weight(2), one_pos, 0, 0)).reshape(
        4, hidden, edges)
    settle(3)
    settle(4)
    hid[13:16] = (dot(weight(3), two_pos, 0, 0) - dot(weight(4), two_neg, 0, 0)).reshape(
        3, hidden, edges)
    hid[16:19] = (dot(weight(3), two_neg, 0, 0) + dot(weight(4), two_pos, 0, 0)).reshape(
        3, hidden, edges)

    def mix(i, carry):
        part = pl.ds(pl.multiple_of(i * BLOCK_H, BLOCK_H), BLOCK_H)
        spread = spreads[0, part, :]
        scalar = hid[0, part, :]
        gating = jax.nn.sigmoid(scalar)
        silu = scalar * gating
        both = gating * spread
        msg[0, part, :] = (silu * spread).astype(BF16)
        d_first = dmsg[0, part, :]
        inner = jnp.zeros_like(scalar)
        for degree in DEGREES:
            size = 2 * degree + 1
            sums = [None] * size
            for azimuth in orders(degree):
                raw = hid[slot(degree, azimuth), part, :]
                value = raw * both
                back_sum = None
                for m in range(size):
                    k = rot_row(degree, azimuth, m)
                    line = rotf[k:k + 1, :]
                    term = line * value
                    sums[m] = term if sums[m] is None else sums[m] + term
                    other = line * dmsg[degree * degree + m, part, :]
                    back_sum = other if back_sum is None else back_sum + other
                inner = inner + back_sum * raw
                dhid[slot(degree, azimuth), part, :] = (back_sum * both).astype(BF16)
            for m in range(size):
                msg[degree * degree + m, part, :] = sums[m].astype(BF16)
        spreads[1, part, :] = inner * gating + d_first * silu
        d_scalar = d_first * spread * gating * (1.0 + scalar * (1.0 - gating)) + (
            inner * spread * gating * (1.0 - gating)
        )
        dhid[0, part, :] = d_scalar.astype(BF16)
        return carry

    lax.fori_loop(0, hidden // BLOCK_H, mix, 0)

    def put(i, value, begin=0):
        block = sizes["terms"][i][0]
        wide = value.shape[1]
        if block % 16:
            for u in range(half):
                for c in range(2):
                    at = (2 * u + c) * block
                    terms[i][u, c, :, begin:begin + wide] = value[at:at + block, :].astype(BF16)
        else:
            terms[i][:, :, :, begin:begin + wide] = value.astype(BF16).reshape(
                half, 2, block, wide)

    flights = {}

    def launch(key, src, dst, send, recv, target):
        copy = remote(src, dst, send, recv, target)
        flights[key] = copy
        started.append(copy)

    def to_sibling(i):
        launch(("core", i), terms[i].at[:, 1 - parity], landed[i], sib_send.at[i], sib_recv.at[i],
               (row, sibling))

    def chip_sum(i, step, chosen):
        unit = flips(chip, powers, chosen)
        total = terms[i][unit, parity] + landed[i][unit]
        for s in range(step):
            total = total + in_xy[i][plan.spot(s, chosen)]
        return total

    def to_chip(i, step):
        if step == 0:
            flights["core", i].wait_recv()
        else:
            flights["xy", step - 1, i].wait_recv()
        begin, end = plan.base[step], plan.base[step + 1]
        for t, rest in enumerate(plan.rest[step]):
            out_xy[i][begin + t] = chip_sum(i, step, (step,) + rest)
        target = (row, 2 * flip(chip, powers[step]) + parity)
        launch(("xy", step, i), out_xy[i].at[begin:end], in_xy[i].at[begin:end],
               xy_send.at[step, i], xy_recv.at[step, i], target)

    def z_copy(i, out, spot, target):
        return pltpu.make_async_remote_copy(
            src_ref=out_z[i].at[out], dst_ref=in_z[i].at[spot],
            send_sem=z_send.at[out, i], recv_sem=z_recv.at[spot, i],
            device_id=(target, me), device_id_type=MESH)

    def inward_copy(i, spot):
        return z_copy(i, 0, spot, inward)

    def swap_copy(i, step):
        return z_copy(i, step, step, flip(row, 2 ** step))

    def outward_copy(i):
        return pltpu.make_async_remote_copy(
            src_ref=final[i], dst_ref=final[i],
            send_sem=z_send.at[deep, i], recv_sem=z_recv.at[z_spots, i],
            device_id=(outward, me), device_id_type=MESH)

    def leave(k):
        return pltpu.make_async_copy(leaving[k], results[k], out_sem.at[k])

    def layer_total(i):
        flights["xy", steps - 1, i].wait_recv()
        out_z[i][0] = chip_sum(i, steps, ())

    def on_line(i, stage):
        if stage == 0:
            layer_total(i)

            @pl.when(is_end)
            def _():
                inward_copy(i, at_middle).start()
        elif stage == 1:
            @pl.when(jnp.logical_not(is_end))
            def _():
                inward_copy(i, 0).wait_recv()
                out_z[i][0] = out_z[i][0] + in_z[i][0]
                inward_copy(i, at_middle).start()
        elif stage == 2:
            @pl.when(is_middle)
            def _():
                inward_copy(i, 1).wait_recv()
                final[i][...] = out_z[i][0] + in_z[i][1]
                leave(2 + i).start()
                if depth > 2:
                    outward_copy(i).start()
        else:
            @pl.when(jnp.logical_not(is_middle))
            def _():
                outward_copy(i).wait_recv()
                if depth > 4:
                    @pl.when(jnp.logical_not(is_end))
                    def _():
                        outward_copy(i).start()
                leave(2 + i).start()

    def on_cube(i, stage):
        if stage == 0:
            layer_total(i)
            swap_copy(i, 0).start()
        elif stage == 1:
            for step in range(1, deep):
                swap_copy(i, step - 1).wait_recv()
                out_z[i][step] = out_z[i][step - 1] + in_z[i][step - 1]
                swap_copy(i, step).start()
        elif stage == 2:
            swap_copy(i, deep - 1).wait_recv()
            final[i][...] = out_z[i][deep - 1] + in_z[i][deep - 1]
            leave(2 + i).start()

    def advance(i, stage):
        if stage == 0:
            to_sibling(i)
        elif stage <= steps:
            to_chip(i, stage - 1)
        else:
            (on_cube if i in CUBE else on_line)(i, stage - 1 - steps)

    def bands(first, number):
        middle = first + number
        last = middle + number
        return (dhid[first:middle].reshape(number * hidden, edges),
                dhid[middle:last].reshape(number * hidden, edges))

    def one_re():
        up, down = bands(5, 4)
        put(0, dot(one_pos, up, 1, 1) + dot(one_neg, down, 1, 1))

    def one_im():
        up, down = bands(5, 4)
        put(1, dot(one_pos, down, 1, 1) - dot(one_neg, up, 1, 1))

    def two():
        up, down = bands(13, 3)
        put(2, dot(two_pos, up, 1, 1) + dot(two_neg, down, 1, 1))
        put(2, dot(two_pos, down, 1, 1) - dot(two_neg, up, 1, 1), 3 * hidden)

    def values():
        d_values = dhid[0:5].reshape(5 * hidden, edges)
        dmixed[:5 * hidden, :] = d_values
        put(3, dot(zero_in, d_values, 1, 1))

    def score_grads(which):
        if which == 0:
            d_weights = jnp.sum(
                spreads[1].reshape(heads, hidden // heads, edges), axis=1
            )
            product = weights * d_weights
            small[0] = product - weights * dot(
                dot(product, member, 1, 1, EXACT), member, 1, 0, EXACT
            )
        group = heads // 2
        for h in range(which * group, (which + 1) * group):
            part = slice(h * width, (h + 1) * width)
            normed = scores[part, :]
            sig = jax.nn.sigmoid(normed)
            gate = 0.2 + 0.8 * sig
            d_logit = small[0, h:h + 1, :]
            d_alphas[:, h:h + 1] = jnp.sum(normed * gate * d_logit, axis=1, keepdims=True)
            d_norm = d_logit * alphas[:, h:h + 1] * (gate + 0.8 * normed * sig * (1.0 - sig))
            first = jnp.mean(d_norm, axis=0, keepdims=True)
            second = jnp.mean(d_norm * normed, axis=0, keepdims=True)
            d_score = small[1, h:h + 1, :] * (d_norm - first - normed * second)
            dmixed[5 * hidden + h * width:5 * hidden + (h + 1) * width, :] = d_score.astype(BF16)
            scores[part, :] = d_score
        begin = 5 * hidden + which * group * width
        put(4 + which, dot(zero_in, dmixed[begin:begin + group * width, :], 1, 1))

    held = {}

    def target_alpha():
        held["atom"] = dot(member, scores[...], 1, 1, EXACT).astype(BF16)
        put(6, dot(ext_ref[:atoms, :channels], held["atom"], 0, 0))
        for u in range(half):
            for c in range(2):
                at = (2 * u + c) * alpha_rows
                terms[7][u, c] = d_alphas[at:at + alpha_rows, :].astype(BF16)

    def turn_zero():
        dturned[0:5] = dot(weight(0), dmixed[...], 1, 0).reshape(5, channels, edges)

    def turn_pair(first, number, re_item, im_item):
        up, down = bands(first, number)
        middle = first + number
        last = middle + number
        dturned[first:middle] = (
            dot(weight(re_item), up, 1, 0) + dot(weight(im_item), down, 1, 0)
        ).reshape(number, channels, edges)
        dturned[middle:last] = (
            dot(weight(re_item), down, 1, 0) - dot(weight(im_item), up, 1, 0)
        ).reshape(number, channels, edges)

    def turn_back(i, carry):
        part = pl.ds(pl.multiple_of(i * BLOCK_C, BLOCK_C), BLOCK_C)
        dxs[0, part, :] = dturned[0, part, :].astype(BF16)
        for degree in DEGREES:
            for m in range(2 * degree + 1):
                total = None
                for azimuth in orders(degree):
                    k = rot_row(degree, azimuth, m)
                    term = rotf[k:k + 1, :] * dturned[slot(degree, azimuth), part, :]
                    total = term if total is None else total + term
                dxs[degree * degree + m, part, :] = total.astype(BF16)
        return carry

    blocks = channels // BLOCK_C

    def source_grads(k):
        part = slice(5 * k * channels, 5 * (k + 1) * channels)
        ext_grad = dot(src_hot, dxs[5 * k:5 * k + 5].reshape(5 * channels, edges), 1, 1)
        grad_ref[:, part] = ext_grad[:atoms]
        if k == 0:
            grad_ref[:, :channels] = ext_grad[:atoms, :channels] + dot(
                held["atom"], weight(5), 1, 1)
        for side in range(2):
            begin = atoms + side * slots
            ghost[side, :, part] = ext_grad[begin:begin + slots].astype(BF16)

    returns = []

    def return_ghosts():
        for side, target in ((0, left), (1, right)):
            returns.append(remote(ghost.at[side], back.at[side], side_send.at[2 + side],
                                  side_recv.at[2 + side], (row, target)))

    def attend():
        att_ref[...] = dot(member_b, msg[...].reshape(25 * hidden, edges), 1, 1).astype(BF16)
        leave(0).start()

    def add_ghosts():
        for copy in returns:
            copy.wait_recv()
        total = grad_ref[...]
        for side, list_ref in ((0, right_ref), (1, left_ref)):
            ids = lax.broadcasted_iota(jnp.int32, (atoms, slots), 0)
            place = (ids == list_ref[...]).astype(F32).astype(BF16)
            total = total + dot(place, back[side], 1, 0)
        grad_ref[...] = total
        leave(1).start()

    work = {
        "g1r": one_re, "g1i": one_im, "g2": two, "gzv": values,
        "ds0": partial(score_grads, 0), "ds1": partial(score_grads, 1), "gwt": target_alpha,
        "dt0": turn_zero, "dt1": partial(turn_pair, 5, 4, 1, 2),
        "dt2": partial(turn_pair, 13, 3, 3, 4),
        "ghost": return_ghosts, "add": add_ghosts, "att": attend,
    }
    for k in range(4):
        work["tb%d" % k] = partial(
            lax.fori_loop, k * blocks // 4, (k + 1) * blocks // 4, turn_back, 0)
    for k in range(5):
        work["eg%d" % k] = partial(source_grads, k)
    for step in ORDER:
        if step in work:
            work[step]()
        else:
            first, last = {
                "s": (0, 1), "x": (1, 2), "y": (2, 1 + steps), "a": (1 + steps, 2 + steps),
                "b": (2 + steps, 3 + steps), "c": (3 + steps, 4 + steps),
                "d": (4 + steps, 5 + steps)}[step[0]]
            for stage in range(first, last):
                for i in step[1:]:
                    advance(int(i), stage)

    for i in range(items):
        if i in CUBE:
            for step in range(deep):
                swap_copy(i, step).wait_send()
            continue
        inward_copy(i, at_middle).wait_send()
        if depth > 2:
            @pl.when(jnp.logical_not(is_end))
            def _():
                outward_copy(i).wait_send()
    for copy in sides + returns + started:
        copy.wait_send()
    for k in range(2 + items):
        leave(k).wait()


def slab(n, depth, features, cotangent, rotation, src, tgt, send_left, send_right, weights):
    atoms = features.shape[0]
    edges = src.shape[1]
    slots = send_left.shape[1]
    heads = weights[6].shape[1]
    head_width = n * weights[6].shape[0]
    channels = n * weights[5].shape[0]
    hidden = weights[1].shape[1] // 4
    half = n // 2
    w_shapes = [tuple(w.shape) for w in weights]
    block = w_shapes[0][0]
    logits = (w_shapes[0][1] - 5 * hidden) // 2
    t_shapes = w_shapes[1:3] + [(w_shapes[3][0], 6 * hidden), (block, 5 * hidden)]
    t_shapes += [(block, logits)] * 2 + w_shapes[5:]
    sizes = {"weights": w_shapes, "terms": t_shapes}
    count, items = len(w_shapes), len(t_shapes)

    shape = jax.ShapeDtypeStruct
    vmem = pl.BlockSpec(memory_space=pltpu.VMEM)
    out_shape = [shape((atoms, 25 * hidden), BF16), shape((atoms, 25 * channels), F32)]
    out_shape += [shape(t, BF16) for t in t_shapes]
    rows = atoms + 2 * slots
    mixed = w_shapes[0][1]
    rots = rotation.shape[1]
    dma = pltpu.SemaphoreType.DMA
    scratch = [
        pltpu.VMEM((rows, 25 * channels), BF16),
        pltpu.VMEM((head_width, heads), F32),
        pltpu.VMEM((head_width, heads), F32),
        pltpu.VMEM((rots, edges), F32),
        pltpu.VMEM((25, channels, edges), F32),
        pltpu.VMEM((19, channels, edges), BF16),
        pltpu.VMEM((19, hidden, edges), F32),
        pltpu.VMEM((25, hidden, edges), BF16),
        pltpu.VMEM((25, hidden, edges), F32),
        pltpu.VMEM((head_width * heads, edges), F32),
        pltpu.VMEM((19, hidden, edges), BF16),
        pltpu.VMEM((mixed, edges), BF16),
        pltpu.VMEM((19, channels, edges), F32),
        pltpu.VMEM((25, channels, edges), BF16),
        pltpu.VMEM((2, heads, edges), F32),
        pltpu.VMEM((2, hidden, edges), F32),
    ]
    scratch += [pltpu.VMEM((2, slots, 25 * channels), BF16) for _ in range(4)]
    scratch += [pltpu.VMEM((half, 2, *w), BF16) for w in w_shapes]
    scratch += [pltpu.VMEM((n * w[0], w[1]) if w[0] % 16 else (8, 128), F32) for w in w_shapes]
    scratch += [pltpu.VMEM((half, 2, *t), BF16) for t in t_shapes]
    scratch += [pltpu.VMEM((half, *t), BF16) for t in t_shapes]
    scratch += [pltpu.VMEM((half - 1, *t), BF16) for _ in range(2) for t in t_shapes]
    steps, deep = Halving(half).steps, Halving(depth).steps
    scratch += [pltpu.VMEM((deep, *t), BF16) for t in t_shapes]
    scratch += [pltpu.VMEM((max(deep, 2), *t), BF16) for t in t_shapes]
    scratch += [dma((4,)) for _ in range(2)]
    parts = len(pieces_of(w_shapes))
    scratch += [dma((half - 1, parts)) for _ in range(2)]
    scratch += [dma((half, parts)) for _ in range(2)]
    scratch += [dma((items,)) for _ in range(2)]
    scratch += [dma((steps, items)) for _ in range(2)]
    scratch += [dma((deep + 1, items)), dma((max(deep, 2) + 1, items)), dma((7 + count,))]
    given = (features, cotangent, rotation, src, tgt, send_left, send_right)
    scratch += [dma((2 + items,))]
    scratch += [pltpu.VMEM(g.shape, g.dtype) for g in (*given, *out_shape)]
    return pl.pallas_call(
        partial(slab_kernel, n, depth, sizes),
        out_shape=tuple(out_shape),
        in_specs=[pl.BlockSpec(memory_space=pl.ANY)] * (7 + count),
        out_specs=[pl.BlockSpec(memory_space=pl.ANY)] * (2 + items),
        scratch_shapes=scratch,
        compiler_params=pltpu.CompilerParams(
            collective_id=0, has_side_effects=True, vmem_limit_bytes=60 * 2**20),
        name="slab",
    )(features, cotangent, rotation, src, tgt, send_left, send_right, *weights)


def finish_kernel(items, hidden, *refs):
    att_ref, grad_ref = refs[:2]
    final = refs[2:2 + items]
    out_att, out_grad = refs[2 + items:4 + items]
    gz_ref, g1r_ref, g1i_ref, g2r_ref, g2i_ref, gt_ref, ga_ref = refs[4 + items:]
    out_att[...] = att_ref[...]
    out_grad[...] = grad_ref[...]

    wide = 3 * hidden
    g1r_ref[...] = final[0][...].astype(F32)
    g1i_ref[...] = final[1][...].astype(F32)
    g2r_ref[...] = final[2][:, :wide].astype(F32)
    g2i_ref[...] = final[2][:, wide:].astype(F32)
    begin = 0
    for source in final[3:6]:
        end = begin + source.shape[1]
        gz_ref[:, begin:end] = source[...].astype(F32)
        begin = end
    gt_ref[...] = final[6][...].astype(F32)
    ga_ref[...] = final[7][...].astype(F32)


def finish(attended, grad, final, weights, hidden):
    items = len(final)
    vmem = pl.BlockSpec(memory_space=pltpu.VMEM)
    shapes = [jax.ShapeDtypeStruct(attended.shape, BF16), jax.ShapeDtypeStruct(grad.shape, F32)]
    shapes += [jax.ShapeDtypeStruct(w.shape, F32) for w in weights]
    return pl.pallas_call(
        partial(finish_kernel, items, hidden),
        out_shape=tuple(shapes),
        in_specs=[vmem] * (2 + items),
        out_specs=[vmem] * len(shapes),
        name="finish",
    )(attended, grad, *final)


def body(n, depth, features, cotangent, rotation, send_left, send_right, edge_src, edge_tgt,
         *weights):
    turned_rotation = jnp.swapaxes(rotation[0], 0, 1)
    attended, grad_features, *final = slab(
        n, depth, features[0], cotangent[0], turned_rotation, edge_src, edge_tgt,
        send_left, send_right, weights)
    attended, grad_features, *grads = finish(
        attended, grad_features, final, weights, weights[1].shape[1] // 4)
    return (attended[None], grad_features[None], *grads)


def solution(mesh):
    cell = P("dp", "graph", None)
    lists = P("dp", "graph")
    shard = P("graph", None)
    in_specs = (cell, cell, P("dp", None, "graph")) + (lists,) * 4 + (shard,) * 7
    out_specs = (cell, cell) + (shard,) * 7
    return jax.shard_map(
        partial(body, mesh.shape["graph"], mesh.shape["dp"]), mesh=mesh,
        in_specs=in_specs, out_specs=out_specs, check_vma=False)
```
